128 devices in a mesh: ctx: 128 (over x, y, z, core).
Axes of the slice: x: 4, y: 4, z: 4, core: 2. Of those that a mesh axis runs over, the one named last changes fastest.
Arguments:
- tiles: bfloat16 [32768, 768], P('ctx'), may hold values from -6 to 6
- w_qkv: bfloat16 [768, 2304], replicated, may hold values from -1 to 1
- w_out: bfloat16 [768, 768], replicated, may hold values from -0.21875 to 0.21875
- cotangent: bfloat16 [32768, 768], P('ctx'), may hold values from -6 to 6
- offsets: int32 [2, 12], replicated, may hold values from 0 to 127, as said below
- pad_count: int32 [1], replicated, may hold values from 0 to 127
Outputs:
- out_rows: bfloat16 [32768, 768], P('ctx')
- grad_tiles: bfloat16 [32768, 768], P('ctx')
- grad_wqkv: float32 [768, 2304], P('ctx')
- grad_wout: float32 [768, 768], P('ctx')
The draws below stay inside these ranges and needn't reach their ends.
Inputs may be any that keep to these rules, and one draw needn't show every extreme that they name: offsets[0, h] is below 8; offsets[1, h] is below 128.
All inputs are finite; a program needn't handle non-finite values.
Results may differ from the reference program's by a relative error of at most 0.033.
Values may be sent and summed in bfloat16 or wider, within the bound.
A program may use at most 128 MiB of HBM per device.

```python
import jax
import jax.numpy as jnp
from jax import lax

D = 768
HEADS = 12
HEAD_DIM = 64
TOK_DEV = 256
GROUP = 8
TOKENS = 32768
N_CTX = 128


def offset_table(key):
    middle = jax.random.randint(jax.random.fold_in(key, 11), (HEADS,), 0, GROUP, dtype=jnp.int32)
    top = jax.random.randint(jax.random.fold_in(key, 12), (HEADS,), 0, TOKENS // TOK_DEV, dtype=jnp.int32)
    head_index = jnp.arange(HEADS, dtype=jnp.int32)
    low_head = jax.random.randint(jax.random.fold_in(key, 13), (), 0, HEADS, dtype=jnp.int32)
    high_head = jax.random.randint(jax.random.fold_in(key, 14), (), 0, HEADS, dtype=jnp.int32)
    middle = jnp.where(head_index == low_head, jnp.int32(0), middle)
    top = jnp.where(head_index == high_head, jnp.int32(TOKENS // TOK_DEV - 1), top)
    return jnp.stack([middle, top])


def draw_offsets(key, part):
    return offset_table(key)


def weight_table(key):
    drawn_weight = jax.random.truncated_normal(jax.random.fold_in(key, 21), -4.0, 4.0, (D, 3 * D), jnp.float32)
    drawn_weight = drawn_weight / jnp.sqrt(jnp.float32(D))
    return drawn_weight


def draw_w_qkv(key, part):
    drawn_weight = weight_table(key)
    return drawn_weight.astype(jnp.bfloat16)


def draw_tiles(key, part):
    return jax.random.truncated_normal(jax.random.fold_in(key, 30), -6.0, 6.0, (TOKENS, D), jnp.float32).astype(jnp.bfloat16)


def block_levels(rng, extent, cuts, smallest, high):
    level = 1.0
    for dim, blocks in cuts:
        draws = jax.random.uniform(jax.random.fold_in(jax.random.fold_in(rng, 6), dim), (blocks,), jnp.float32, smallest / len(cuts), high / len(cuts))
        level = level * jnp.repeat(jnp.exp(draws), extent[dim] // blocks).reshape((-1,) + (1,) * (len(extent) - 1 - dim))
    return level


def centred(own_key, extent, scale, reach, cuts=(), held_as=jnp.bfloat16):
    loudness = block_levels(own_key, extent, cuts, -0.22, 0.18) if cuts else 1.0
    entries = jax.random.normal(own_key, extent, jnp.float32) * scale * loudness
    return jnp.minimum(jnp.maximum(entries, -reach), reach).astype(held_as)


def setup_inputs(seed: int = 0) -> dict:
    arg_keys = jax.random.split(jax.random.key(seed), 7)
    return {
        "tiles": draw_tiles(jax.random.fold_in(arg_keys[6], 71), 0),
        "w_qkv": draw_w_qkv(jax.random.fold_in(arg_keys[6], 71), 0),
        "w_out": centred(arg_keys[2], (D, D), D ** -0.5, 0.21875),
        "cotangent": centred(arg_keys[3], (TOKENS, D), 1.0, 6.0, ((0, 128),)),
        "offsets": draw_offsets(jax.random.fold_in(arg_keys[6], 71), 0),
        "pad_count": jax.random.randint(arg_keys[5], (1,), 0, TOK_DEV // 2).astype(jnp.int32),
    }


scale_factor = 0.125


def rounded(array_in):
    return lax.optimization_barrier(array_in.astype(jnp.bfloat16)).astype(jnp.float32)


def pick_rows(array_in, stride, offsets_row):
    row_count = array_in.shape[0]
    blocked = array_in.reshape((row_count // stride, stride) + array_in.shape[1:])
    chosen = jnp.arange(stride, dtype=jnp.int32)[:, None] == offsets_row[None, :].astype(jnp.int32)
    chosen = chosen.reshape((1, stride, offsets_row.shape[0]) + (1,) * (array_in.ndim - 2))
    return jnp.sum(jnp.where(chosen, blocked, jnp.zeros((), array_in.dtype)), axis=1).astype(array_in.dtype)


def spread_rows(array_in, stride, offsets_row, fill):
    chosen = jnp.arange(stride, dtype=jnp.int32)[:, None] == offsets_row[None, :].astype(jnp.int32)
    chosen = chosen.reshape((1, stride, offsets_row.shape[0]) + (1,) * (array_in.ndim - 2))
    widened = jnp.where(chosen, array_in[:, None], jnp.asarray(fill, array_in.dtype))
    return widened.reshape((array_in.shape[0] * stride,) + array_in.shape[1:])


def masked_scores(queries, key_rows, key_valid):
    scores = jnp.einsum("nhe,mhe->hnm", queries.astype(jnp.float32), key_rows.astype(jnp.float32),
                        precision=lax.Precision.HIGHEST) * scale_factor
    return jnp.where(key_valid[:, None, :], scores, -jnp.inf)


def level_forward(queries, key_rows, value_rows, key_valid):
    scores = masked_scores(queries, key_rows, key_valid)
    peak = jnp.max(scores, axis=-1, keepdims=True)
    log_total = peak[..., 0] + jnp.log(jnp.sum(jnp.exp(scores - peak), axis=-1))
    weights = rounded(jnp.exp(scores - log_total[..., None]))
    mixed = jnp.einsum("hnm,mhe->nhe", weights, value_rows.astype(jnp.float32), precision=lax.Precision.HIGHEST)
    return mixed, log_total.T


def level_grads(queries, key_rows, value_rows, key_valid, log_total, grad_out, delta_rows):
    scores = masked_scores(queries, key_rows, key_valid)
    probs = jnp.exp(scores - log_total.T[:, :, None])
    grad_probs = jnp.einsum("nhe,mhe->hnm", grad_out.astype(jnp.float32), value_rows.astype(jnp.float32),
                            precision=lax.Precision.HIGHEST)
    grad_scores = rounded(probs * (grad_probs - delta_rows.T[:, :, None]))
    grad_query = scale_factor * jnp.einsum("hnm,mhe->nhe", grad_scores, key_rows.astype(jnp.float32),
                                           precision=lax.Precision.HIGHEST)
    grad_key = scale_factor * jnp.einsum("hnm,nhe->mhe", grad_scores, queries.astype(jnp.float32),
                                         precision=lax.Precision.HIGHEST)
    grad_value = jnp.einsum("hnm,nhe->mhe", rounded(probs), grad_out.astype(jnp.float32),
                            precision=lax.Precision.HIGHEST)
    return grad_query, grad_key, grad_value


def reference(tiles, w_qkv, w_out, cotangent, offsets, pad_count):
    token_count = tiles.shape[0]
    shaped = (token_count, HEADS, HEAD_DIM)
    packed = jnp.dot(tiles, w_qkv, preferred_element_type=jnp.float32).astype(jnp.bfloat16)
    queries = packed[:, :D].reshape(shaped)
    key_all = packed[:, D:2 * D].reshape(shaped)
    value_all = packed[:, 2 * D:].reshape(shaped)
    limit = token_count - pad_count[0]
    levels = ((1, jnp.zeros((HEADS,), jnp.int32)), (GROUP, offsets[0]), (N_CTX, offsets[1]))

    def segments_of(array_in, stride, offs):
        picked = pick_rows(array_in, stride, offs)
        return picked.reshape((picked.shape[0] // TOK_DEV, TOK_DEV) + picked.shape[1:])

    def valid_of(stride, offs):
        selected = token_count // stride
        key_pos = jnp.arange(selected, dtype=jnp.int32)[:, None] * stride + offs[None, :].astype(jnp.int32)
        return (key_pos < limit).reshape(selected // TOK_DEV, TOK_DEV, HEADS).transpose(0, 2, 1)

    mixed_levels = []
    lse_levels = []
    for stride, offs in levels:
        parts = (segments_of(queries, stride, offs), segments_of(key_all, stride, offs),
                 segments_of(value_all, stride, offs), valid_of(stride, offs))
        mixed, lse_part = lax.map(lambda block: level_forward(*block), parts)
        mixed_levels.append(spread_rows(mixed.reshape(-1, HEADS, HEAD_DIM), stride, offs, 0.0))
        lse_levels.append(spread_rows(lse_part.reshape(-1, HEADS), stride, offs, -jnp.inf))
    log_total = jnp.logaddexp(jnp.logaddexp(lse_levels[0], lse_levels[1]), lse_levels[2])
    combined = jnp.exp(lse_levels[0] - log_total)[..., None] * mixed_levels[0]
    combined = combined + jnp.exp(lse_levels[1] - log_total)[..., None] * mixed_levels[1]
    combined = combined + jnp.exp(lse_levels[2] - log_total)[..., None] * mixed_levels[2]
    attn = combined.astype(jnp.bfloat16).reshape(token_count, D)
    out_rows = (tiles.astype(jnp.float32) + jnp.dot(attn, w_out, preferred_element_type=jnp.float32)).astype(jnp.bfloat16)
    grad_attn = jnp.dot(cotangent, w_out.T, preferred_element_type=jnp.float32).astype(jnp.bfloat16)
    grad_wout = jnp.dot(attn.T, cotangent, preferred_element_type=jnp.float32)
    grad_heads = grad_attn.reshape(shaped)
    delta_rows = jnp.sum(grad_heads.astype(jnp.float32) * attn.reshape(shaped).astype(jnp.float32), axis=-1)
    grad_sums = None
    for stride, offs in levels:
        parts = (segments_of(queries, stride, offs), segments_of(key_all, stride, offs),
                 segments_of(value_all, stride, offs), valid_of(stride, offs),
                 segments_of(log_total, stride, offs), segments_of(grad_heads, stride, offs),
                 segments_of(delta_rows, stride, offs))
        results = lax.map(lambda block: level_grads(*block), parts)
        spread = [spread_rows(item.reshape(-1, HEADS, HEAD_DIM), stride, offs, 0.0) for item in results]
        grad_sums = spread if grad_sums is None else [grad_sums[i] + spread[i] for i in range(3)]
    grad_packed = jnp.concatenate([item.reshape(token_count, D) for item in grad_sums], axis=1).astype(jnp.bfloat16)
    grad_tiles = jnp.dot(grad_packed, w_qkv.T, preferred_element_type=jnp.float32).astype(jnp.bfloat16)
    grad_wqkv = jnp.dot(tiles.T, grad_packed, preferred_element_type=jnp.float32)
    return out_rows, grad_tiles, grad_wqkv, grad_wout
```

```python
import jax
import jax.numpy as jnp
from jax import lax
from jax.experimental import pallas as pl
from jax.experimental.pallas import tpu as pltpu
from jax.sharding import PartitionSpec as P

MESH = pl.DeviceIdType.MESH
N = 256
D = 768
H = 12
E = 64
NEG = -1e30
F32 = jnp.float32
BF = jnp.bfloat16
I32 = jnp.int32


def dot(a, b, ca, cb, precision=None):
    dims = (((ca,), (cb,)), ((), ()))
    return lax.dot_general(a, b, dims, precision=precision, preferred_element_type=F32)


def nn(a, b):
    return dot(a, b, 1, 0)


def nt(a, b):
    return dot(a, b, 1, 1)


def tn(a, b):
    return dot(a, b, 0, 0)


def iota(shape, dim):
    return lax.broadcasted_iota(I32, shape, dim)


def head_mask(h, dtype):
    return jnp.where(iota((1, D), 1) // E == h, 1.0, 0.0).astype(dtype)


def block_diag(x):
    return jnp.concatenate([x * head_mask(h, x.dtype) for h in range(H)], axis=0)


def diag_sum(x, rows):
    head = iota((rows, D), 1) // E
    out = jnp.zeros((rows, D), F32)
    for h in range(H):
        out = jnp.where(head == h, x[h * rows : (h + 1) * rows], out)
    return out


def per_head(cols, rows):
    head = iota((rows, D), 1) // E
    out = jnp.zeros((rows, D), F32)
    for h in range(H):
        out = jnp.where(head == h, cols[h * rows : (h + 1) * rows], out)
    return out


def kernel(
    offs, pad, tiles, wqkv, wout, cot,
    out_rows, grad_tiles, g_qkv, g_out,
    pk, midm, farm, emat, num, den, mx,
    gkv, gqd, gst, far1kv, far1qd, far1st, far2kv, far2qd, far2st,
    floc, mnum, mden, mmax, fnum, fden, fmax, emid, efar,
    attn, sdo, npr, mlse, mprod, flse, fprod,
    dq, dk, dv, dmid, dfar, gp, tilest, attnt,
    f1s, f1r, f2s, f2r, f3s, f3r, m1s, m1r, m2s, m2r,
):
    me = lax.axis_index("ctx")
    c = me % 2
    z = me // 2 % 4
    g = me // 8
    part = g * 8 + z * 2 + (1 - c)

    def zpeer(k):
        return g * 8 + (z + k) % 4 * 2 + c

    def gpeer(k):
        return (g + k) % 16 * 8 + z * 2 + c

    def rc(src, dst, ss, rs, dev):
        return pltpu.make_async_remote_copy(
            src_ref=src, dst_ref=dst, send_sem=ss, recv_sem=rs, device_id=(dev,), device_id_type=MESH
        )

    barrier = pltpu.get_barrier_semaphore()
    peers = [part] + [zpeer(k) for k in (1, 2, 3)] + [gpeer(k) for k in range(1, 16)]
    for p in peers:
        pl.semaphore_signal(barrier, inc=1, device_id=(p,), device_id_type=MESH)
    pl.semaphore_wait(barrier, len(peers))

    FAR1 = (far1kv, far1qd, far1st)
    FAR2 = (far2kv, far2qd, far2st)
    MID = (gkv, gqd, gst)

    def f1_copy(t, k):
        return rc(FAR1[t].at[z], FAR1[t].at[z], f1s.at[t, k], f1r.at[t, z], zpeer(k))

    def f1_start(t):
        for k in (1, 3, 2):
            f1_copy(t, k).start()

    def f1_wait(t):
        for k in (1, 3, 2):
            o = (z + k) % 4
            rc(FAR1[t].at[o], FAR1[t].at[o], f1s.at[t, k], f1r.at[t, o], zpeer(k)).wait_recv()

    def f2_copy(t, k):
        return rc(FAR2[t].at[c, g], FAR2[t].at[c, g], f2s.at[t, k], f2r.at[t, g], gpeer(k))

    def f2_start(t):
        a = FAR1[t]
        FAR2[t][c, g] = (
            a[0].astype(F32) + a[1].astype(F32) + a[2].astype(F32) + a[3].astype(F32)
        ).astype(a.dtype)
        for k in range(1, 16):
            f2_copy(t, k).start()

    def f2_wait(t):
        for k in range(1, 16):
            o = (g + k) % 16
            rc(FAR2[t].at[c, o], FAR2[t].at[c, o], f2s.at[t, k], f2r.at[t, o], gpeer(k)).wait_recv()

    def f3_copy(t):
        return rc(FAR2[t].at[c], FAR2[t].at[c], f3s.at[t], f3r.at[t], part)

    def f3_wait(t):
        rc(FAR2[t].at[1 - c], FAR2[t].at[1 - c], f3s.at[t], f3r.at[t], part).wait_recv()

    def m1_copy(t, k):
        return rc(MID[t].at[c, z], MID[t].at[c, z], m1s.at[t, k], m1r.at[t, z], zpeer(k))

    def m2_copy(t, k):
        o = (z + k) % 4
        return rc(MID[t].at[c, o], MID[t].at[c, o], m2s.at[t, k], m2r.at[t, o], part)

    def m1_start(t):
        for k in (1, 3, 2):
            m1_copy(t, k).start()
        m2_copy(t, 0).start()

    def m1_forward(t):
        for k in (1, 3, 2):
            o = (z + k) % 4
            rc(MID[t].at[c, o], MID[t].at[c, o], m1s.at[t, k], m1r.at[t, o], zpeer(k)).wait_recv()
            m2_copy(t, k).start()

    def m2_wait(t):
        for k in range(4):
            o = (z + k) % 4
            rc(MID[t].at[1 - c, o], MID[t].at[1 - c, o], m2s.at[t, k], m2r.at[t, o], part).wait_recv()

    limit = N * 128 - pad[0]
    lane_head = iota((1, D), 1) // E
    o0 = jnp.zeros((1, D), I32)
    o1 = jnp.zeros((1, D), I32)
    for h in range(H):
        o0 = jnp.where(lane_head == h, offs[0, h], o0)
        o1 = jnp.where(lane_head == h, offs[1, h], o1)
    midm[...] = jnp.where(iota((N, D), 0) % 8 == o0, 1.0, 0.0).astype(BF)
    farm[...] = jnp.where(iota((N, D), 0) % 128 == o1, 1.0, 0.0).astype(BF)

    pool_mid = jnp.where(iota((32, N), 1) // 8 == iota((32, N), 0), 1.0, 0.0).astype(BF)
    two = iota((16, N), 1) // 128
    row = iota((16, N), 0)
    pool_far = jnp.where(row == two, 1.0, 0.0).astype(BF)
    place = jnp.concatenate(
        [
            jnp.where(row == 2 * z + two, 1.0, 0.0),
            jnp.where(row == 8 + 2 * z + two, 1.0, 0.0),
        ],
        axis=1,
    ).astype(BF)

    def picks(t, i, a, b):
        ls = pl.ds(pl.multiple_of(i * N, N), N)
        hi = pl.ds(pl.multiple_of(D + i * N, N), N)
        mk = midm[:, ls]
        fk = farm[:, ls]
        fa = a * fk
        fb = b * fk
        FAR1[t][z, :, ls] = nn(place, jnp.concatenate([fa, fb], axis=0)).astype(BF)
        MID[t][c, z, :, ls] = nn(pool_mid, a * mk).astype(BF)
        MID[t][c, z, :, hi] = nn(pool_mid, b * mk).astype(BF)
        floc[2 * t, :, ls] = nn(pool_far, fa).astype(BF)
        floc[2 * t + 1, :, ls] = nn(pool_far, fb).astype(BF)

    @pl.loop(0, 3)
    def _(i):
        kc = pl.ds(pl.multiple_of(D + i * N, N), N)
        vc = pl.ds(pl.multiple_of(2 * D + i * N, N), N)
        x = tiles[...]
        kk = nn(x, wqkv[:, kc]).astype(BF)
        vv = nn(x, wqkv[:, vc]).astype(BF)
        pk[:, kc] = kk
        pk[:, vc] = vv
        picks(0, i, kk, vv)

    f1_start(0)
    m1_start(0)

    @pl.loop(0, 3)
    def _(i):
        qc = pl.ds(pl.multiple_of(i * N, N), N)
        dc = pl.ds(pl.multiple_of(3 * D + i * N, N), N)
        qq = nn(tiles[...], wqkv[:, qc]).astype(BF) * jnp.asarray(0.125, BF)
        dd = nt(cot[...], wout[qc, :]).astype(BF)
        pk[:, qc] = qq
        pk[:, dc] = dd
        picks(1, i, qq, dd)

    f1_start(1)
    m1_start(1)

    half = iota((1, 128), 1) // E
    hm = [jnp.where(half == a, 1.0, 0.0).astype(BF) for a in range(2)]

    def lanes(p, base=0):
        return pl.ds(pl.multiple_of(base + p * 128, 128), 128)

    def near_forward(lo, hi):
        @pl.loop(lo, hi)
        def _(p):
            q2 = pk[:, lanes(p)]
            k2 = pk[:, lanes(p, D)]
            v2 = pk[:, lanes(p, 2 * D)]
            bias = jnp.where(me * N + iota((1, N), 1) < limit, 0.0, NEG)
            es, ms = [], []
            for a in range(2):
                s = nt(q2 * hm[a], k2) + bias
                m = jnp.max(s, axis=1, keepdims=True)
                e = jnp.exp(s - m).astype(BF)
                emat[2 * p + a] = e
                es.append(e)
                ms.append(m)
            rhs = jnp.concatenate(
                [
                    jnp.concatenate([v2 * hm[a], jnp.broadcast_to(hm[a], (N, 128))], axis=1)
                    for a in range(2)
                ],
                axis=0,
            )
            nd = nn(jnp.concatenate(es, axis=1), rhs)
            num[:, lanes(p)] = nd[:, :128]
            den[:, lanes(p)] = nd[:, 128:]
            mx[:, lanes(p)] = jnp.where(iota((N, 128), 1) < E, ms[0], ms[1])

    near_forward(0, 2)
    f1_wait(0)
    f2_start(0)
    near_forward(2, 4)
    m1_forward(0)
    f1_wait(1)
    f2_start(1)
    near_forward(4, 6)
    tilest[...] = tiles[...].T

    m2_wait(0)
    kg = gkv[:, :, :, :D].reshape(N, D)
    vg = gkv[:, :, :, D:].reshape(N, D)
    gdev = g * 8 + iota((32, N), 1) // 32 % 4 * 2 + iota((32, N), 1) // 128
    gpos = gdev * N + iota((32, N), 1) % 32 * 8
    gbias = jnp.concatenate(
        [jnp.where(gpos + offs[0, h] < limit, 0.0, NEG) for h in range(H)], axis=0
    )
    s = nt(block_diag(gqd[c, z, :, :D]), kg) + gbias
    m = jnp.max(s, axis=1, keepdims=True)
    e = jnp.exp(s - m)
    total = jnp.sum(e, axis=1, keepdims=True)
    e = e.astype(BF)
    emid[...] = e
    mnum[...] = diag_sum(nn(e, vg), 32)
    mden[...] = per_head(total, 32)
    mmax[...] = per_head(m, 32)

    f2_wait(0)
    f3_copy(0).start()
    m1_forward(1)
    f3_wait(0)

    col = iota((16, 512), 1)
    fdev = col // 16 % 16 * 8 + col // 2 % 4 * 2 + col // 256
    fpos = (fdev * 2 + col % 2) * 128
    lead = col // 8 % 2 == 0
    fbias = jnp.concatenate(
        [
            jnp.where(jnp.logical_and(lead, fpos + offs[1, h] < limit), 0.0, NEG)
            for h in range(H)
        ],
        axis=0,
    )
    kvf = far2kv[...].reshape(512, D)
    s = nt(block_diag(floc[2]), kvf) + fbias
    m = jnp.max(s, axis=1, keepdims=True)
    e = jnp.exp(s - m)
    efar[...] = e
    fnum[...] = diag_sum(nn(pltpu.roll(e, 8, 1).astype(BF), kvf), 16)
    fden[...] = per_head(jnp.sum(e, axis=1, keepdims=True), 16)
    fmax[...] = per_head(m, 16)

    def spread_mid(x):
        return jnp.broadcast_to(x[:, None, :], (32, 8, 128)).reshape(N, 128)

    def spread_far(x):
        return jnp.concatenate(
            [jnp.broadcast_to(x[0:1], (128, 128)), jnp.broadcast_to(x[1:2], (128, 128))], axis=0
        )

    def pick_mid(x):
        return jnp.sum(x.reshape(32, 8, 128), axis=1)

    def pick_far(x):
        return jnp.concatenate(
            [
                jnp.sum(x[:128], axis=0, keepdims=True),
                jnp.sum(x[128:], axis=0, keepdims=True),
                jnp.zeros((14, 128), F32),
            ],
            axis=0,
        )

    @pl.loop(0, 6)
    def _(p):
        ls = lanes(p)
        mm = midm[:, ls].astype(F32)
        fm = farm[:, ls].astype(F32)
        m0 = mx[:, ls]
        m1 = jnp.where(mm > 0.5, spread_mid(mmax[:, ls]), NEG)
        m2 = jnp.where(fm > 0.5, spread_far(fmax[0:2, ls]), NEG)
        top = jnp.maximum(jnp.maximum(m0, m1), m2)
        w0 = jnp.exp(m0 - top)
        w1 = jnp.exp(m1 - top)
        w2 = jnp.exp(m2 - top)
        total = w0 * den[:, ls] + w1 * spread_mid(mden[:, ls]) + w2 * spread_far(fden[0:2, ls])
        inv = 1.0 / total
        mixed = w0 * num[:, ls] + w1 * spread_mid(mnum[:, ls]) + w2 * spread_far(fnum[0:2, ls])
        at = (mixed * inv).astype(BF)
        attn[:, ls] = at
        do = pk[:, lanes(p, 3 * D)].astype(F32)
        prod = do * at.astype(F32)
        scale = w0 * inv
        sdo[:, ls] = (scale * do).astype(BF)
        npr[:, ls] = (-scale * prod).astype(BF)
        lse = top + jnp.log(total)
        mlse[:, ls] = pick_mid(lse * mm)
        mprod[:, ls] = pick_mid(prod * mm)
        flse[:, ls] = pick_far(lse * fm)
        fprod[:, ls] = pick_far(prod * fm)

    hi = lax.Precision.HIGHEST
    r0 = iota((D, 128), 0)
    l0 = iota((D, 128), 1)
    sel1 = jnp.where(jnp.logical_and(r0 == l0 * E, l0 < H), 1.0, 0.0)
    sel2 = jnp.where(r0 // E == l0 - H, 1.0, 0.0)
    gst[c, z] = dot(mlse[...], sel1, 1, 0, hi) + dot(mprod[...], sel2, 1, 0, hi)
    fs = dot(flse[...], sel1, 1, 0, hi) + dot(fprod[...], sel2, 1, 0, hi)
    r16 = iota((16, 128), 0)
    far1st[z] = jnp.where(r16 == 2 * z, fs[0:1], jnp.where(r16 == 2 * z + 1, fs[1:2], 0.0))
    f1_start(2)
    m1_start(2)

    attnt[...] = attn[...].T

    @pl.loop(0, 3)
    def _(i):
        ls = pl.ds(pl.multiple_of(i * N, N), N)
        g_out[:, ls] = nn(attnt[...], cot[:, ls])
        out_rows[:, ls] = (tiles[:, ls].astype(F32) + nn(attn[...], wout[:, ls])).astype(BF)

    def near_backward(lo, hi_):
        @pl.loop(lo, hi_)
        def _(p):
            ls = lanes(p)
            q2 = pk[:, ls]
            k2 = pk[:, lanes(p, D)]
            v2 = pk[:, lanes(p, 2 * D)]
            so = sdo[:, ls]
            sp = npr[:, ls]
            rhs = jnp.concatenate([v2, jnp.ones((N, 128), BF)], axis=1)
            es, ds = [], []
            for a in range(2):
                lhs = jnp.concatenate([so * hm[a], sp * hm[a]], axis=1)
                t = nt(lhs, rhs)
                e = emat[2 * p + a]
                es.append(e)
                ds.append((e.astype(F32) * t).astype(BF))
            dq[:, ls] = 0.125 * nn(
                jnp.concatenate(ds, axis=1), jnp.concatenate([k2 * hm[0], k2 * hm[1]], axis=0)
            )
            dk[:, ls] = tn(
                jnp.concatenate(ds, axis=0), jnp.concatenate([q2 * hm[0], q2 * hm[1]], axis=0)
            )
            dv[:, ls] = tn(
                jnp.concatenate(es, axis=0), jnp.concatenate([so * hm[0], so * hm[1]], axis=0)
            )

    near_backward(0, 2)
    f1_wait(2)
    f2_start(2)
    m1_forward(2)
    near_backward(2, 6)

    kg = gkv[:, :, :, :D].reshape(N, D)
    vg = gkv[:, :, :, D:].reshape(N, D)
    scale = jnp.exp(mmax[...] - mlse[...])
    so = (scale * gqd[c, z, :, D:].astype(F32)).astype(BF)
    sp = scale * mprod[...]
    dl = jnp.concatenate(
        [jnp.sum(sp * head_mask(h, F32), axis=1, keepdims=True) for h in range(H)], axis=0
    )
    ds = (emid[...].astype(F32) * (nt(block_diag(so), vg) - dl)).astype(BF)
    dmid[0] = 0.125 * diag_sum(nn(ds, kg), 32)

    scale = jnp.exp(fmax[...] - flse[...])
    so = (scale * floc[3].astype(F32)).astype(BF)
    sp = scale * fprod[...]
    dl = jnp.concatenate(
        [jnp.sum(sp * head_mask(h, F32), axis=1, keepdims=True) for h in range(H)], axis=0
    )
    kvf = far2kv[...].reshape(512, D)
    t = pltpu.roll(nt(block_diag(so), kvf), 504, 1)
    dfar[0] = 0.125 * diag_sum(nn((efar[...] * (t - dl)).astype(BF), kvf), 16)

    f2_wait(1)
    f3_copy(1).start()
    m2_wait(1)
    f2_wait(2)
    f3_copy(2).start()
    m2_wait(2)

    hs = iota((16, 128), 1)
    hr = iota((16, 128), 0)
    pick1 = jnp.where(hs == hr, 1.0, 0.0)
    pick2 = jnp.where(hs == hr + H, 1.0, 0.0)
    st = gst[...].reshape(N, 128)
    ls_rows = dot(pick1, st, 1, 1, hi)
    dl_rows = dot(pick2, st, 1, 1, hi)
    qg = gqd[:, :, :, :D].reshape(N, D)
    og = gqd[:, :, :, D:].reshape(N, D)
    s = nt(block_diag(gkv[c, z, :, :D]), qg)
    t = nt(block_diag(gkv[c, z, :, D:]), og)
    ps, dss = [], []
    for h in range(H):
        ok = me * N + iota((32, N), 0) * 8 + offs[0, h] < limit
        p = jnp.exp(jnp.where(ok, s[h * 32 : (h + 1) * 32] - ls_rows[h : h + 1], NEG))
        ps.append(p.astype(BF))
        dss.append((p * (t[h * 32 : (h + 1) * 32] - dl_rows[h : h + 1])).astype(BF))
    dmid[1] = diag_sum(nn(jnp.concatenate(dss, axis=0), qg), 32)
    dmid[2] = diag_sum(nn(jnp.concatenate(ps, axis=0), og), 32)

    f3_wait(1)
    f3_wait(2)
    st = far2st[...].reshape(512, 128)
    ls_rows = dot(pick1, st, 1, 1, hi)
    dl_rows = dot(pick2, st, 1, 1, hi)
    qdf = far2qd[...].reshape(512, D)
    s = nt(block_diag(floc[0]), qdf)
    t = pltpu.roll(nt(block_diag(floc[1]), qdf), 504, 1)
    ps, dss = [], []
    rr = iota((16, 512), 0)
    for h in range(H):
        ok = jnp.logical_and((me * 2 + rr) * 128 + offs[1, h] < limit, jnp.logical_and(lead, rr < 2))
        p = jnp.exp(jnp.where(ok, s[h * 16 : (h + 1) * 16] - ls_rows[h : h + 1], NEG))
        ps.append(p)
        dss.append((p * (t[h * 16 : (h + 1) * 16] - dl_rows[h : h + 1])).astype(BF))
    dfar[1] = diag_sum(nn(jnp.concatenate(dss, axis=0), qdf), 16)
    pall = pltpu.roll(jnp.concatenate(ps, axis=0), 8, 1).astype(BF)
    dfar[2] = diag_sum(nn(pall, qdf), 16)

    @pl.loop(0, 6)
    def _(p):
        ls = lanes(p)
        mm = midm[:, ls].astype(F32)
        fm = farm[:, ls].astype(F32)
        for a, near in enumerate((dq, dk, dv)):
            v = near[:, ls] + mm * spread_mid(dmid[a, :, ls]) + fm * spread_far(dfar[a, 0:2, ls])
            gp[:, lanes(p, a * D)] = v.astype(BF)

    @pl.loop(0, 9)
    def _(i):
        ls = pl.ds(pl.multiple_of(i * N, N), N)
        g_qkv[:, ls] = nn(tilest[...], gp[:, ls])

    @pl.loop(0, 3)
    def _(i):
        ls = pl.ds(pl.multiple_of(i * N, N), N)
        grad_tiles[:, ls] = nt(gp[...], wqkv[ls, :]).astype(BF)

    for t in range(3):
        for k in (1, 2, 3):
            f1_copy(t, k).wait_send()
            m1_copy(t, k).wait_send()
        for k in range(1, 16):
            f2_copy(t, k).wait_send()
        f3_copy(t).wait_send()
        for k in range(4):
            m2_copy(t, k).wait_send()


def per_device(tiles, w_qkv, w_out, cotangent, offsets, pad_count):
    vm = pl.BlockSpec(memory_space=pltpu.VMEM)
    sm = pl.BlockSpec(memory_space=pltpu.SMEM)
    V = pltpu.VMEM
    dma = pltpu.SemaphoreType.DMA
    big = V((N, D), F32)
    bigb = V((N, D), BF)
    m32 = V((32, D), F32)
    f16 = V((16, D), F32)
    out_rows, grad_tiles, g_qkv, g_out = pl.pallas_call(
        kernel,
        out_shape=(
            jax.ShapeDtypeStruct((N, D), BF),
            jax.ShapeDtypeStruct((N, D), BF),
            jax.ShapeDtypeStruct((D, 3 * D), F32),
            jax.ShapeDtypeStruct((D, D), F32),
        ),
        in_specs=[sm, sm, vm, vm, vm, vm],
        out_specs=(vm, vm, vm, vm),
        scratch_shapes=[
            V((N, 4 * D), BF), bigb, bigb, V((H, N, N), BF), big, big, big,
            V((2, 4, 32, 2 * D), BF), V((2, 4, 32, 2 * D), BF), V((2, 4, 32, 128), F32),
            V((4, 16, D), BF), V((4, 16, D), BF), V((4, 16, 128), F32),
            V((2, 16, 16, D), BF), V((2, 16, 16, D), BF), V((2, 16, 16, 128), F32),
            V((4, 16, D), BF), m32, m32, m32, f16, f16, f16, V((H * 32, N), BF), V((H * 16, 512), F32),
            bigb, bigb, bigb, m32, m32, f16, f16,
            big, big, big, V((3, 32, D), F32), V((3, 16, D), F32), V((N, 3 * D), BF),
            V((D, N), BF), V((D, N), BF),
            dma((3, 4)), dma((3, 4)), dma((3, 16)), dma((3, 16)), dma((3,)), dma((3,)),
            dma((3, 4)), dma((3, 4)), dma((3, 4)), dma((3, 4)),
        ],
        compiler_params=pltpu.CompilerParams(
            collective_id=0, has_side_effects=True, vmem_limit_bytes=60 * 1024 * 1024
        ),
        name="layer",
    )(offsets, pad_count, tiles, w_qkv, w_out, cotangent)
    grad = jnp.concatenate([g_qkv, g_out], axis=1)
    mine = lax.psum_scatter(grad, "ctx", scatter_dimension=0, tiled=True)
    return out_rows, grad_tiles, mine[:, : 3 * D], mine[:, 3 * D :]


def solution(mesh):
    row = P("ctx", None)
    return jax.shard_map(
        per_device,
        mesh=mesh,
        in_specs=(row, P(), P(), row, P(), P()),
        out_specs=(row, row, row, row),
        check_vma=False,
    )
```

```python
import jax
import jax.numpy as jnp
from jax import lax
from jax.experimental import pallas as pl
from jax.experimental.pallas import tpu as pltpu
from jax.sharding import PartitionSpec as P

MESH = pl.DeviceIdType.MESH
N = 256
D = 768
H = 12
E = 64
NEG = -1e30
F32 = jnp.float32
BF = jnp.bfloat16
I32 = jnp.int32


def dot(a, b, ca, cb, precision=None):
    dims = (((ca,), (cb,)), ((), ()))
    return lax.dot_general(a, b, dims, precision=precision, preferred_element_type=F32)


def nn(a, b):
    return dot(a, b, 1, 0)


def nt(a, b):
    return dot(a, b, 1, 1)


def tn(a, b):
    return dot(a, b, 0, 0)


def iota(shape, dim):
    return lax.broadcasted_iota(I32, shape, dim)


def head_mask(h, dtype):
    return jnp.where(iota((1, D), 1) // E == h, 1.0, 0.0).astype(dtype)


def block_diag(x):
    return jnp.concatenate([x * head_mask(h, x.dtype) for h in range(H)], axis=0)


def diag_sum(x, rows):
    head = iota((rows, D), 1) // E
    out = jnp.zeros((rows, D), F32)
    for h in range(H):
        out = jnp.where(head == h, x[h * rows : (h + 1) * rows], out)
    return out


def per_head(cols, rows):
    head = iota((rows, D), 1) // E
    out = jnp.zeros((rows, D), F32)
    for h in range(H):
        out = jnp.where(head == h, cols[h * rows : (h + 1) * rows], out)
    return out


def kernel(
    offs, pad, tiles, wqkv, wout, cot,
    out_rows, grad_tiles, g_qkv, g_out,
    pk, midm, farm, emat, num, den, mx,
    gkv, gqd, gst, far1kv, far1qd, far1st, far2kv, far2qd, far2st,
    floc, mnum, mden, mmax, fnum, fden, fmax, emid, efar,
    attn, sdo, npr, mlse, mprod, flse, fprod,
    dq, dk, dv, dmid, dfar, gp, tilest, attnt, cotr, gph, gpr,
    part, ra1, rb1, rc1, ta, tb, tc, ra2, rb2, rc2, acca, accb, accc,
    sa2, sb2, sc2, acca2, accb2, accc2, sa3, sb3, sc3, fin, finr,
    f1s, f1r, f2s, f2r, f3s, f3r, m1s, m1r, m2s, m2r,
    xs, xr, rs, rr_, ss, sr, es_, er_,
):
    me = lax.axis_index("ctx")
    c = me % 2
    z = me // 2 % 4
    g = me // 8
    x = g // 4
    y = g % 4
    mate = g * 8 + z * 2 + (1 - c)

    def zpeer(k):
        return g * 8 + (z + k) % 4 * 2 + c

    def gpeer(k):
        return (g + k) % 16 * 8 + z * 2 + c

    def rc(src, dst, ss, rs, dev):
        return pltpu.make_async_remote_copy(
            src_ref=src, dst_ref=dst, send_sem=ss, recv_sem=rs, device_id=(dev,), device_id_type=MESH
        )

    barrier = pltpu.get_barrier_semaphore()
    peers = [mate] + [zpeer(k) for k in (1, 2, 3)] + [gpeer(k) for k in range(1, 16)]
    peers += [g * 8 + (z + k) % 4 * 2 + (1 - c) for k in (1, 2, 3)]
    for p in peers:
        pl.semaphore_signal(barrier, inc=1, device_id=(p,), device_id_type=MESH)
    pl.semaphore_wait(barrier, len(peers))

    FAR1 = (far1kv, far1qd, far1st)
    FAR2 = (far2kv, far2qd, far2st)
    MID = (gkv, gqd, gst)

    def f1_copy(t, k):
        return rc(FAR1[t].at[z], FAR1[t].at[z], f1s.at[t, k], f1r.at[t, z], zpeer(k))

    def f1_start(t):
        for k in (1, 3, 2):
            f1_copy(t, k).start()

    def f1_wait(t):
        for k in (1, 3, 2):
            o = (z + k) % 4
            rc(FAR1[t].at[o], FAR1[t].at[o], f1s.at[t, k], f1r.at[t, o], zpeer(k)).wait_recv()

    def f2_copy(t, k):
        return rc(FAR2[t].at[c, g], FAR2[t].at[c, g], f2s.at[t, k], f2r.at[t, g], gpeer(k))

    def f2_start(t):
        a = FAR1[t]
        FAR2[t][c, g] = (
            a[0].astype(F32) + a[1].astype(F32) + a[2].astype(F32) + a[3].astype(F32)
        ).astype(a.dtype)
        for k in range(1, 16):
            f2_copy(t, k).start()

    def f2_wait(t):
        for k in range(1, 16):
            o = (g + k) % 16
            rc(FAR2[t].at[c, o], FAR2[t].at[c, o], f2s.at[t, k], f2r.at[t, o], gpeer(k)).wait_recv()

    def f3_copy(t):
        return rc(FAR2[t].at[c], FAR2[t].at[c], f3s.at[t], f3r.at[t], mate)

    def f3_wait(t):
        rc(FAR2[t].at[1 - c], FAR2[t].at[1 - c], f3s.at[t], f3r.at[t], mate).wait_recv()

    def m1_copy(t, k):
        return rc(MID[t].at[c, z], MID[t].at[c, z], m1s.at[t, k], m1r.at[t, z], zpeer(k))

    def m2_copy(t, k):
        o = (z + k) % 4
        return rc(MID[t].at[c, o], MID[t].at[c, o], m2s.at[t, k], m2r.at[t, o], mate)

    def m1_start(t):
        for k in (1, 3, 2):
            m1_copy(t, k).start()
        m2_copy(t, 0).start()

    def m1_forward(t):
        for k in (1, 3, 2):
            o = (z + k) % 4
            rc(MID[t].at[c, o], MID[t].at[c, o], m1s.at[t, k], m1r.at[t, o], zpeer(k)).wait_recv()
            m2_copy(t, k).start()

    def m2_wait(t):
        for k in range(4):
            o = (z + k) % 4
            rc(MID[t].at[1 - c, o], MID[t].at[1 - c, o], m2s.at[t, k], m2r.at[t, o], mate).wait_recv()

    def to_mate(t, src, dst):
        return rc(src, dst, xs.at[t], xr.at[t], mate)

    half_cols = pl.ds(pl.multiple_of(384 * (1 - c), 128), 384)
    own_cols = pl.ds(pl.multiple_of(384 * c, 128), 384)
    to_mate(0, cot.at[:, half_cols], cotr).start()

    limit = N * 128 - pad[0]
    lane_head = iota((1, D), 1) // E
    o0 = jnp.zeros((1, D), I32)
    o1 = jnp.zeros((1, D), I32)
    for h in range(H):
        o0 = jnp.where(lane_head == h, offs[0, h], o0)
        o1 = jnp.where(lane_head == h, offs[1, h], o1)
    midm[...] = jnp.where(iota((N, D), 0) % 8 == o0, 1.0, 0.0).astype(BF)
    farm[...] = jnp.where(iota((N, D), 0) % 128 == o1, 1.0, 0.0).astype(BF)

    pool_mid = jnp.where(iota((32, N), 1) // 8 == iota((32, N), 0), 1.0, 0.0).astype(BF)
    two = iota((16, N), 1) // 128
    row = iota((16, N), 0)
    pool_far = jnp.where(row == two, 1.0, 0.0).astype(BF)
    place = jnp.concatenate(
        [
            jnp.where(row == 2 * z + two, 1.0, 0.0),
            jnp.where(row == 8 + 2 * z + two, 1.0, 0.0),
        ],
        axis=1,
    ).astype(BF)

    def picks(t, i, a, b):
        ls = pl.ds(pl.multiple_of(i * N, N), N)
        hi = pl.ds(pl.multiple_of(D + i * N, N), N)
        mk = midm[:, ls]
        fk = farm[:, ls]
        fa = a * fk
        fb = b * fk
        FAR1[t][z, :, ls] = nn(place, jnp.concatenate([fa, fb], axis=0)).astype(BF)
        MID[t][c, z, :, ls] = nn(pool_mid, a * mk).astype(BF)
        MID[t][c, z, :, hi] = nn(pool_mid, b * mk).astype(BF)
        floc[2 * t, :, ls] = nn(pool_far, fa).astype(BF)
        floc[2 * t + 1, :, ls] = nn(pool_far, fb).astype(BF)

    @pl.loop(0, 3)
    def _(i):
        kc = pl.ds(pl.multiple_of(D + i * N, N), N)
        vc = pl.ds(pl.multiple_of(2 * D + i * N, N), N)
        x = tiles[...]
        kk = nn(x, wqkv[:, kc]).astype(BF)
        vv = nn(x, wqkv[:, vc]).astype(BF)
        pk[:, kc] = kk
        pk[:, vc] = vv
        picks(0, i, kk, vv)

    f1_start(0)
    m1_start(0)

    @pl.loop(0, 3)
    def _(i):
        qc = pl.ds(pl.multiple_of(i * N, N), N)
        dc = pl.ds(pl.multiple_of(3 * D + i * N, N), N)
        qq = nn(tiles[...], wqkv[:, qc]).astype(BF) * jnp.asarray(0.125, BF)
        dd = nt(cot[...], wout[qc, :]).astype(BF)
        pk[:, qc] = qq
        pk[:, dc] = dd
        picks(1, i, qq, dd)

    f1_start(1)
    m1_start(1)

    half = iota((1, 128), 1) // E
    hm = [jnp.where(half == a, 1.0, 0.0).astype(BF) for a in range(2)]

    def lanes(p, base=0):
        return pl.ds(pl.multiple_of(base + p * 128, 128), 128)

    def near_forward(lo, hi):
        @pl.loop(lo, hi)
        def _(p):
            q2 = pk[:, lanes(p)]
            k2 = pk[:, lanes(p, D)]
            v2 = pk[:, lanes(p, 2 * D)]
            bias = jnp.where(me * N + iota((1, N), 1) < limit, 0.0, NEG)
            es, ms = [], []
            for a in range(2):
                s = nt(q2 * hm[a], k2) + bias
                m = jnp.max(s, axis=1, keepdims=True)
                e = jnp.exp(s - m).astype(BF)
                emat[2 * p + a] = e
                es.append(e)
                ms.append(m)
            rhs = jnp.concatenate(
                [
                    jnp.concatenate([v2 * hm[a], jnp.broadcast_to(hm[a], (N, 128))], axis=1)
                    for a in range(2)
                ],
                axis=0,
            )
            nd = nn(jnp.concatenate(es, axis=1), rhs)
            num[:, lanes(p)] = nd[:, :128]
            den[:, lanes(p)] = nd[:, 128:]
            mx[:, lanes(p)] = jnp.where(iota((N, 128), 1) < E, ms[0], ms[1])

    near_forward(0, 2)
    f1_wait(0)
    f2_start(0)
    near_forward(2, 4)
    m1_forward(0)
    f1_wait(1)
    f2_start(1)
    near_forward(4, 6)
    tilest[c] = tiles[...].T
    to_mate(1, tilest.at[c], tilest.at[c]).start()

    m2_wait(0)
    kg = gkv[:, :, :, :D].reshape(N, D)
    vg = gkv[:, :, :, D:].reshape(N, D)
    gdev = g * 8 + iota((32, N), 1) // 32 % 4 * 2 + iota((32, N), 1) // 128
    gpos = gdev * N + iota((32, N), 1) % 32 * 8
    gbias = jnp.concatenate(
        [jnp.where(gpos + offs[0, h] < limit, 0.0, NEG) for h in range(H)], axis=0
    )
    s = nt(block_diag(gqd[c, z, :, :D]), kg) + gbias
    m = jnp.max(s, axis=1, keepdims=True)
    e = jnp.exp(s - m)
    total = jnp.sum(e, axis=1, keepdims=True)
    e = e.astype(BF)
    emid[...] = e
    mnum[...] = diag_sum(nn(e, vg), 32)
    mden[...] = per_head(total, 32)
    mmax[...] = per_head(m, 32)

    f2_wait(0)
    f3_copy(0).start()
    m1_forward(1)
    f3_wait(0)

    col = iota((16, 512), 1)
    fdev = col // 16 % 16 * 8 + col // 2 % 4 * 2 + col // 256
    fpos = (fdev * 2 + col % 2) * 128
    lead = col // 8 % 2 == 0
    fbias = jnp.concatenate(
        [
            jnp.where(jnp.logical_and(lead, fpos + offs[1, h] < limit), 0.0, NEG)
            for h in range(H)
        ],
        axis=0,
    )
    kvf = far2kv[...].reshape(512, D)
    s = nt(block_diag(floc[2]), kvf) + fbias
    m = jnp.max(s, axis=1, keepdims=True)
    e = jnp.exp(s - m)
    efar[...] = e
    fnum[...] = diag_sum(nn(pltpu.roll(e, 8, 1).astype(BF), kvf), 16)
    fden[...] = per_head(jnp.sum(e, axis=1, keepdims=True), 16)
    fmax[...] = per_head(m, 16)

    def spread_mid(x):
        return jnp.broadcast_to(x[:, None, :], (32, 8, 128)).reshape(N, 128)

    def spread_far(x):
        return jnp.concatenate(
            [jnp.broadcast_to(x[0:1], (128, 128)), jnp.broadcast_to(x[1:2], (128, 128))], axis=0
        )

    def pick_mid(x):
        return jnp.sum(x.reshape(32, 8, 128), axis=1)

    def pick_far(x):
        return jnp.concatenate(
            [
                jnp.sum(x[:128], axis=0, keepdims=True),
                jnp.sum(x[128:], axis=0, keepdims=True),
                jnp.zeros((14, 128), F32),
            ],
            axis=0,
        )

    @pl.loop(0, 6)
    def _(p):
        ls = lanes(p)
        mm = midm[:, ls].astype(F32)
        fm = farm[:, ls].astype(F32)
        m0 = mx[:, ls]
        m1 = jnp.where(mm > 0.5, spread_mid(mmax[:, ls]), NEG)
        m2 = jnp.where(fm > 0.5, spread_far(fmax[0:2, ls]), NEG)
        top = jnp.maximum(jnp.maximum(m0, m1), m2)
        w0 = jnp.exp(m0 - top)
        w1 = jnp.exp(m1 - top)
        w2 = jnp.exp(m2 - top)
        total = w0 * den[:, ls] + w1 * spread_mid(mden[:, ls]) + w2 * spread_far(fden[0:2, ls])
        inv = 1.0 / total
        mixed = w0 * num[:, ls] + w1 * spread_mid(mnum[:, ls]) + w2 * spread_far(fnum[0:2, ls])
        at = (mixed * inv).astype(BF)
        attn[:, ls] = at
        do = pk[:, lanes(p, 3 * D)].astype(F32)
        prod = do * at.astype(F32)
        scale = w0 * inv
        sdo[:, ls] = (scale * do).astype(BF)
        npr[:, ls] = (-scale * prod).astype(BF)
        lse = top + jnp.log(total)
        mlse[:, ls] = pick_mid(lse * mm)
        mprod[:, ls] = pick_mid(prod * mm)
        flse[:, ls] = pick_far(lse * fm)
        fprod[:, ls] = pick_far(prod * fm)

    hi = lax.Precision.HIGHEST
    r0 = iota((D, 128), 0)
    l0 = iota((D, 128), 1)
    sel1 = jnp.where(jnp.logical_and(r0 == l0 * E, l0 < H), 1.0, 0.0)
    sel2 = jnp.where(r0 // E == l0 - H, 1.0, 0.0)
    gst[c, z] = dot(mlse[...], sel1, 1, 0, hi) + dot(mprod[...], sel2, 1, 0, hi)
    fs = dot(flse[...], sel1, 1, 0, hi) + dot(fprod[...], sel2, 1, 0, hi)
    r16 = iota((16, 128), 0)
    far1st[z] = jnp.where(r16 == 2 * z, fs[0:1], jnp.where(r16 == 2 * z + 1, fs[1:2], 0.0))
    f1_start(2)
    m1_start(2)

    attnt[c] = attn[...].T
    to_mate(2, attnt.at[c], attnt.at[c]).start()

    @pl.loop(0, 3)
    def _(i):
        ls = pl.ds(pl.multiple_of(i * N, N), N)
        out_rows[:, ls] = (tiles[:, ls].astype(F32) + nn(attn[...], wout[:, ls])).astype(BF)

    def near_backward(lo, hi_):
        @pl.loop(lo, hi_)
        def _(p):
            ls = lanes(p)
            q2 = pk[:, ls]
            k2 = pk[:, lanes(p, D)]
            v2 = pk[:, lanes(p, 2 * D)]
            so = sdo[:, ls]
            sp = npr[:, ls]
            rhs = jnp.concatenate([v2, jnp.ones((N, 128), BF)], axis=1)
            es, ds = [], []
            for a in range(2):
                lhs = jnp.concatenate([so * hm[a], sp * hm[a]], axis=1)
                t = nt(lhs, rhs)
                e = emat[2 * p + a]
                es.append(e)
                ds.append((e.astype(F32) * t).astype(BF))
            dq[:, ls] = 0.125 * nn(
                jnp.concatenate(ds, axis=1), jnp.concatenate([k2 * hm[0], k2 * hm[1]], axis=0)
            )
            dk[:, ls] = tn(
                jnp.concatenate(ds, axis=0), jnp.concatenate([q2 * hm[0], q2 * hm[1]], axis=0)
            )
            dv[:, ls] = tn(
                jnp.concatenate(es, axis=0), jnp.concatenate([so * hm[0], so * hm[1]], axis=0)
            )

    near_backward(0, 2)
    f1_wait(2)
    f2_start(2)
    m1_forward(2)
    near_backward(2, 6)

    kg = gkv[:, :, :, :D].reshape(N, D)
    vg = gkv[:, :, :, D:].reshape(N, D)
    scale = jnp.exp(mmax[...] - mlse[...])
    so = (scale * gqd[c, z, :, D:].astype(F32)).astype(BF)
    sp = scale * mprod[...]
    dl = jnp.concatenate(
        [jnp.sum(sp * head_mask(h, F32), axis=1, keepdims=True) for h in range(H)], axis=0
    )
    ds = (emid[...].astype(F32) * (nt(block_diag(so), vg) - dl)).astype(BF)
    dmid[0] = 0.125 * diag_sum(nn(ds, kg), 32)

    scale = jnp.exp(fmax[...] - flse[...])
    so = (scale * floc[3].astype(F32)).astype(BF)
    sp = scale * fprod[...]
    dl = jnp.concatenate(
        [jnp.sum(sp * head_mask(h, F32), axis=1, keepdims=True) for h in range(H)], axis=0
    )
    kvf = far2kv[...].reshape(512, D)
    t = pltpu.roll(nt(block_diag(so), kvf), 504, 1)
    dfar[0] = 0.125 * diag_sum(nn((efar[...] * (t - dl)).astype(BF), kvf), 16)

    f2_wait(1)
    f3_copy(1).start()
    m2_wait(1)
    f2_wait(2)
    f3_copy(2).start()
    m2_wait(2)

    hs = iota((16, 128), 1)
    hr = iota((16, 128), 0)
    pick1 = jnp.where(hs == hr, 1.0, 0.0)
    pick2 = jnp.where(hs == hr + H, 1.0, 0.0)
    st = gst[...].reshape(N, 128)
    ls_rows = dot(pick1, st, 1, 1, hi)
    dl_rows = dot(pick2, st, 1, 1, hi)
    qg = gqd[:, :, :, :D].reshape(N, D)
    og = gqd[:, :, :, D:].reshape(N, D)
    s = nt(block_diag(gkv[c, z, :, :D]), qg)
    t = nt(block_diag(gkv[c, z, :, D:]), og)
    ps, dss = [], []
    for h in range(H):
        ok = me * N + iota((32, N), 0) * 8 + offs[0, h] < limit
        p = jnp.exp(jnp.where(ok, s[h * 32 : (h + 1) * 32] - ls_rows[h : h + 1], NEG))
        ps.append(p.astype(BF))
        dss.append((p * (t[h * 32 : (h + 1) * 32] - dl_rows[h : h + 1])).astype(BF))
    dmid[1] = diag_sum(nn(jnp.concatenate(dss, axis=0), qg), 32)
    dmid[2] = diag_sum(nn(jnp.concatenate(ps, axis=0), og), 32)

    f3_wait(1)
    f3_wait(2)
    st = far2st[...].reshape(512, 128)
    ls_rows = dot(pick1, st, 1, 1, hi)
    dl_rows = dot(pick2, st, 1, 1, hi)
    qdf = far2qd[...].reshape(512, D)
    s = nt(block_diag(floc[0]), qdf)
    t = pltpu.roll(nt(block_diag(floc[1]), qdf), 504, 1)
    ps, dss = [], []
    rr = iota((16, 512), 0)
    for h in range(H):
        ok = jnp.logical_and((me * 2 + rr) * 128 + offs[1, h] < limit, jnp.logical_and(lead, rr < 2))
        p = jnp.exp(jnp.where(ok, s[h * 16 : (h + 1) * 16] - ls_rows[h : h + 1], NEG))
        ps.append(p)
        dss.append((p * (t[h * 16 : (h + 1) * 16] - dl_rows[h : h + 1])).astype(BF))
    dfar[1] = diag_sum(nn(jnp.concatenate(dss, axis=0), qdf), 16)
    pall = pltpu.roll(jnp.concatenate(ps, axis=0), 8, 1).astype(BF)
    dfar[2] = diag_sum(nn(pall, qdf), 16)

    @pl.loop(0, 6)
    def _(p):
        ls = lanes(p)
        mm = midm[:, ls].astype(F32)
        fm = farm[:, ls].astype(F32)
        for a, near in enumerate((dq, dk, dv)):
            v = near[:, ls] + mm * spread_mid(dmid[a, :, ls]) + fm * spread_far(dfar[a, 0:2, ls])
            v = v.astype(BF)
            gp[:, lanes(p, a * D)] = v
            gph[p // 3, :, pl.ds(pl.multiple_of(a * 384 + p % 3 * 128, 128), 128)] = v

    to_mate(3, gph.at[1 - c], gpr).start()

    @pl.loop(0, 3)
    def _(i):
        ls = pl.ds(pl.multiple_of(i * N, N), N)
        grad_tiles[:, ls] = nt(gp[...], wqkv[ls, :]).astype(BF)

    def put_part(b, v):
        v = v.astype(BF).reshape(4, 4, 48, 384)
        for i in range(3):
            at = pl.ds(pl.multiple_of(512 * i + 128 * b, 128), 128)
            part[:, :, :, at] = v[:, :, :, 128 * i : 128 * i + 128]

    to_mate(0, cotr, cotr).wait_recv()
    to_mate(2, attnt.at[1 - c], attnt.at[1 - c]).wait_recv()
    put_part(3, nn(attnt[c], cot[:, own_cols]) + nn(attnt[1 - c], cotr[...]))
    to_mate(1, tilest.at[1 - c], tilest.at[1 - c]).wait_recv()
    to_mate(3, gpr, gpr).wait_recv()

    @pl.loop(0, 3)
    def _(b):
        ls = pl.ds(pl.multiple_of(b * 384, 128), 384)
        put_part(b, nn(tilest[c], gph[c, :, ls]) + nn(tilest[1 - c], gpr[:, ls]))

    def dev(x_, y_, z_):
        return ((x_ % 4 * 4 + y_ % 4) * 4 + z_ % 4) * 2 + c

    pos = (x, y, z)
    step = (
        lambda k: dev(x + k, y, z),
        lambda k: dev(x, y + k, z),
        lambda k: dev(x, y, z + k),
    )

    def where_in(i, q, h):
        first = slice(None) if h is None else pl.ds(2 * h, 2)
        if i == 0:
            return (q, first, slice(None), pl.ds(0, 512))
        if i == 1:
            return (first, q, slice(None), pl.ds(512, 512))
        return (first, slice(None), slice(None), pl.ds(pl.multiple_of(1024 + 128 * q, 128), 128))

    R1 = (ra1, rb1, rc1)
    TMP = (ta, tb, tc)
    R2 = (ra2, rb2, rc2)
    ACC = (acca, accb, accc)

    def ring_copy(i, n):
        p = pos[i]
        nxt, prv = step[i](1), step[i](3)
        up, down, far = (p + 1) % 4, (p + 3) % 4, (p + 2) % 4
        src, dst, to = (
            lambda: (part.at[where_in(i, far, 0)], R1[i].at[0], nxt),
            lambda: (part.at[where_in(i, far, 1)], R1[i].at[1], prv),
            lambda: (part.at[where_in(i, up, 1)], R2[i].at[0, pl.ds(2, 2)], nxt),
            lambda: (part.at[where_in(i, down, 0)], R2[i].at[1, pl.ds(0, 2)], prv),
            lambda: (TMP[i].at[0], R2[i].at[0, pl.ds(0, 2)], nxt),
            lambda: (TMP[i].at[1], R2[i].at[1, pl.ds(2, 2)], prv),
        )[n]()
        return rc(src, dst, rs.at[i, n], rr_.at[i, n], to)

    for i in range(3):
        for n in range(4):
            ring_copy(i, n).start()
    for i in range(3):
        p = pos[i]
        for h, q in ((0, (p + 1) % 4), (1, (p + 3) % 4)):
            ring_copy(i, h).wait_recv()
            TMP[i][h] = (part[where_in(i, q, h)].astype(F32) + R1[i][h].astype(F32)).astype(BF)
            ring_copy(i, 4 + h).start()

    S2 = (sa2, sb2, sc2)
    S3 = (sa3, sb3, sc3)
    ACC2 = (acca2, accb2, accc2)

    def col128(q):
        return pl.ds(pl.multiple_of(128 * q, 128), 128)

    def second(i, k):
        j = (i + 1) % 3
        q = (pos[j] + k) % 4
        view = (lambda: acca.at[q], lambda: accb.at[:, :, col128(q)], lambda: accc.at[q])[i]()
        return rc(view, S2[i].at[pos[j]], ss.at[0, i, k], sr.at[0, i, pos[j]], step[j](k))

    def third(i, k):
        j = (i + 2) % 3
        q = (pos[j] + k) % 4
        view = (lambda: acca2.at[:, col128(q)], lambda: accb2.at[q], lambda: accc2.at[q])[i]()
        return rc(view, S3[i].at[pos[j]], ss.at[1, i, k], sr.at[1, i, pos[j]], step[j](k))

    def arrived(stage, i, buf, j, k):
        q = (pos[j] + k) % 4
        rc(buf.at[q], buf.at[q], ss.at[stage, i, k], sr.at[stage, i, q], step[j](k)).wait_recv()

    for i in range(3):
        for n in range(2, 6):
            ring_copy(i, n).wait_recv()
        mine = part[where_in(i, pos[i], None)].astype(F32)
        ACC[i][...] = (mine + R2[i][0].astype(F32) + R2[i][1].astype(F32)).astype(BF)
        for k in (2, 1, 3):
            second(i, k).start()

    for i in range(3):
        j = (i + 1) % 3
        q = pos[j]
        if i == 0:
            mine = acca[q]
        elif i == 1:
            mine = accb[:, :, col128(q)]
        else:
            mine = accc[q]
        total = mine.astype(F32)
        for k in (1, 3, 2):
            arrived(0, i, S2[i], j, k)
            total = total + S2[i][(q + k) % 4].astype(F32)
        ACC2[i][...] = total.astype(BF)
        for k in (2, 1, 3):
            third(i, k).start()

    done = []
    for i in range(3):
        j = (i + 2) % 3
        q = pos[j]
        if i == 0:
            mine = acca2[:, col128(q)]
        elif i == 1:
            mine = accb2[q]
        else:
            mine = accc2[q]
        total = mine.astype(F32)
        for k in (1, 3, 2):
            arrived(1, i, S3[i], j, k)
            total = total + S3[i][(q + k) % 4].astype(F32)
        done.append(total)
    er = iota((64, 48), 0)
    sel = jnp.where(jnp.logical_and(iota((64, 48), 1) == er // 8 * 6 + er % 8, er % 8 < 6), 1.0, 0.0)
    fin[...] = dot(sel, jnp.concatenate(done, axis=1), 1, 0, hi).reshape(8, 8, 384)
    own = z * 2 + c
    for k in range(1, 8):
        o = (own + k) % 8
        rc(fin.at[o], finr.at[own], es_.at[k], er_.at[own], g * 8 + o).start()
    finr[own] = fin[own]
    for k in range(1, 8):
        o = (own + k) % 8
        rc(finr.at[o], finr.at[o], es_.at[k], er_.at[o], g * 8 + o).wait_recv()
    for o in range(8):
        v = finr[o][0:6]
        if o < 6:
            g_qkv[:, 384 * o : 384 * o + 384] = v
        else:
            g_out[:, 384 * (o - 6) : 384 * (o - 6) + 384] = v

    to_mate(0, cot.at[:, half_cols], cotr).wait_send()
    to_mate(1, tilest.at[c], tilest.at[c]).wait_send()
    to_mate(2, attnt.at[c], attnt.at[c]).wait_send()
    to_mate(3, gph.at[1 - c], gpr).wait_send()
    for i in range(3):
        for n in range(6):
            ring_copy(i, n).wait_send()
        for k in (1, 2, 3):
            second(i, k).wait_send()
            third(i, k).wait_send()
    for k in range(1, 8):
        o = (own + k) % 8
        rc(fin.at[o], finr.at[own], es_.at[k], er_.at[own], g * 8 + o).wait_send()
    for t in range(3):
        for k in (1, 2, 3):
            f1_copy(t, k).wait_send()
            m1_copy(t, k).wait_send()
        for k in range(1, 16):
            f2_copy(t, k).wait_send()
        f3_copy(t).wait_send()
        for k in range(4):
            m2_copy(t, k).wait_send()


def per_device(tiles, w_qkv, w_out, cotangent, offsets, pad_count):
    vm = pl.BlockSpec(memory_space=pltpu.VMEM)
    sm = pl.BlockSpec(memory_space=pltpu.SMEM)
    V = pltpu.VMEM
    dma = pltpu.SemaphoreType.DMA
    big = V((N, D), F32)
    bigb = V((N, D), BF)
    m32 = V((32, D), F32)
    f16 = V((16, D), F32)
    out_rows, grad_tiles, g_qkv, g_out = pl.pallas_call(
        kernel,
        out_shape=(
            jax.ShapeDtypeStruct((N, D), BF),
            jax.ShapeDtypeStruct((N, D), BF),
            jax.ShapeDtypeStruct((6, 3 * D), F32),
            jax.ShapeDtypeStruct((6, D), F32),
        ),
        in_specs=[sm, sm, vm, vm, vm, vm],
        out_specs=(vm, vm, vm, vm),
        scratch_shapes=[
            V((N, 4 * D), BF), bigb, bigb, V((H, N, N), BF), big, big, big,
            V((2, 4, 32, 2 * D), BF), V((2, 4, 32, 2 * D), BF), V((2, 4, 32, 128), F32),
            V((4, 16, D), BF), V((4, 16, D), BF), V((4, 16, 128), F32),
            V((2, 16, 16, D), BF), V((2, 16, 16, D), BF), V((2, 16, 16, 128), F32),
            V((4, 16, D), BF), m32, m32, m32, f16, f16, f16, V((H * 32, N), BF), V((H * 16, 512), F32),
            bigb, bigb, bigb, m32, m32, f16, f16,
            big, big, big, V((3, 32, D), F32), V((3, 16, D), F32), V((N, 3 * D), BF),
            V((2, D, N), BF), V((2, D, N), BF), V((N, 384), BF), V((2, N, 1152), BF), V((N, 1152), BF),
            V((4, 4, 48, 1536), BF),
            V((2, 2, 48, 512), BF), V((2, 2, 48, 512), BF), V((2, 2, 4, 48, 128), BF),
            V((2, 2, 48, 512), BF), V((2, 2, 48, 512), BF), V((2, 2, 4, 48, 128), BF),
            V((2, 4, 48, 512), BF), V((2, 4, 48, 512), BF), V((2, 4, 4, 48, 128), BF),
            V((4, 48, 512), BF), V((4, 48, 512), BF), V((4, 4, 48, 128), BF),
            V((4, 48, 512), BF), V((4, 4, 48, 128), BF), V((4, 4, 48, 128), BF),
            V((48, 512), BF), V((4, 48, 128), BF), V((4, 48, 128), BF),
            V((4, 48, 128), BF), V((4, 48, 128), BF), V((4, 48, 128), BF),
            V((8, 8, 384), F32), V((8, 8, 384), F32),
            dma((3, 4)), dma((3, 4)), dma((3, 16)), dma((3, 16)), dma((3,)), dma((3,)),
            dma((3, 4)), dma((3, 4)), dma((3, 4)), dma((3, 4)),
            dma((4,)), dma((4,)), dma((3, 6)), dma((3, 6)), dma((2, 3, 4)), dma((2, 3, 4)),
            dma((8,)), dma((8,)),
        ],
        compiler_params=pltpu.CompilerParams(
            collective_id=0, has_side_effects=True, vmem_limit_bytes=60 * 1024 * 1024
        ),
        name="layer",
    )(offsets, pad_count, tiles, w_qkv, w_out, cotangent)
    return out_rows, grad_tiles, g_qkv, g_out


def solution(mesh):
    row = P("ctx", None)
    return jax.shard_map(
        per_device,
        mesh=mesh,
        in_specs=(row, P(), P(), row, P(), P()),
        out_specs=(row, row, row, row),
        check_vma=False,
    )
```

```python
import jax
import jax.numpy as jnp
from jax import lax
from jax.experimental import pallas as pl
from jax.experimental.pallas import tpu as pltpu
from jax.sharding import PartitionSpec as P

MESH = pl.DeviceIdType.MESH
N = 256
D = 768
H = 12
E = 64
NEG = -1e30
F32 = jnp.float32
BF = jnp.bfloat16
I32 = jnp.int32


def dot(a, b, ca, cb, precision=None):
    dims = (((ca,), (cb,)), ((), ()))
    return lax.dot_general(a, b, dims, precision=precision, preferred_element_type=F32)


def nn(a, b):
    return dot(a, b, 1, 0)


def nt(a, b):
    return dot(a, b, 1, 1)


def tn(a, b):
    return dot(a, b, 0, 0)


def iota(shape, dim):
    return lax.broadcasted_iota(I32, shape, dim)


def head_mask(h, dtype):
    return jnp.where(iota((1, D), 1) // E == h, 1.0, 0.0).astype(dtype)


def block_diag(x):
    return jnp.concatenate([x * head_mask(h, x.dtype) for h in range(H)], axis=0)


def diag_sum(x, rows):
    head = iota((rows, D), 1) // E
    out = jnp.zeros((rows, D), F32)
    for h in range(H):
        out = jnp.where(head == h, x[h * rows : (h + 1) * rows], out)
    return out


def per_head(cols, rows):
    head = iota((rows, D), 1) // E
    out = jnp.zeros((rows, D), F32)
    for h in range(H):
        out = jnp.where(head == h, cols[h * rows : (h + 1) * rows], out)
    return out


def kernel(
    offs, pad, tiles_h, wqkv_h, wout_h, cot_h,
    rows_h, gtil_h, g_qkv, g_out,
    tiles, wqkv, wout, cot, out_rows, grad_tiles,
    pk, midm, farm, sel1, sel2, hsel, emat, num, den, mx,
    gkv, gqd, gst, far1kv, far1qd, far1st, far2kv, far2qd, far2st,
    floc, mnum, mden, mmax, fnum, fden, fmax, emid, efar,
    attn, sdo, npr, mlse, mprod, flse, fprod,
    dq, dk, dv, dmid, dfar, gp, tilest, attnt, cotr, gph, gpr,
    part, r1, tmp, r2, acc, s2, tot, fin, finr,
    ls_, os_, f1s, f1r, f2s, f2r, f3s, f3r, m1s, m1r, m2s, m2r,
    xs, xr, rs, rr_, ss, sr, es_, er_,
):
    me = lax.axis_index("ctx")
    c = me % 2
    z = me // 2 % 4
    g = me // 8
    x = g // 4
    y = g % 4
    mate = g * 8 + z * 2 + (1 - c)

    def zpeer(k):
        return g * 8 + (z + k) % 4 * 2 + c

    def gpeer(k):
        return (g + k) % 16 * 8 + z * 2 + c

    def rc(src, dst, ss, rs, dev):
        return pltpu.make_async_remote_copy(
            src_ref=src, dst_ref=dst, send_sem=ss, recv_sem=rs, device_id=(dev,), device_id_type=MESH
        )

    kv_cols = pl.ds(D, 2 * D)
    q_cols = pl.ds(0, D)
    loads = (
        pltpu.make_async_copy(tiles_h, tiles, ls_.at[0]),
        pltpu.make_async_copy(wqkv_h.at[:, kv_cols], wqkv.at[:, kv_cols], ls_.at[1]),
        pltpu.make_async_copy(wqkv_h.at[:, q_cols], wqkv.at[:, q_cols], ls_.at[2]),
        pltpu.make_async_copy(cot_h, cot, ls_.at[3]),
        pltpu.make_async_copy(wout_h, wout, ls_.at[4]),
    )
    for item in loads:
        item.start()
    barrier = pltpu.get_barrier_semaphore()
    peers = [mate] + [zpeer(k) for k in (1, 2, 3)] + [gpeer(k) for k in range(1, 16)]
    peers += [g * 8 + (z + k) % 4 * 2 + (1 - c) for k in (1, 2, 3)]
    for p in peers:
        pl.semaphore_signal(barrier, inc=1, device_id=(p,), device_id_type=MESH)

    FAR1 = (far1kv, far1qd, far1st)
    FAR2 = (far2kv, far2qd, far2st)
    MID = (gkv, gqd, gst)

    def f1_copy(t, k):
        return rc(FAR1[t].at[z], FAR1[t].at[z], f1s.at[t, k], f1r.at[t, z], zpeer(k))

    def f1_start(t):
        for k in (1, 3, 2):
            f1_copy(t, k).start()

    def f1_wait(t):
        for k in (1, 3, 2):
            o = (z + k) % 4
            rc(FAR1[t].at[o], FAR1[t].at[o], f1s.at[t, k], f1r.at[t, o], zpeer(k)).wait_recv()

    def f2_copy(t, k):
        return rc(FAR2[t].at[c, g], FAR2[t].at[c, g], f2s.at[t, k], f2r.at[t, g], gpeer(k))

    def f2_start(t):
        a = FAR1[t]
        FAR2[t][c, g] = (
            a[0].astype(F32) + a[1].astype(F32) + a[2].astype(F32) + a[3].astype(F32)
        ).astype(a.dtype)
        for k in range(1, 16):
            f2_copy(t, k).start()

    def f2_wait(t):
        for k in range(1, 16):
            o = (g + k) % 16
            rc(FAR2[t].at[c, o], FAR2[t].at[c, o], f2s.at[t, k], f2r.at[t, o], gpeer(k)).wait_recv()

    def f3_copy(t):
        return rc(FAR2[t].at[c], FAR2[t].at[c], f3s.at[t], f3r.at[t], mate)

    def f3_wait(t):
        rc(FAR2[t].at[1 - c], FAR2[t].at[1 - c], f3s.at[t], f3r.at[t], mate).wait_recv()

    def m1_copy(t, k):
        return rc(MID[t].at[c, z], MID[t].at[c, z], m1s.at[t, k], m1r.at[t, z], zpeer(k))

    def m2_copy(t, k):
        o = (z + k) % 4
        return rc(MID[t].at[c, o], MID[t].at[c, o], m2s.at[t, k], m2r.at[t, o], mate)

    def m1_start(t):
        for k in (1, 3, 2):
            m1_copy(t, k).start()
        m2_copy(t, 0).start()

    def m1_forward(t):
        for k in (1, 3, 2):
            o = (z + k) % 4
            rc(MID[t].at[c, o], MID[t].at[c, o], m1s.at[t, k], m1r.at[t, o], zpeer(k)).wait_recv()
            m2_copy(t, k).start()

    def m2_wait(t):
        for k in range(4):
            o = (z + k) % 4
            rc(MID[t].at[1 - c, o], MID[t].at[1 - c, o], m2s.at[t, k], m2r.at[t, o], mate).wait_recv()

    def to_mate(t, src, dst):
        return rc(src, dst, xs.at[t], xr.at[t], mate)

    half_cols = pl.ds(pl.multiple_of(384 * (1 - c), 128), 384)
    own_cols = pl.ds(pl.multiple_of(384 * c, 128), 384)

    limit = N * 128 - pad[0]
    lane_head = iota((1, D), 1) // E
    o0 = jnp.zeros((1, D), I32)
    o1 = jnp.zeros((1, D), I32)
    for h in range(H):
        o0 = jnp.where(lane_head == h, offs[0, h], o0)
        o1 = jnp.where(lane_head == h, offs[1, h], o1)
    midm[...] = jnp.where(iota((N, D), 0) % 8 == o0, 1.0, 0.0).astype(BF)
    farm[...] = jnp.where(iota((N, D), 0) % 128 == o1, 1.0, 0.0).astype(BF)

    r0 = iota((D, 128), 0)
    l0 = iota((D, 128), 1)
    sel1[...] = jnp.where(jnp.logical_and(r0 == l0 * E, l0 < H), 1.0, 0.0).astype(BF)
    sel2[...] = jnp.where(r0 // E == l0 - H, 1.0, 0.0).astype(BF)
    hsel[...] = jnp.where(iota((16, D), 1) // E == iota((16, D), 0), 1.0, 0.0)
    pool_mid = jnp.where(iota((32, N), 1) // 8 == iota((32, N), 0), 1.0, 0.0).astype(BF)
    two = iota((16, N), 1) // 128
    row = iota((16, N), 0)
    pool_far = jnp.where(row == two, 1.0, 0.0).astype(BF)
    place = jnp.concatenate(
        [
            jnp.where(row == 2 * z + two, 1.0, 0.0),
            jnp.where(row == 8 + 2 * z + two, 1.0, 0.0),
        ],
        axis=1,
    ).astype(BF)

    def picks(t, i, a, b):
        ls = pl.ds(pl.multiple_of(i * N, N), N)
        hi = pl.ds(pl.multiple_of(D + i * N, N), N)
        mk = midm[:, ls]
        fk = farm[:, ls]
        fa = a * fk
        fb = b * fk
        FAR1[t][z, :, ls] = nn(place, jnp.concatenate([fa, fb], axis=0)).astype(BF)
        MID[t][c, z, :, ls] = nn(pool_mid, a * mk).astype(BF)
        MID[t][c, z, :, hi] = nn(pool_mid, b * mk).astype(BF)
        floc[2 * t, :, ls] = nn(pool_far, fa).astype(BF)
        floc[2 * t + 1, :, ls] = nn(pool_far, fb).astype(BF)

    loads[0].wait()
    loads[1].wait()

    @pl.loop(0, 3)
    def _(i):
        kc = pl.ds(pl.multiple_of(D + i * N, N), N)
        vc = pl.ds(pl.multiple_of(2 * D + i * N, N), N)
        x = tiles[...]
        kk = nn(x, wqkv[:, kc]).astype(BF)
        vv = nn(x, wqkv[:, vc]).astype(BF)
        pk[:, kc] = kk
        pk[:, vc] = vv
        picks(0, i, kk, vv)

    pl.semaphore_wait(barrier, len(peers))
    f1_start(0)
    m1_start(0)
    for item in loads[2:]:
        item.wait()
    to_mate(0, cot.at[:, half_cols], cotr).start()

    @pl.loop(0, 3)
    def _(i):
        qc = pl.ds(pl.multiple_of(i * N, N), N)
        dc = pl.ds(pl.multiple_of(3 * D + i * N, N), N)
        qq = nn(tiles[...], wqkv[:, qc]).astype(BF) * jnp.asarray(0.125, BF)
        dd = nt(cot[...], wout[qc, :]).astype(BF)
        pk[:, qc] = qq
        pk[:, dc] = dd
        picks(1, i, qq, dd)


    half = iota((1, 128), 1) // E
    hm = [jnp.where(half == a, 1.0, 0.0).astype(BF) for a in range(2)]

    def lanes(p, base=0):
        return pl.ds(pl.multiple_of(base + p * 128, 128), 128)

    def near_forward(lo, hi):
        @pl.loop(lo, hi)
        def _(p):
            q2 = pk[:, lanes(p)]
            k2 = pk[:, lanes(p, D)]
            v2 = pk[:, lanes(p, 2 * D)]
            bias = jnp.where(me * N + iota((1, N), 1) < limit, 0.0, NEG)
            es, ms = [], []
            for a in range(2):
                s = nt(q2 * hm[a], k2) + bias
                m = jnp.max(s, axis=1, keepdims=True)
                e = jnp.exp(s - m).astype(BF)
                emat[2 * p + a] = e
                es.append(e)
                ms.append(m)
            rhs = jnp.concatenate(
                [
                    jnp.concatenate([v2 * hm[a], jnp.broadcast_to(hm[a], (N, 128))], axis=1)
                    for a in range(2)
                ],
                axis=0,
            )
            nd = nn(jnp.concatenate(es, axis=1), rhs)
            num[:, lanes(p)] = nd[:, :128]
            den[:, lanes(p)] = nd[:, 128:]
            mx[:, lanes(p)] = jnp.where(iota((N, 128), 1) < E, ms[0], ms[1])

    near_forward(0, 2)
    f1_wait(0)
    f2_start(0)
    near_forward(2, 6)
    tilest[c] = tiles[...].T
    m1_forward(0)
    f1_start(1)
    m1_start(1)
    to_mate(1, tilest.at[c], tilest.at[c]).start()

    m2_wait(0)
    kg = gkv[:, :, :, :D].reshape(N, D)
    vg = gkv[:, :, :, D:].reshape(N, D)
    gdev = g * 8 + iota((32, N), 1) // 32 % 4 * 2 + iota((32, N), 1) // 128
    gpos = gdev * N + iota((32, N), 1) % 32 * 8
    gbias = jnp.concatenate(
        [jnp.where(gpos + offs[0, h] < limit, 0.0, NEG) for h in range(H)], axis=0
    )
    s = nt(block_diag(gqd[c, z, :, :D]), kg) + gbias
    m = jnp.max(s, axis=1, keepdims=True)
    e = jnp.exp(s - m)
    total = jnp.sum(e, axis=1, keepdims=True)
    e = e.astype(BF)
    emid[...] = e
    mnum[...] = diag_sum(nn(e, vg), 32)
    mden[...] = per_head(total, 32)
    mmax[...] = per_head(m, 32)

    f2_wait(0)
    f3_copy(0).start()
    f3_wait(0)

    heads = hsel[...]
    headb = heads.astype(BF)

    def far_diag(v):
        return jnp.concatenate([v[0:1] * headb, v[1:2] * headb], axis=0)

    def far_fold(v):
        return jnp.concatenate(
            [jnp.sum(v[16 * r : 16 * r + 16] * heads, axis=0, keepdims=True) for r in range(2)],
            axis=0,
        )

    col = iota((16, 512), 1)
    fdev = col // 16 % 16 * 8 + col // 2 % 4 * 2 + col // 256
    fpos = (fdev * 2 + col % 2) * 128
    lead = col // 8 % 2 == 0
    off_col = jnp.zeros((16, 512), I32)
    for h in range(H):
        off_col = jnp.where(iota((16, 512), 0) == h, offs[1, h], off_col)
    fbias = jnp.where(jnp.logical_and(lead, fpos + off_col < limit), 0.0, NEG)
    fbias = jnp.concatenate([fbias, fbias], axis=0)
    kvf = far2kv[...].reshape(512, D)
    s = nt(far_diag(floc[2]), kvf) + fbias
    m = jnp.max(s, axis=1, keepdims=True)
    e = jnp.exp(s - m)
    efar[...] = e
    fnum[0:2] = far_fold(nn(pltpu.roll(e, 8, 1).astype(BF), kvf))
    fden[0:2] = far_fold(jnp.broadcast_to(jnp.sum(e, axis=1, keepdims=True), (32, D)))
    fmax[0:2] = far_fold(jnp.broadcast_to(m, (32, D)))

    def spread_mid(x):
        return jnp.broadcast_to(x[:, None, :], (32, 8, 128)).reshape(N, 128)

    def spread_far(x):
        return jnp.concatenate(
            [jnp.broadcast_to(x[0:1], (128, 128)), jnp.broadcast_to(x[1:2], (128, 128))], axis=0
        )

    def pick_mid(x):
        return jnp.sum(x.reshape(32, 8, 128), axis=1)

    def pick_far(x):
        return jnp.concatenate(
            [
                jnp.sum(x[:128], axis=0, keepdims=True),
                jnp.sum(x[128:], axis=0, keepdims=True),
                jnp.zeros((14, 128), F32),
            ],
            axis=0,
        )

    @pl.loop(0, 6)
    def _(p):
        ls = lanes(p)
        mm = midm[:, ls].astype(F32)
        fm = farm[:, ls].astype(F32)
        m0 = mx[:, ls]
        m1 = jnp.where(mm > 0.5, spread_mid(mmax[:, ls]), NEG)
        m2 = jnp.where(fm > 0.5, spread_far(fmax[0:2, ls]), NEG)
        top = jnp.maximum(jnp.maximum(m0, m1), m2)
        w0 = jnp.exp(m0 - top)
        w1 = jnp.exp(m1 - top)
        w2 = jnp.exp(m2 - top)
        total = w0 * den[:, ls] + w1 * spread_mid(mden[:, ls]) + w2 * spread_far(fden[0:2, ls])
        inv = 1.0 / total
        mixed = w0 * num[:, ls] + w1 * spread_mid(mnum[:, ls]) + w2 * spread_far(fnum[0:2, ls])
        at = (mixed * inv).astype(BF)
        attn[:, ls] = at
        do = pk[:, lanes(p, 3 * D)].astype(F32)
        prod = do * at.astype(F32)
        scale = w0 * inv
        sdo[:, ls] = (scale * do).astype(BF)
        npr[:, ls] = (-scale * prod).astype(BF)
        lse = top + jnp.log(total)
        mlse[:, ls] = pick_mid(lse * mm)
        mprod[:, ls] = pick_mid(prod * mm)
        flse[:, ls] = pick_far(lse * fm)
        fprod[:, ls] = pick_far(prod * fm)

    lse_rows = jnp.concatenate([mlse[...], flse[...]], axis=0)
    prod_rows = jnp.concatenate([mprod[...], fprod[...]], axis=0)
    l_hi = lse_rows.astype(BF)
    left = lse_rows - l_hi.astype(F32)
    l_mid = left.astype(BF)
    l_lo = (left - l_mid.astype(F32)).astype(BF)
    p_hi = prod_rows.astype(BF)
    p_lo = (prod_rows - p_hi.astype(F32)).astype(BF)
    lt = nn(jnp.concatenate([l_hi, l_mid, l_lo], axis=0), sel1[...])
    pt = nn(jnp.concatenate([p_hi, p_lo], axis=0), sel2[...])
    st = lt[0:48] + lt[48:96] + lt[96:144] + pt[0:48] + pt[48:96]
    gst[c, z] = st[0:32]
    fs = st[32:48]
    r16 = iota((16, 128), 0)
    far1st[z] = jnp.where(r16 == 2 * z, fs[0:1], jnp.where(r16 == 2 * z + 1, fs[1:2], 0.0))
    f1_start(2)
    m1_start(2)

    attnt[c] = attn[...].T
    to_mate(2, attnt.at[c], attnt.at[c]).start()
    out_copy = pltpu.make_async_copy(out_rows, rows_h, os_.at[0])
    til_copy = pltpu.make_async_copy(grad_tiles, gtil_h, os_.at[1])

    @pl.loop(0, 3)
    def _(i):
        ls = pl.ds(pl.multiple_of(i * N, N), N)
        out_rows[:, ls] = (tiles[:, ls].astype(F32) + nn(attn[...], wout[:, ls])).astype(BF)

    def put_part(b, v):
        part[b] = v.astype(BF).reshape(4, 4, 48, 384)

    def dev(x_, y_):
        return ((x_ % 4 * 4 + y_ % 4) * 4 + z) * 2 + c

    pos = (x, y)
    step = (lambda k: dev(x + k, y), lambda k: dev(x, y + k))

    def where_in(b, q, h):
        some = slice(None) if h is None else pl.ds(2 * h, 2)
        return (b, q, some) if b % 2 == 0 else (b, some, q)

    def ring_copy(b, n):
        p = pos[b % 2]
        nxt, prv = step[b % 2](1), step[b % 2](3)
        up, down, far = (p + 1) % 4, (p + 3) % 4, (p + 2) % 4
        src, dst, to = (
            lambda: (part.at[where_in(b, far, 0)], r1.at[b, 0], nxt),
            lambda: (part.at[where_in(b, far, 1)], r1.at[b, 1], prv),
            lambda: (part.at[where_in(b, up, 1)], r2.at[b, 0, pl.ds(2, 2)], nxt),
            lambda: (part.at[where_in(b, down, 0)], r2.at[b, 1, pl.ds(0, 2)], prv),
            lambda: (tmp.at[b, 0], r2.at[b, 0, pl.ds(0, 2)], nxt),
            lambda: (tmp.at[b, 1], r2.at[b, 1, pl.ds(2, 2)], prv),
        )[n]()
        return rc(src, dst, rs.at[b, n], rr_.at[b, n], to)

    def ring_a(b):
        for n in range(4):
            ring_copy(b, n).start()

    def ring_b(b):
        p = pos[b % 2]
        for h, q in ((0, (p + 1) % 4), (1, (p + 3) % 4)):
            ring_copy(b, h).wait_recv()
            tmp[b, h] = (part[where_in(b, q, h)].astype(F32) + r1[b, h].astype(F32)).astype(BF)
            ring_copy(b, 4 + h).start()

    def second(b, k):
        j = (b + 1) % 2
        q = (pos[j] + k) % 4
        return rc(acc.at[b, q], s2.at[b, pos[j]], ss.at[b, k], sr.at[b, pos[j]], step[j](k))

    def ring_c(b):
        for n in range(2, 6):
            ring_copy(b, n).wait_recv()
        mine = part[where_in(b, pos[b % 2], None)].astype(F32)
        acc[b] = (mine + r2[b, 0].astype(F32) + r2[b, 1].astype(F32)).astype(BF)
        for k in (2, 1, 3):
            second(b, k).start()

    def ring_d(b):
        j = (b + 1) % 2
        total = acc[b, pos[j]].astype(F32)
        for k in (1, 3, 2):
            q = (pos[j] + k) % 4
            rc(s2.at[b, q], s2.at[b, q], ss.at[b, k], sr.at[b, q], step[j](k)).wait_recv()
            total = total + s2[b, q].astype(F32)
        tot[b // 2, b % 2] = total.astype(BF)

    own = z * 2 + c
    er = iota((128, 96), 0)
    ek = er % 8
    spread = jnp.where(
        jnp.logical_and(iota((128, 96), 1) == er // 8 % 2 * 48 + er // 16 * 6 + ek, ek < 6), 1.0, 0.0
    ).astype(BF)

    def fin_copy(r, k):
        o = (own + k) % 8
        return rc(fin.at[r, o], finr.at[r, own], es_.at[r, k], er_.at[r, own], g * 8 + o)

    def fin_start(r):
        fin[r] = nn(spread, tot[r].reshape(96, 384)).astype(BF).reshape(8, 16, 384)
        for k in range(1, 8):
            fin_copy(r, k).start()
        finr[r, own] = fin[r, own]

    def fin_end(r):
        for k in range(1, 8):
            o = (own + k) % 8
            rc(finr.at[r, o], finr.at[r, o], es_.at[r, k], er_.at[r, o], g * 8 + o).wait_recv()
        for a in range(2):
            v = finr[r, a].astype(F32)
            for o in (2, 4, 6):
                v = v + finr[r, o + a].astype(F32)
            for i in range(2):
                w = v[8 * i : 8 * i + 6]
                at = (2 * r - 1 + i) * D + 384 * a
                if r == 0 and i == 0:
                    g_out[:, 384 * a : 384 * a + 384] = w
                else:
                    g_qkv[:, at : at + 384] = w

    to_mate(0, cotr, cotr).wait_recv()
    to_mate(2, attnt.at[1 - c], attnt.at[1 - c]).wait_recv()
    put_part(0, nn(attnt[c], cot[:, own_cols]) + nn(attnt[1 - c], cotr[...]))
    ring_a(0)
    out_copy.start()
    f1_wait(1)
    f2_start(1)

    def near_backward(lo, hi_):
        @pl.loop(lo, hi_)
        def _(p):
            ls = lanes(p)
            q2 = pk[:, ls]
            k2 = pk[:, lanes(p, D)]
            v2 = pk[:, lanes(p, 2 * D)]
            so = sdo[:, ls]
            sp = npr[:, ls]
            rhs = jnp.concatenate([v2, jnp.ones((N, 128), BF)], axis=1)
            es, ds = [], []
            for a in range(2):
                lhs = jnp.concatenate([so * hm[a], sp * hm[a]], axis=1)
                t = nt(lhs, rhs)
                e = emat[2 * p + a]
                es.append(e)
                ds.append((e.astype(F32) * t).astype(BF))
            dq[:, ls] = 0.125 * nn(
                jnp.concatenate(ds, axis=1), jnp.concatenate([k2 * hm[0], k2 * hm[1]], axis=0)
            )
            dk[:, ls] = tn(
                jnp.concatenate(ds, axis=0), jnp.concatenate([q2 * hm[0], q2 * hm[1]], axis=0)
            )
            dv[:, ls] = tn(
                jnp.concatenate(es, axis=0), jnp.concatenate([so * hm[0], so * hm[1]], axis=0)
            )

    near_backward(0, 2)
    f1_wait(2)
    f2_start(2)
    m1_forward(1)
    m1_forward(2)
    near_backward(2, 4)
    ring_b(0)
    near_backward(4, 6)

    kg = gkv[:, :, :, :D].reshape(N, D)
    vg = gkv[:, :, :, D:].reshape(N, D)
    scale = jnp.exp(mmax[...] - mlse[...])
    so = (scale * gqd[c, z, :, D:].astype(F32)).astype(BF)
    sp = scale * mprod[...]
    dl = jnp.concatenate(
        [jnp.sum(sp * head_mask(h, F32), axis=1, keepdims=True) for h in range(H)], axis=0
    )
    ds = (emid[...].astype(F32) * (nt(block_diag(so), vg) - dl)).astype(BF)
    dmid[0] = 0.125 * diag_sum(nn(ds, kg), 32)

    scale = jnp.exp(fmax[0:2] - flse[0:2])
    so = (scale * floc[3, 0:2].astype(F32)).astype(BF)
    sp = scale * fprod[0:2]
    dl = jnp.concatenate(
        [jnp.sum(sp[r : r + 1] * heads, axis=1, keepdims=True) for r in range(2)], axis=0
    )
    kvf = far2kv[...].reshape(512, D)
    t = pltpu.roll(nt(far_diag(so), kvf), 504, 1)
    dfar[0, 0:2] = 0.125 * far_fold(nn((efar[...] * (t - dl)).astype(BF), kvf))

    def grad_part(a, near):
        @pl.loop(0, 6)
        def _(p):
            ls = lanes(p)
            mm = midm[:, ls].astype(F32)
            fm = farm[:, ls].astype(F32)
            v = near[:, ls] + mm * spread_mid(dmid[a, :, ls]) + fm * spread_far(dfar[a, 0:2, ls])
            v = v.astype(BF)
            gp[:, lanes(p, a * D)] = v
            gph[a, p // 3, :, lanes(p % 3)] = v

        to_mate(3 + a, gph.at[a, 1 - c], gpr.at[a]).start()

    def weight_part(a):
        to_mate(3 + a, gpr.at[a], gpr.at[a]).wait_recv()
        put_part(1 + a, nn(tilest[c], gph[a, c]) + nn(tilest[1 - c], gpr[a]))
        ring_a(1 + a)

    grad_part(0, dq)
    ring_c(0)
    f2_wait(1)
    f3_copy(1).start()
    m2_wait(1)
    f2_wait(2)
    f3_copy(2).start()
    m2_wait(2)

    st = gst[...].reshape(N, 128).T
    ls_rows = st[0:16]
    dl_rows = st[12:28]
    qg = gqd[:, :, :, :D].reshape(N, D)
    og = gqd[:, :, :, D:].reshape(N, D)
    s = nt(block_diag(gkv[c, z, :, :D]), qg)
    t = nt(block_diag(gkv[c, z, :, D:]), og)
    ps, dss = [], []
    for h in range(H):
        ok = me * N + iota((32, N), 0) * 8 + offs[0, h] < limit
        p = jnp.exp(jnp.where(ok, s[h * 32 : (h + 1) * 32] - ls_rows[h : h + 1], NEG))
        ps.append(p.astype(BF))
        dss.append((p * (t[h * 32 : (h + 1) * 32] - dl_rows[h : h + 1])).astype(BF))
    dmid[1] = diag_sum(nn(jnp.concatenate(dss, axis=0), qg), 32)
    dmid[2] = diag_sum(nn(jnp.concatenate(ps, axis=0), og), 32)

    to_mate(1, tilest.at[1 - c], tilest.at[1 - c]).wait_recv()
    weight_part(0)
    f3_wait(1)
    f3_wait(2)
    st = far2st[...].reshape(512, 128).T
    ls_rows = jnp.concatenate([st[0:16], st[0:16]], axis=0)
    dl_rows = jnp.concatenate([st[12:28], st[12:28]], axis=0)
    qdf = far2qd[...].reshape(512, D)
    s = nt(far_diag(floc[0]), qdf)
    t = pltpu.roll(nt(far_diag(floc[1]), qdf), 504, 1)
    row_h = iota((16, 512), 0)
    oks = [
        jnp.logical_and(
            jnp.logical_and(lead, row_h < H), (me * 2 + r) * 128 + off_col < limit
        )
        for r in range(2)
    ]
    expo = jnp.concatenate(
        [jnp.where(oks[r], (s - ls_rows)[16 * r : 16 * r + 16], NEG) for r in range(2)], axis=0
    )
    p = jnp.exp(expo)
    dfar[1, 0:2] = far_fold(nn((p * (t - dl_rows)).astype(BF), qdf))
    dfar[2, 0:2] = far_fold(nn(pltpu.roll(p, 8, 1).astype(BF), qdf))

    grad_part(1, dk)
    grad_part(2, dv)
    ring_d(0)
    ring_b(1)
    weight_part(1)
    weight_part(2)
    ring_c(1)

    @pl.loop(0, 3)
    def _(i):
        ls = pl.ds(pl.multiple_of(i * N, N), N)
        grad_tiles[:, ls] = nt(gp[...], wqkv[ls, :]).astype(BF)

    til_copy.start()
    ring_b(2)
    ring_b(3)
    ring_d(1)
    fin_start(0)
    ring_c(2)
    ring_c(3)
    fin_end(0)
    ring_d(2)
    ring_d(3)
    fin_start(1)
    fin_end(1)

    to_mate(0, cot.at[:, half_cols], cotr).wait_send()
    to_mate(1, tilest.at[c], tilest.at[c]).wait_send()
    to_mate(2, attnt.at[c], attnt.at[c]).wait_send()
    for a in range(3):
        to_mate(3 + a, gph.at[a, 1 - c], gpr.at[a]).wait_send()
    for b in range(4):
        for n in range(6):
            ring_copy(b, n).wait_send()
        for k in (1, 2, 3):
            second(b, k).wait_send()
    for r in range(2):
        for k in range(1, 8):
            fin_copy(r, k).wait_send()
    out_copy.wait()
    til_copy.wait()
    for t in range(3):
        for k in (1, 2, 3):
            f1_copy(t, k).wait_send()
            m1_copy(t, k).wait_send()
        for k in range(1, 16):
            f2_copy(t, k).wait_send()
        f3_copy(t).wait_send()
        for k in range(4):
            m2_copy(t, k).wait_send()


def copy_kernel(*refs):
    for src, dst in zip(refs[:4], refs[4:]):
        dst[...] = src[...]


def per_device(tiles, w_qkv, w_out, cotangent, offsets, pad_count):
    vm = pl.BlockSpec(memory_space=pltpu.VMEM)
    sm = pl.BlockSpec(memory_space=pltpu.SMEM)
    hbm = pl.BlockSpec(memory_space=pl.ANY)
    V = pltpu.VMEM
    dma = pltpu.SemaphoreType.DMA
    big = V((N, D), F32)
    bigb = V((N, D), BF)
    m32 = V((32, D), F32)
    f16 = V((16, D), F32)
    shapes = (
        jax.ShapeDtypeStruct((N, D), BF),
        jax.ShapeDtypeStruct((N, D), BF),
        jax.ShapeDtypeStruct((6, 3 * D), F32),
        jax.ShapeDtypeStruct((6, D), F32),
    )
    outs = pl.pallas_call(
        kernel,
        out_shape=shapes,
        in_specs=[sm, sm, hbm, hbm, hbm, hbm],
        out_specs=(hbm, hbm, vm, vm),
        scratch_shapes=[
            bigb, V((D, 3 * D), BF), V((D, D), BF), bigb, bigb, bigb,
            V((N, 4 * D), BF), bigb, bigb, V((D, 128), BF), V((D, 128), BF), f16,
            V((H, N, N), BF), big, big, big,
            V((2, 4, 32, 2 * D), BF), V((2, 4, 32, 2 * D), BF), V((2, 4, 32, 128), F32),
            V((4, 16, D), BF), V((4, 16, D), BF), V((4, 16, 128), F32),
            V((2, 16, 16, D), BF), V((2, 16, 16, D), BF), V((2, 16, 16, 128), F32),
            V((4, 16, D), BF), m32, m32, m32, f16, f16, f16, V((H * 32, N), BF), V((32, 512), F32),
            bigb, bigb, bigb, m32, m32, f16, f16,
            big, big, big, V((3, 32, D), F32), V((3, 16, D), F32), V((N, 3 * D), BF),
            V((2, D, N), BF), V((2, D, N), BF), V((N, 384), BF),
            V((3, 2, N, 384), BF), V((3, N, 384), BF),
            V((4, 4, 4, 48, 384), BF),
            V((4, 2, 2, 48, 384), BF), V((4, 2, 2, 48, 384), BF), V((4, 2, 4, 48, 384), BF),
            V((4, 4, 48, 384), BF), V((4, 4, 48, 384), BF), V((2, 2, 48, 384), BF),
            V((2, 8, 16, 384), BF), V((2, 8, 16, 384), BF),
            dma((5,)), dma((2,)),
            dma((3, 4)), dma((3, 4)), dma((3, 16)), dma((3, 16)), dma((3,)), dma((3,)),
            dma((3, 4)), dma((3, 4)), dma((3, 4)), dma((3, 4)),
            dma((6,)), dma((6,)), dma((4, 6)), dma((4, 6)), dma((4, 4)), dma((4, 4)),
            dma((2, 8)), dma((2, 8)),
        ],
        compiler_params=pltpu.CompilerParams(
            collective_id=0, has_side_effects=True, vmem_limit_bytes=64 * 1024 * 1024 - 65536
        ),
        name="layer",
    )(offsets, pad_count, tiles, w_qkv, w_out, cotangent)
    return pl.pallas_call(
        copy_kernel, out_shape=shapes, in_specs=[vm] * 4, out_specs=(vm,) * 4, name="results"
    )(*outs)


def solution(mesh):
    row = P("ctx", None)
    return jax.shard_map(
        per_device,
        mesh=mesh,
        in_specs=(row, P(), P(), row, P(), P()),
        out_specs=(row, row, row, row),
        check_vma=False,
    )
```

```python
import jax
import jax.numpy as jnp
from jax import lax
from jax.experimental import pallas as pl
from jax.experimental.pallas import tpu as pltpu
from jax.sharding import PartitionSpec as P

MESH = pl.DeviceIdType.MESH
N = 256
D = 768
H = 12
E = 64
NEG = -1e30
F32 = jnp.float32
BF = jnp.bfloat16
I32 = jnp.int32


def dot(a, b, ca, cb, precision=None):
    dims = (((ca,), (cb,)), ((), ()))
    return lax.dot_general(a, b, dims, precision=precision, preferred_element_type=F32)


def nn(a, b):
    return dot(a, b, 1, 0)


def nt(a, b):
    return dot(a, b, 1, 1)


def tn(a, b):
    return dot(a, b, 0, 0)


def iota(shape, dim):
    return lax.broadcasted_iota(I32, shape, dim)


def head_mask(h, dtype):
    return jnp.where(iota((1, D), 1) // E == h, 1.0, 0.0).astype(dtype)


def block_diag(x):
    return jnp.concatenate([x * head_mask(h, x.dtype) for h in range(H)], axis=0)


def diag_sum(x, rows):
    head = iota((rows, D), 1) // E
    out = jnp.zeros((rows, D), F32)
    for h in range(H):
        out = jnp.where(head == h, x[h * rows : (h + 1) * rows], out)
    return out


def per_head(cols, rows):
    head = iota((rows, D), 1) // E
    out = jnp.zeros((rows, D), F32)
    for h in range(H):
        out = jnp.where(head == h, cols[h * rows : (h + 1) * rows], out)
    return out


def kernel(
    offs, pad, tiles_h, wqkv_h, wout_h, cot_h,
    rows_h, gtil_h, g_qkv, g_out,
    tiles, wqkv, wout, cot, out_rows, grad_tiles,
    pk, midm, farm, sel1, sel2, hsel, emat, num, den, mx,
    gkv, gqd, gst, far1kv, far1qd, far1st, far2kv, far2qd, far2st,
    floc, mnum, mden, mmax, fnum, fden, fmax, emid, efar,
    attn, sdo, npr, mlse, mprod, flse, fprod,
    dq, dk, dv, dmid, dfar, gp, tilest, attnt, cotr, gph, gpr,
    part, r1, tmp, r2, acc, s2, tot, fin, finr,
    ls_, os_, f1s, f1r, f2s, f2r, f3s, f3r, m1s, m1r, m2s, m2r,
    xs, xr, rs, rr_, ss, sr, es_, er_,
):
    me = lax.axis_index("ctx")
    c = me % 2
    z = me // 2 % 4
    g = me // 8
    x = g // 4
    y = g % 4
    mate = g * 8 + z * 2 + (1 - c)

    def zpeer(k):
        return g * 8 + (z + k) % 4 * 2 + c

    def gpeer(k):
        return (g + k) % 16 * 8 + z * 2 + c

    def rc(src, dst, ss, rs, dev):
        return pltpu.make_async_remote_copy(
            src_ref=src, dst_ref=dst, send_sem=ss, recv_sem=rs, device_id=(dev,), device_id_type=MESH
        )

    def load(src, dst, n):
        return pltpu.make_async_copy(src, dst, ls_.at[n])

    loads = [load(tiles_h, tiles, 0)]
    for i in range(3):
        for a in (1, 2):
            cols = pl.ds(a * D + i * N, N)
            loads.append(load(wqkv_h.at[:, cols], wqkv.at[:, cols], 1 + i))
    later = [
        load(wqkv_h.at[:, pl.ds(0, D)], wqkv.at[:, pl.ds(0, D)], 4),
        load(cot_h, cot, 5),
        load(wout_h, wout, 6),
    ]
    for item in loads:
        item.start()
    barrier = pltpu.get_barrier_semaphore()
    peers = [mate] + [zpeer(k) for k in (1, 2, 3)] + [gpeer(k) for k in range(1, 16)]
    peers += [g * 8 + (z + k) % 4 * 2 + (1 - c) for k in (1, 2, 3)]
    for p in peers:
        pl.semaphore_signal(barrier, inc=1, device_id=(p,), device_id_type=MESH)

    FAR1 = (far1kv, far1qd, far1st)
    FAR2 = (far2kv, far2qd, far2st)
    MID = (gkv, gqd, gst)

    def f1_copy(t, k):
        return rc(FAR1[t].at[z], FAR1[t].at[z], f1s.at[t], f1r.at[t], zpeer(k))

    def f1_all(t):
        some = FAR1[t].at[pl.ds(0, 3)]
        return rc(some, some, f1s.at[t], f1r.at[t], zpeer(1))

    def f1_start(t):
        for k in (1, 3, 2):
            f1_copy(t, k).start()

    def f1_wait(t):
        f1_all(t).wait_recv()

    def f2_copy(t, k):
        return rc(FAR2[t].at[c, g], FAR2[t].at[c, g], f2s.at[t], f2r.at[t], gpeer(k))

    def f2_all(t):
        some = FAR2[t].at[c, pl.ds(0, 15)]
        return rc(some, some, f2s.at[t], f2r.at[t], gpeer(1))

    def f2_start(t):
        a = FAR1[t]
        FAR2[t][c, g] = (
            a[0].astype(F32) + a[1].astype(F32) + a[2].astype(F32) + a[3].astype(F32)
        ).astype(a.dtype)
        for k in range(1, 16):
            f2_copy(t, k).start()

    def f2_wait(t):
        f2_all(t).wait_recv()

    def f3_copy(t):
        return rc(FAR2[t].at[c], FAR2[t].at[c], f3s.at[t], f3r.at[t], mate)

    def f3_wait(t):
        rc(FAR2[t].at[1 - c], FAR2[t].at[1 - c], f3s.at[t], f3r.at[t], mate).wait_recv()

    def m1_copy(t, k):
        return rc(MID[t].at[c, z], MID[t].at[c, z], m1s.at[t], m1r.at[t], zpeer(k))

    def m1_all(t):
        some = MID[t].at[c, pl.ds(0, 3)]
        return rc(some, some, m1s.at[t], m1r.at[t], zpeer(1))

    def m2_copy(t, k):
        o = (z + k) % 4
        return rc(MID[t].at[c, o], MID[t].at[c, o], m2s.at[t], m2r.at[t], mate)

    def m2_all(t, who):
        return rc(MID[t].at[who], MID[t].at[who], m2s.at[t], m2r.at[t], mate)

    def m1_start(t):
        for k in (1, 3, 2):
            m1_copy(t, k).start()
        m2_copy(t, 0).start()

    def m1_forward(t):
        m1_all(t).wait_recv()
        for k in (1, 3, 2):
            m2_copy(t, k).start()

    def m2_wait(t):
        m2_all(t, 1 - c).wait_recv()

    def to_mate(t, src, dst):
        return rc(src, dst, xs.at[t], xr.at[t], mate)

    half_cols = pl.ds(pl.multiple_of(384 * (1 - c), 128), 384)
    own_cols = pl.ds(pl.multiple_of(384 * c, 128), 384)

    limit = N * 128 - pad[0]
    lane_head = iota((1, D), 1) // E
    o0 = jnp.zeros((1, D), I32)
    o1 = jnp.zeros((1, D), I32)
    for h in range(H):
        o0 = jnp.where(lane_head == h, offs[0, h], o0)
        o1 = jnp.where(lane_head == h, offs[1, h], o1)
    midm[...] = jnp.where(iota((N, D), 0) % 8 == o0, 1.0, 0.0).astype(BF)
    farm[...] = jnp.where(iota((N, D), 0) % 128 == o1, 1.0, 0.0).astype(BF)

    r0 = iota((D, 128), 0)
    l0 = iota((D, 128), 1)
    sel1[...] = jnp.where(jnp.logical_and(r0 == l0 * E, l0 < H), 1.0, 0.0).astype(BF)
    sel2[...] = jnp.where(r0 // E == l0 - H, 1.0, 0.0).astype(BF)
    hsel[...] = jnp.where(iota((16, D), 1) // E == iota((16, D), 0), 1.0, 0.0)
    pool_mid = jnp.where(iota((32, N), 1) // 8 == iota((32, N), 0), 1.0, 0.0).astype(BF)
    two = iota((16, N), 1) // 128
    row = iota((16, N), 0)
    pool_far = jnp.where(row == two, 1.0, 0.0).astype(BF)
    place = jnp.concatenate(
        [
            jnp.where(row == 2 * z + two, 1.0, 0.0),
            jnp.where(row == 8 + 2 * z + two, 1.0, 0.0),
        ],
        axis=1,
    ).astype(BF)

    def picks(t, i, a, b):
        ls = pl.ds(pl.multiple_of(i * N, N), N)
        hi = pl.ds(pl.multiple_of(D + i * N, N), N)
        mk = midm[:, ls]
        fk = farm[:, ls]
        fa = a * fk
        fb = b * fk
        FAR1[t][z, :, ls] = nn(place, jnp.concatenate([fa, fb], axis=0)).astype(BF)
        MID[t][c, z, :, ls] = nn(pool_mid, a * mk).astype(BF)
        MID[t][c, z, :, hi] = nn(pool_mid, b * mk).astype(BF)
        floc[2 * t, :, ls] = nn(pool_far, fa).astype(BF)
        floc[2 * t + 1, :, ls] = nn(pool_far, fb).astype(BF)

    loads[0].wait()

    for i in range(3):
        cols = pl.ds(i * 2 * N, 2 * N)
        load(wqkv_h.at[:, cols], wqkv.at[:, cols], 1 + i).wait()
        if i == 0:
            for item in later:
                item.start()
        kc = pl.ds(D + i * N, N)
        vc = pl.ds(2 * D + i * N, N)
        kk = nn(tiles[...], wqkv[:, kc]).astype(BF)
        vv = nn(tiles[...], wqkv[:, vc]).astype(BF)
        pk[:, kc] = kk
        pk[:, vc] = vv
        picks(0, i, kk, vv)

    pl.semaphore_wait(barrier, len(peers))
    f1_start(0)
    m1_start(0)
    for item in later:
        item.wait()
    to_mate(0, cot.at[:, half_cols], cotr).start()

    @pl.loop(0, 3)
    def _(i):
        qc = pl.ds(pl.multiple_of(i * N, N), N)
        dc = pl.ds(pl.multiple_of(3 * D + i * N, N), N)
        qq = nn(tiles[...], wqkv[:, qc]).astype(BF) * jnp.asarray(0.125, BF)
        dd = nt(cot[...], wout[qc, :]).astype(BF)
        pk[:, qc] = qq
        pk[:, dc] = dd
        picks(1, i, qq, dd)


    half = iota((1, 128), 1) // E
    hm = [jnp.where(half == a, 1.0, 0.0).astype(BF) for a in range(2)]

    def lanes(p, base=0):
        return pl.ds(pl.multiple_of(base + p * 128, 128), 128)

    def near_forward(lo, hi):
        @pl.loop(lo, hi)
        def _(p):
            q2 = pk[:, lanes(p)]
            k2 = pk[:, lanes(p, D)]
            v2 = pk[:, lanes(p, 2 * D)]
            bias = jnp.where(me * N + iota((1, N), 1) < limit, 0.0, NEG)
            es, ms = [], []
            for a in range(2):
                s = nt(q2 * hm[a], k2) + bias
                m = jnp.max(s, axis=1, keepdims=True)
                e = jnp.exp(s - m).astype(BF)
                emat[2 * p + a] = e
                es.append(e)
                ms.append(m)
            rhs = jnp.concatenate(
                [
                    jnp.concatenate([v2 * hm[a], jnp.broadcast_to(hm[a], (N, 128))], axis=1)
                    for a in range(2)
                ],
                axis=0,
            )
            nd = nn(jnp.concatenate(es, axis=1), rhs)
            num[:, lanes(p)] = nd[:, :128]
            den[:, lanes(p)] = nd[:, 128:]
            mx[:, lanes(p)] = jnp.where(iota((N, 128), 1) < E, ms[0], ms[1])

    f1_wait(0)
    f2_start(0)
    near_forward(0, 6)
    tilest[c] = tiles[...].T
    m1_forward(0)
    f1_start(1)
    m1_start(1)
    to_mate(1, tilest.at[c], tilest.at[c]).start()

    m2_wait(0)
    kg = gkv[:, :, :, :D].reshape(N, D)
    vg = gkv[:, :, :, D:].reshape(N, D)
    gdev = g * 8 + iota((32, N), 1) // 32 % 4 * 2 + iota((32, N), 1) // 128
    gpos = gdev * N + iota((32, N), 1) % 32 * 8
    gbias = jnp.concatenate(
        [jnp.where(gpos + offs[0, h] < limit, 0.0, NEG) for h in range(H)], axis=0
    )
    s = nt(block_diag(gqd[c, z, :, :D]), kg) + gbias
    m = jnp.max(s, axis=1, keepdims=True)
    e = jnp.exp(s - m)
    total = jnp.sum(e, axis=1, keepdims=True)
    e = e.astype(BF)
    emid[...] = e
    mnum[...] = diag_sum(nn(e, vg), 32)
    mden[...] = per_head(total, 32)
    mmax[...] = per_head(m, 32)

    f2_wait(0)
    f3_copy(0).start()
    f1_wait(1)
    f2_start(1)
    f3_wait(0)

    heads = hsel[...]
    headb = heads.astype(BF)

    def far_diag(v):
        return jnp.concatenate([v[0:1] * headb, v[1:2] * headb], axis=0)

    def far_fold(v):
        return jnp.concatenate(
            [jnp.sum(v[16 * r : 16 * r + 16] * heads, axis=0, keepdims=True) for r in range(2)],
            axis=0,
        )

    col = iota((16, 512), 1)
    fdev = col // 16 % 16 * 8 + col // 2 % 4 * 2 + col // 256
    fpos = (fdev * 2 + col % 2) * 128
    lead = col // 8 % 2 == 0
    off_col = jnp.zeros((16, 512), I32)
    for h in range(H):
        off_col = jnp.where(iota((16, 512), 0) == h, offs[1, h], off_col)
    fbias = jnp.where(jnp.logical_and(lead, fpos + off_col < limit), 0.0, NEG)
    fbias = jnp.concatenate([fbias, fbias], axis=0)
    kvf = far2kv[...].reshape(512, D)
    s = nt(far_diag(floc[2]), kvf) + fbias
    m = jnp.max(s, axis=1, keepdims=True)
    e = jnp.exp(s - m)
    efar[...] = e
    fnum[0:2] = far_fold(nn(pltpu.roll(e, 8, 1).astype(BF), kvf))
    fden[0:2] = far_fold(jnp.broadcast_to(jnp.sum(e, axis=1, keepdims=True), (32, D)))
    fmax[0:2] = far_fold(jnp.broadcast_to(m, (32, D)))

    def spread_mid(x):
        return jnp.broadcast_to(x[:, None, :], (32, 8, 128)).reshape(N, 128)

    def spread_far(x):
        return jnp.concatenate(
            [jnp.broadcast_to(x[0:1], (128, 128)), jnp.broadcast_to(x[1:2], (128, 128))], axis=0
        )

    def pick_mid(x):
        return jnp.sum(x.reshape(32, 8, 128), axis=1)

    def pick_far(x):
        return jnp.concatenate(
            [
                jnp.sum(x[:128], axis=0, keepdims=True),
                jnp.sum(x[128:], axis=0, keepdims=True),
                jnp.zeros((14, 128), F32),
            ],
            axis=0,
        )

    @pl.loop(0, 6)
    def _(p):
        ls = lanes(p)
        mm = midm[:, ls].astype(F32)
        fm = farm[:, ls].astype(F32)
        m0 = mx[:, ls]
        m1 = jnp.where(mm > 0.5, spread_mid(mmax[:, ls]), NEG)
        m2 = jnp.where(fm > 0.5, spread_far(fmax[0:2, ls]), NEG)
        top = jnp.maximum(jnp.maximum(m0, m1), m2)
        w0 = jnp.exp(m0 - top)
        w1 = jnp.exp(m1 - top)
        w2 = jnp.exp(m2 - top)
        total = w0 * den[:, ls] + w1 * spread_mid(mden[:, ls]) + w2 * spread_far(fden[0:2, ls])
        inv = 1.0 / total
        mixed = w0 * num[:, ls] + w1 * spread_mid(mnum[:, ls]) + w2 * spread_far(fnum[0:2, ls])
        at = (mixed * inv).astype(BF)
        attn[:, ls] = at
        do = pk[:, lanes(p, 3 * D)].astype(F32)
        prod = do * at.astype(F32)
        scale = w0 * inv
        sdo[:, ls] = (scale * do).astype(BF)
        npr[:, ls] = (-scale * prod).astype(BF)
        lse = top + jnp.log(total)
        mlse[:, ls] = pick_mid(lse * mm)
        mprod[:, ls] = pick_mid(prod * mm)
        flse[:, ls] = pick_far(lse * fm)
        fprod[:, ls] = pick_far(prod * fm)

    lse_rows = jnp.concatenate([mlse[...], flse[...]], axis=0)
    prod_rows = jnp.concatenate([mprod[...], fprod[...]], axis=0)
    l_hi = lse_rows.astype(BF)
    left = lse_rows - l_hi.astype(F32)
    l_mid = left.astype(BF)
    l_lo = (left - l_mid.astype(F32)).astype(BF)
    p_hi = prod_rows.astype(BF)
    p_lo = (prod_rows - p_hi.astype(F32)).astype(BF)
    lt = nn(jnp.concatenate([l_hi, l_mid, l_lo], axis=0), sel1[...])
    pt = nn(jnp.concatenate([p_hi, p_lo], axis=0), sel2[...])
    st = lt[0:48] + lt[48:96] + lt[96:144] + pt[0:48] + pt[48:96]
    gst[c, z] = st[0:32]
    fs = st[32:48]
    r8 = iota((8, 128), 0)
    far1st[z] = jnp.where(r8 == 2 * z, fs[0:1], jnp.where(r8 == 2 * z + 1, fs[1:2], 0.0))
    f1_start(2)
    m1_start(2)

    attnt[c] = attn[...].T
    to_mate(2, attnt.at[c], attnt.at[c]).start()
    out_copy = pltpu.make_async_copy(out_rows, rows_h, os_.at[0])
    til_copy = pltpu.make_async_copy(grad_tiles, gtil_h, os_.at[1])

    @pl.loop(0, 3)
    def _(i):
        ls = pl.ds(pl.multiple_of(i * N, N), N)
        out_rows[:, ls] = (tiles[:, ls].astype(F32) + nn(attn[...], wout[:, ls])).astype(BF)

    def put_part(b, v):
        part[b] = v.astype(BF).reshape(4, 4, 48, 384)

    def dev(x_, y_):
        return ((x_ % 4 * 4 + y_ % 4) * 4 + z) * 2 + c

    pos = (x, y)
    step = (lambda k: dev(x + k, y), lambda k: dev(x, y + k))

    def where_in(b, q, h):
        some = slice(None) if h is None else pl.ds(2 * h, 2)
        return (b, q, some) if b % 2 == 0 else (b, some, q)

    def ring_copy(b, n):
        p = pos[b % 2]
        nxt, prv = step[b % 2](1), step[b % 2](3)
        up, down, far = (p + 1) % 4, (p + 3) % 4, (p + 2) % 4
        src, dst, to = (
            lambda: (part.at[where_in(b, far, 0)], r1.at[b, 0], nxt),
            lambda: (part.at[where_in(b, far, 1)], r1.at[b, 1], prv),
            lambda: (part.at[where_in(b, up, 1)], r2.at[b, 0, pl.ds(2, 2)], nxt),
            lambda: (part.at[where_in(b, down, 0)], r2.at[b, 1, pl.ds(0, 2)], prv),
            lambda: (tmp.at[b, 0], r2.at[b, 0, pl.ds(0, 2)], nxt),
            lambda: (tmp.at[b, 1], r2.at[b, 1, pl.ds(2, 2)], prv),
        )[n]()
        return rc(src, dst, rs.at[b], rr_.at[b, min(n, 2)], to)

    def ring_a(b):
        for n in range(4):
            ring_copy(b, n).start()

    def ring_b(b):
        p = pos[b % 2]
        for h, q in ((0, (p + 1) % 4), (1, (p + 3) % 4)):
            ring_copy(b, h).wait_recv()
            tmp[b, h] = (part[where_in(b, q, h)].astype(F32) + r1[b, h].astype(F32)).astype(BF)
            ring_copy(b, 4 + h).start()

    def second(b, k):
        j = (b + 1) % 2
        q = (pos[j] + k) % 4
        return rc(acc.at[b, q], s2.at[b, pos[j]], ss.at[b], sr.at[b], step[j](k))

    def second_all(b):
        some = s2.at[b, pl.ds(0, 3)]
        return rc(some, some, ss.at[b], sr.at[b], mate)

    def ring_c(b):
        rc(r2.at[b], r2.at[b], rs.at[b], rr_.at[b, 2], mate).wait_recv()
        mine = part[where_in(b, pos[b % 2], None)].astype(F32)
        acc[b] = (mine + r2[b, 0].astype(F32) + r2[b, 1].astype(F32)).astype(BF)
        for k in (2, 1, 3):
            second(b, k).start()

    def ring_d(b):
        j = (b + 1) % 2
        total = acc[b, pos[j]].astype(F32)
        second_all(b).wait_recv()
        for k in (1, 3, 2):
            total = total + s2[b, (pos[j] + k) % 4].astype(F32)
        tot[b // 2, b % 2] = total.astype(BF)

    own = z * 2 + c
    er = iota((128, 96), 0)
    ek = er % 8
    spread = jnp.where(
        jnp.logical_and(iota((128, 96), 1) == er // 8 % 2 * 48 + er // 16 * 6 + ek, ek < 6), 1.0, 0.0
    ).astype(BF)

    def fin_copy(r, k):
        o = (own + k) % 8
        return rc(fin.at[r, o], finr.at[r, own], es_.at[r], er_.at[r], g * 8 + o)

    def fin_all(r):
        some = finr.at[r, pl.ds(0, 7)]
        return rc(some, some, es_.at[r], er_.at[r], mate)

    def fin_start(r):
        fin[r] = nn(spread, tot[r].reshape(96, 384)).astype(BF).reshape(8, 16, 384)
        for k in range(1, 8):
            fin_copy(r, k).start()
        finr[r, own] = fin[r, own]

    def fin_end(r):
        fin_all(r).wait_recv()
        for a in range(2):
            v = finr[r, a].astype(F32)
            for o in (2, 4, 6):
                v = v + finr[r, o + a].astype(F32)
            for i in range(2):
                w = v[8 * i : 8 * i + 6]
                at = (2 * r - 1 + i) * D + 384 * a
                if r == 0 and i == 0:
                    g_out[:, 384 * a : 384 * a + 384] = w
                else:
                    g_qkv[:, at : at + 384] = w

    f1_wait(2)
    f2_start(2)
    to_mate(0, cotr, cotr).wait_recv()
    to_mate(2, attnt.at[1 - c], attnt.at[1 - c]).wait_recv()
    put_part(0, nn(attnt[c], cot[:, own_cols]) + nn(attnt[1 - c], cotr[...]))
    ring_a(0)
    out_copy.start()

    def near_backward(lo, hi_):
        @pl.loop(lo, hi_)
        def _(p):
            ls = lanes(p)
            q2 = pk[:, ls]
            k2 = pk[:, lanes(p, D)]
            v2 = pk[:, lanes(p, 2 * D)]
            so = sdo[:, ls]
            sp = npr[:, ls]
            rhs = jnp.concatenate([v2, jnp.ones((N, 128), BF)], axis=1)
            es, ds = [], []
            for a in range(2):
                lhs = jnp.concatenate([so * hm[a], sp * hm[a]], axis=1)
                t = nt(lhs, rhs)
                e = emat[2 * p + a]
                es.append(e)
                ds.append((e.astype(F32) * t).astype(BF))
            dq[:, ls] = 0.125 * nn(
                jnp.concatenate(ds, axis=1), jnp.concatenate([k2 * hm[0], k2 * hm[1]], axis=0)
            )
            dk[:, ls] = tn(
                jnp.concatenate(ds, axis=0), jnp.concatenate([q2 * hm[0], q2 * hm[1]], axis=0)
            )
            dv[:, ls] = tn(
                jnp.concatenate(es, axis=0), jnp.concatenate([so * hm[0], so * hm[1]], axis=0)
            )

    near_backward(0, 2)
    m1_forward(1)
    m1_forward(2)
    near_backward(2, 4)
    f2_wait(1)
    f3_copy(1).start()
    near_backward(4, 6)
    f2_wait(2)
    f3_copy(2).start()

    kg = gkv[:, :, :, :D].reshape(N, D)
    vg = gkv[:, :, :, D:].reshape(N, D)
    scale = jnp.exp(mmax[...] - mlse[...])
    so = (scale * gqd[c, z, :, D:].astype(F32)).astype(BF)
    sp = scale * mprod[...]
    dl = jnp.concatenate(
        [jnp.sum(sp * head_mask(h, F32), axis=1, keepdims=True) for h in range(H)], axis=0
    )
    ds = (emid[...].astype(F32) * (nt(block_diag(so), vg) - dl)).astype(BF)
    dmid[0] = 0.125 * diag_sum(nn(ds, kg), 32)

    scale = jnp.exp(fmax[0:2] - flse[0:2])
    so = (scale * floc[3, 0:2].astype(F32)).astype(BF)
    sp = scale * fprod[0:2]
    dl = jnp.concatenate(
        [jnp.sum(sp[r : r + 1] * heads, axis=1, keepdims=True) for r in range(2)], axis=0
    )
    kvf = far2kv[...].reshape(512, D)
    t = pltpu.roll(nt(far_diag(so), kvf), 504, 1)
    dfar[0, 0:2] = 0.125 * far_fold(nn((efar[...] * (t - dl)).astype(BF), kvf))

    def grad_part(a, near):
        @pl.loop(0, 6)
        def _(p):
            ls = lanes(p)
            mm = midm[:, ls].astype(F32)
            fm = farm[:, ls].astype(F32)
            v = near[:, ls] + mm * spread_mid(dmid[a, :, ls]) + fm * spread_far(dfar[a, 0:2, ls])
            v = v.astype(BF)
            gp[:, lanes(p, a * D)] = v
            gph[a, p // 3, :, lanes(p % 3)] = v

        to_mate(3 + a, gph.at[a, 1 - c], gpr.at[a]).start()

    def weight_part(a):
        to_mate(3 + a, gpr.at[a], gpr.at[a]).wait_recv()
        put_part(1 + a, nn(tilest[c], gph[a, c]) + nn(tilest[1 - c], gpr[a]))
        ring_a(1 + a)

    grad_part(0, dq)
    ring_b(0)
    m2_wait(1)
    m2_wait(2)

    st = gst[...].reshape(N, 128).T
    ls_rows = st[0:16]
    dl_rows = st[12:28]
    qg = gqd[:, :, :, :D].reshape(N, D)
    og = gqd[:, :, :, D:].reshape(N, D)
    s = nt(block_diag(gkv[c, z, :, :D]), qg)
    t = nt(block_diag(gkv[c, z, :, D:]), og)
    ps, dss = [], []
    for h in range(H):
        ok = me * N + iota((32, N), 0) * 8 + offs[0, h] < limit
        p = jnp.exp(jnp.where(ok, s[h * 32 : (h + 1) * 32] - ls_rows[h : h + 1], NEG))
        ps.append(p.astype(BF))
        dss.append((p * (t[h * 32 : (h + 1) * 32] - dl_rows[h : h + 1])).astype(BF))
    dmid[1] = diag_sum(nn(jnp.concatenate(dss, axis=0), qg), 32)
    dmid[2] = diag_sum(nn(jnp.concatenate(ps, axis=0), og), 32)

    to_mate(1, tilest.at[1 - c], tilest.at[1 - c]).wait_recv()
    weight_part(0)
    f3_wait(1)
    f3_wait(2)
    st = far2st[...].reshape(32, 8, 128)
    st = jnp.concatenate([st, jnp.zeros_like(st)], axis=1).reshape(512, 128).T
    ls_rows = jnp.concatenate([st[0:16], st[0:16]], axis=0)
    dl_rows = jnp.concatenate([st[12:28], st[12:28]], axis=0)
    qdf = far2qd[...].reshape(512, D)
    s = nt(far_diag(floc[0]), qdf)
    t = pltpu.roll(nt(far_diag(floc[1]), qdf), 504, 1)
    row_h = iota((16, 512), 0)
    oks = [
        jnp.logical_and(
            jnp.logical_and(lead, row_h < H), (me * 2 + r) * 128 + off_col < limit
        )
        for r in range(2)
    ]
    expo = jnp.concatenate(
        [jnp.where(oks[r], (s - ls_rows)[16 * r : 16 * r + 16], NEG) for r in range(2)], axis=0
    )
    p = jnp.exp(expo)
    dfar[1, 0:2] = far_fold(nn((p * (t - dl_rows)).astype(BF), qdf))
    dfar[2, 0:2] = far_fold(nn(pltpu.roll(p, 8, 1).astype(BF), qdf))

    grad_part(1, dk)
    grad_part(2, dv)
    ring_c(0)
    weight_part(1)
    weight_part(2)

    @pl.loop(0, 3)
    def _(i):
        ls = pl.ds(pl.multiple_of(i * N, N), N)
        grad_tiles[:, ls] = nt(gp[...], wqkv[ls, :]).astype(BF)

    ring_b(1)
    til_copy.start()
    ring_b(2)
    ring_b(3)
    ring_c(1)
    ring_d(0)
    ring_c(2)
    ring_c(3)
    ring_d(1)
    fin_start(0)
    ring_d(2)
    ring_d(3)
    fin_start(1)
    fin_end(0)
    fin_end(1)

    to_mate(0, cot.at[:, half_cols], cotr).wait_send()
    to_mate(1, tilest.at[c], tilest.at[c]).wait_send()
    to_mate(2, attnt.at[c], attnt.at[c]).wait_send()
    for a in range(3):
        to_mate(3 + a, gph.at[a, 1 - c], gpr.at[a]).wait_send()
    for b in range(4):
        some = part.at[b, pl.ds(0, 3)]
        rc(some, some, rs.at[b], rr_.at[b, 2], mate).wait_send()
        second_all(b).wait_send()
    for r in range(2):
        fin_all(r).wait_send()
    out_copy.wait()
    til_copy.wait()
    for t in range(3):
        f1_all(t).wait_send()
        m1_all(t).wait_send()
        f2_all(t).wait_send()
        f3_copy(t).wait_send()
        m2_all(t, c).wait_send()


def copy_kernel(*refs):
    for src, dst in zip(refs[:4], refs[4:]):
        dst[...] = src[...]


def per_device(tiles, w_qkv, w_out, cotangent, offsets, pad_count):
    vm = pl.BlockSpec(memory_space=pltpu.VMEM)
    sm = pl.BlockSpec(memory_space=pltpu.SMEM)
    hbm = pl.BlockSpec(memory_space=pl.ANY)
    V = pltpu.VMEM
    dma = pltpu.SemaphoreType.DMA
    big = V((N, D), F32)
    bigb = V((N, D), BF)
    m32 = V((32, D), F32)
    f16 = V((16, D), F32)
    shapes = (
        jax.ShapeDtypeStruct((N, D), BF),
        jax.ShapeDtypeStruct((N, D), BF),
        jax.ShapeDtypeStruct((6, 3 * D), F32),
        jax.ShapeDtypeStruct((6, D), F32),
    )
    outs = pl.pallas_call(
        kernel,
        out_shape=shapes,
        in_specs=[sm, sm, hbm, hbm, hbm, hbm],
        out_specs=(hbm, hbm, vm, vm),
        scratch_shapes=[
            bigb, V((D, 3 * D), BF), V((D, D), BF), bigb, bigb, bigb,
            V((N, 4 * D), BF), bigb, bigb, V((D, 128), BF), V((D, 128), BF), f16,
            V((H, N, N), BF), big, big, big,
            V((2, 4, 32, 2 * D), BF), V((2, 4, 32, 2 * D), BF), V((2, 4, 32, 128), F32),
            V((4, 16, D), BF), V((4, 16, D), BF), V((4, 8, 128), F32),
            V((2, 16, 16, D), BF), V((2, 16, 16, D), BF), V((2, 16, 8, 128), F32),
            V((4, 16, D), BF), m32, m32, m32, f16, f16, f16, V((H * 32, N), BF), V((32, 512), F32),
            bigb, bigb, bigb, m32, m32, f16, f16,
            big, big, big, V((3, 32, D), F32), V((3, 16, D), F32), V((N, 3 * D), BF),
            V((2, D, N), BF), V((2, D, N), BF), V((N, 384), BF),
            V((3, 2, N, 384), BF), V((3, N, 384), BF),
            V((4, 4, 4, 48, 384), BF),
            V((4, 2, 2, 48, 384), BF), V((4, 2, 2, 48, 384), BF), V((4, 2, 4, 48, 384), BF),
            V((4, 4, 48, 384), BF), V((4, 4, 48, 384), BF), V((2, 2, 48, 384), BF),
            V((2, 8, 16, 384), BF), V((2, 8, 16, 384), BF),
            dma((7,)), dma((2,)),
            dma((3,)), dma((3,)), dma((3,)), dma((3,)), dma((3,)), dma((3,)),
            dma((3,)), dma((3,)), dma((3,)), dma((3,)),
            dma((6,)), dma((6,)), dma((4,)), dma((4, 3)), dma((4,)), dma((4,)),
            dma((2,)), dma((2,)),
        ],
        compiler_params=pltpu.CompilerParams(
            collective_id=0, has_side_effects=True, vmem_limit_bytes=64 * 1024 * 1024 - 65536
        ),
        name="layer",
    )(offsets, pad_count, tiles, w_qkv, w_out, cotangent)
    return pl.pallas_call(
        copy_kernel, out_shape=shapes, in_specs=[vm] * 4, out_specs=(vm,) * 4, name="results"
    )(*outs)


def solution(mesh):
    row = P("ctx", None)
    return jax.shard_map(
        per_device,
        mesh=mesh,
        in_specs=(row, P(), P(), row, P(), P()),
        out_specs=(row, row, row, row),
        check_vma=False,
    )
```

```python
import jax
import jax.numpy as jnp
from jax import lax
from jax.experimental import pallas as pl
from jax.experimental.pallas import tpu as pltpu
from jax.sharding import PartitionSpec as P

MESH = pl.DeviceIdType.MESH
N = 256
D = 768
H = 12
E = 64
NEG = -1e30
F32 = jnp.float32
BF = jnp.bfloat16
I32 = jnp.int32


def dot(a, b, ca, cb, precision=None):
    dims = (((ca,), (cb,)), ((), ()))
    return lax.dot_general(a, b, dims, precision=precision, preferred_element_type=F32)


def nn(a, b):
    return dot(a, b, 1, 0)


def nt(a, b):
    return dot(a, b, 1, 1)


def tn(a, b):
    return dot(a, b, 0, 0)


def iota(shape, dim):
    return lax.broadcasted_iota(I32, shape, dim)


def head_mask(h, dtype):
    return jnp.where(iota((1, D), 1) // E == h, 1.0, 0.0).astype(dtype)


def block_diag(x):
    return jnp.concatenate([x * head_mask(h, x.dtype) for h in range(H)], axis=0)


def diag_sum(x, rows):
    head = iota((rows, D), 1) // E
    out = jnp.zeros((rows, D), F32)
    for h in range(H):
        out = jnp.where(head == h, x[h * rows : (h + 1) * rows], out)
    return out


def per_head(cols, rows):
    head = iota((rows, D), 1) // E
    out = jnp.zeros((rows, D), F32)
    for h in range(H):
        out = jnp.where(head == h, cols[h * rows : (h + 1) * rows], out)
    return out


def kernel(
    offs_h, pad_h, tiles_h, wqkv_h, wout_h, cot_h,
    rows_h, gtil_h, g_qkv, g_out,
    offs, pad, tiles, wqkv, wout, cot, out_rows, grad_tiles,
    pk, midm, farm, nfar, sel1, sel2, hsel, emat, dsm, num, den, mx,
    gkv, gqd, gst, far1kv, far1qd, far1st, far2kv, far2qd, far2st,
    floc, mnum, mden, mmax, fnum, fden, fmax, emid, efar,
    attn, sdo, npr, mlse, mprod, flse, fprod, fat, fsc,
    dq, dk, dv, dmid, dfar, gp, tilest, tilesp, attnt, cotr, perm, gph, gpr,
    part, r1, tmp, r2, acc, s2, tot, fin, finr,
    stage, pz, z1, zt, z2, zacc, zs, zf, zm,
    ls_, os_, f1s, f1r, f2s, f2r, f3s, f3r, m1s, m1r, m2s, m2r,
    xs, xr, rs, rr_, ss, sr, es_, er_,
    zrs, zrr, zss, zsr, zms, zmr,
):
    me = lax.axis_index("ctx")
    c = me % 2
    z = me // 2 % 4
    g = me // 8
    x = g // 4
    y = g % 4
    mate = g * 8 + z * 2 + (1 - c)

    def zpeer(k):
        return g * 8 + (z + k) % 4 * 2 + c

    def gpeer(k):
        return (g + k) % 16 * 8 + z * 2 + c

    def rc(src, dst, ss, rs, dev):
        return pltpu.make_async_remote_copy(
            src_ref=src, dst_ref=dst, send_sem=ss, recv_sem=rs, device_id=(dev,), device_id_type=MESH
        )

    def load(src, dst, n):
        return pltpu.make_async_copy(src, dst, ls_.at[n])

    loads = [load(tiles_h, tiles, 0)]
    for i in range(3):
        for a in (1, 2):
            cols = pl.ds(a * D + i * N, N)
            loads.append(load(wqkv_h.at[:, cols], wqkv.at[:, cols], 1 + i))
    later = [
        load(wqkv_h.at[:, pl.ds(0, D)], wqkv.at[:, pl.ds(0, D)], 4),
        load(cot_h, cot, 5),
        load(wout_h, wout, 6),
    ]
    small = (load(offs_h, offs, 7), load(pad_h, pad, 8))
    for item in small:
        item.start()
    for item in loads:
        item.start()
    barrier = pltpu.get_barrier_semaphore()
    peers = [mate] + [zpeer(k) for k in (1, 2, 3)] + [gpeer(k) for k in range(1, 16)]
    peers += [g * 8 + (z + k) % 4 * 2 + (1 - c) for k in (1, 2, 3)]
    for p in peers:
        pl.semaphore_signal(barrier, inc=1, device_id=(p,), device_id_type=MESH)

    FAR1 = (far1kv, far1qd, far1st)
    FAR2 = (far2kv, far2qd, far2st)
    MID = (gkv, gqd, gst)

    def f1_copy(t, k):
        return rc(FAR1[t].at[z], FAR1[t].at[z], f1s.at[t], f1r.at[t], zpeer(k))

    def f1_all(t):
        some = FAR1[t].at[pl.ds(0, 3)]
        return rc(some, some, f1s.at[t], f1r.at[t], zpeer(1))

    def f1_start(t):
        for k in (1, 3, 2):
            f1_copy(t, k).start()

    def f1_wait(t):
        f1_all(t).wait_recv()

    def f2_copy(t, k):
        return rc(FAR2[t].at[c, g], FAR2[t].at[c, g], f2s.at[t], f2r.at[t], gpeer(k))

    def f2_all(t):
        some = FAR2[t].at[c, pl.ds(0, 15)]
        return rc(some, some, f2s.at[t], f2r.at[t], gpeer(1))

    def f2_start(t):
        a = FAR1[t]
        FAR2[t][c, g] = (
            a[0].astype(F32) + a[1].astype(F32) + a[2].astype(F32) + a[3].astype(F32)
        ).astype(a.dtype)
        for k in range(1, 16):
            f2_copy(t, k).start()

    def f2_wait(t):
        f2_all(t).wait_recv()

    def f3_copy(t):
        return rc(FAR2[t].at[c], FAR2[t].at[c], f3s.at[t], f3r.at[t], mate)

    def f3_wait(t):
        rc(FAR2[t].at[1 - c], FAR2[t].at[1 - c], f3s.at[t], f3r.at[t], mate).wait_recv()

    def m1_copy(t, k):
        return rc(MID[t].at[c, z], MID[t].at[c, z], m1s.at[t], m1r.at[t], zpeer(k))

    def m1_all(t):
        some = MID[t].at[c, pl.ds(0, 3)]
        return rc(some, some, m1s.at[t], m1r.at[t], zpeer(1))

    def m2_copy(t, k):
        o = (z + k) % 4
        return rc(MID[t].at[c, o], MID[t].at[c, o], m2s.at[t], m2r.at[t], mate)

    def m2_all(t, who):
        return rc(MID[t].at[who], MID[t].at[who], m2s.at[t], m2r.at[t], mate)

    def m1_start(t):
        for k in (1, 3, 2):
            m1_copy(t, k).start()
        m2_copy(t, 0).start()

    def m1_forward(t):
        m1_all(t).wait_recv()
        for k in (1, 3, 2):
            m2_copy(t, k).start()

    def m2_wait(t):
        m2_all(t, 1 - c).wait_recv()

    def to_mate(t, src, dst):
        return rc(src, dst, xs.at[t], xr.at[t], mate)

    half_cols = pl.ds(pl.multiple_of(384 * (1 - c), 128), 384)
    own_cols = pl.ds(pl.multiple_of(384 * c, 128), 384)

    for item in small:
        item.wait()
    limit = N * 128 - pad[0]
    lane_head = iota((1, D), 1) // E
    o0 = jnp.zeros((1, D), I32)
    o1 = jnp.zeros((1, D), I32)
    for h in range(H):
        o0 = jnp.where(lane_head == h, offs[0, h], o0)
        o1 = jnp.where(lane_head == h, offs[1, h], o1)
    midm[...] = jnp.where(iota((N, D), 0) % 8 == o0, 1.0, 0.0).astype(BF)
    farm[...] = jnp.where(iota((N, D), 0) % 128 == o1, 1.0, 0.0).astype(BF)

    nfar[...] = jnp.where(iota((N, D), 0) % 128 == o1, 0.0, 1.0).astype(BF)
    r0 = iota((D, 128), 0)
    l0 = iota((D, 128), 1)
    sel1[...] = jnp.where(jnp.logical_and(r0 == l0 * E, l0 < H), 1.0, 0.0).astype(BF)
    sel2[...] = jnp.where(r0 // E == l0 - H, 1.0, 0.0).astype(BF)
    hsel[...] = jnp.where(iota((16, D), 1) // E == iota((16, D), 0), 1.0, 0.0)
    pool_mid = jnp.where(iota((32, N), 1) // 8 == iota((32, N), 0), 1.0, 0.0).astype(BF)
    two = iota((16, N), 1) // 128
    row = iota((16, N), 0)
    pool_far = jnp.where(row == two, 1.0, 0.0).astype(BF)
    place = jnp.concatenate(
        [
            jnp.where(row == 2 * z + two, 1.0, 0.0),
            jnp.where(row == 8 + 2 * z + two, 1.0, 0.0),
        ],
        axis=1,
    ).astype(BF)

    def picks(t, i, a, b):
        ls = pl.ds(pl.multiple_of(i * N, N), N)
        hi = pl.ds(pl.multiple_of(D + i * N, N), N)
        mk = midm[:, ls]
        fk = farm[:, ls]
        fa = a * fk
        fb = b * fk
        FAR1[t][z, :, ls] = nn(place, jnp.concatenate([fa, fb], axis=0)).astype(BF)
        MID[t][c, z, :, ls] = nn(pool_mid, a * mk).astype(BF)
        MID[t][c, z, :, hi] = nn(pool_mid, b * mk).astype(BF)
        floc[2 * t, :, ls] = nn(pool_far, fa).astype(BF)
        floc[2 * t + 1, :, ls] = nn(pool_far, fb).astype(BF)

    loads[0].wait()

    for i in range(3):
        cols = pl.ds(i * 2 * N, 2 * N)
        load(wqkv_h.at[:, cols], wqkv.at[:, cols], 1 + i).wait()
        if i == 2:
            for item in later:
                item.start()
        kc = pl.ds(D + i * N, N)
        vc = pl.ds(2 * D + i * N, N)
        kk = nn(tiles[...], wqkv[:, kc]).astype(BF)
        vv = nn(tiles[...], wqkv[:, vc]).astype(BF)
        pk[:, kc] = kk
        pk[:, vc] = vv
        picks(0, i, kk, vv)

    pl.semaphore_wait(barrier, len(peers))
    f1_start(0)
    for item in later:
        item.wait()
    to_mate(0, cot.at[:, half_cols], cotr).start()

    for i in range(3):
        if i == 1:
            m1_start(0)
        qc = pl.ds(i * N, N)
        dc = pl.ds(3 * D + i * N, N)
        qq = nn(tiles[...], wqkv[:, qc]).astype(BF) * jnp.asarray(0.125, BF)
        dd = nt(cot[...], wout[qc, :]).astype(BF)
        pk[:, qc] = qq
        pk[:, dc] = dd
        picks(1, i, qq, dd)


    half = iota((1, 128), 1) // E
    hm = [jnp.where(half == a, 1.0, 0.0).astype(BF) for a in range(2)]

    def lanes(p, base=0):
        return pl.ds(pl.multiple_of(base + p * 128, 128), 128)

    def near_forward(lo, hi):
        @pl.loop(lo, hi)
        def _(p):
            q2 = pk[:, lanes(p)]
            k2 = pk[:, lanes(p, D)]
            v2 = pk[:, lanes(p, 2 * D)]
            bias = jnp.where(me * N + iota((1, N), 1) < limit, 0.0, NEG)
            es, ms = [], []
            for a in range(2):
                s = nt(q2 * hm[a], k2) + bias
                m = jnp.max(s, axis=1, keepdims=True)
                e = jnp.exp(s - m).astype(BF)
                emat[2 * p + a] = e
                es.append(e)
                ms.append(m)
            rhs = jnp.concatenate(
                [
                    jnp.concatenate([v2 * hm[a], jnp.broadcast_to(hm[a], (N, 128))], axis=1)
                    for a in range(2)
                ],
                axis=0,
            )
            nd = nn(jnp.concatenate(es, axis=1), rhs)
            num[:, lanes(p)] = nd[:, :128]
            den[:, lanes(p)] = nd[:, 128:]
            mx[:, lanes(p)] = jnp.where(iota((N, 128), 1) < E, ms[0], ms[1])

    f1_wait(0)
    f2_start(0)
    near_forward(0, 6)
    tilest[c] = tiles[...].T
    m1_forward(0)
    f1_start(1)
    m1_start(1)
    to_mate(1, tilest.at[c], tilest.at[c]).start()
    pr = iota((D, D), 0)
    want = pr // 12 % 16 * 48 + pr // 192 * 12 + pr % 12
    perm[...] = jnp.where(iota((D, D), 1) == want, 1.0, 0.0).astype(BF)
    tilesp[c] = nt(perm[...], tiles[...]).astype(BF)
    to_mate(6, tilesp.at[c], tilesp.at[c]).start()

    m2_wait(0)
    kg = gkv[:, :, :, :D].reshape(N, D)
    vg = gkv[:, :, :, D:].reshape(N, D)
    gdev = g * 8 + iota((32, N), 1) // 32 % 4 * 2 + iota((32, N), 1) // 128
    gpos = gdev * N + iota((32, N), 1) % 32 * 8
    gbias = jnp.concatenate(
        [jnp.where(gpos + offs[0, h] < limit, 0.0, NEG) for h in range(H)], axis=0
    )
    s = nt(block_diag(gqd[c, z, :, :D]), kg) + gbias
    m = jnp.max(s, axis=1, keepdims=True)
    e = jnp.exp(s - m)
    total = jnp.sum(e, axis=1, keepdims=True)
    e = e.astype(BF)
    emid[...] = e
    mnum[...] = diag_sum(nn(e, vg), 32)
    mden[...] = per_head(total, 32)
    mmax[...] = per_head(m, 32)

    f2_wait(0)
    f3_copy(0).start()

    def spread_mid(x):
        return jnp.broadcast_to(x[:, None, :], (32, 8, 128)).reshape(N, 128)

    def spread_far(x):
        return jnp.concatenate(
            [jnp.broadcast_to(x[0:1], (128, 128)), jnp.broadcast_to(x[1:2], (128, 128))], axis=0
        )

    def pick_mid(x):
        return jnp.sum(x.reshape(32, 8, 128), axis=1)

    def pick_far(x):
        return jnp.concatenate(
            [
                jnp.sum(x[:128], axis=0, keepdims=True),
                jnp.sum(x[128:], axis=0, keepdims=True),
            ],
            axis=0,
        )

    @pl.loop(0, 6)
    def _(p):
        ls = lanes(p)
        mm = midm[:, ls].astype(F32)
        fm = farm[:, ls].astype(F32)
        m0 = mx[:, ls]
        m1 = jnp.where(mm > 0.5, spread_mid(mmax[:, ls]), NEG)
        top = jnp.maximum(m0, m1)
        w0 = jnp.exp(m0 - top)
        w1 = jnp.exp(m1 - top)
        total = w0 * den[:, ls] + w1 * spread_mid(mden[:, ls])
        inv = 1.0 / total
        exact = (w0 * num[:, ls] + w1 * spread_mid(mnum[:, ls])) * inv
        at = exact.astype(BF)
        attn[:, ls] = at
        do = pk[:, lanes(p, 3 * D)].astype(F32)
        prod = do * at.astype(F32)
        scale = w0 * inv
        sdo[:, ls] = (scale * do).astype(BF)
        npr[:, ls] = (-scale * prod).astype(BF)
        lse = top + jnp.log(total)
        mlse[:, ls] = pick_mid(lse * mm)
        mprod[:, ls] = pick_mid(prod * mm)
        flse[0:2, ls] = pick_far(lse * fm)
        fat[0:2, ls] = pick_far(exact * fm)
        fsc[0:2, ls] = pick_far(scale * fm)

    f3_wait(0)
    f1_wait(1)
    f2_start(1)

    heads = hsel[...]
    headb = heads.astype(BF)

    def far_diag(v):
        return jnp.concatenate([v[0:1] * headb, v[1:2] * headb], axis=0)

    def far_fold(v):
        return jnp.concatenate(
            [jnp.sum(v[16 * r : 16 * r + 16] * heads, axis=0, keepdims=True) for r in range(2)],
            axis=0,
        )

    col = iota((16, 512), 1)
    fdev = col // 16 % 16 * 8 + col // 2 % 4 * 2 + col // 256
    fpos = (fdev * 2 + col % 2) * 128
    lead = col // 8 % 2 == 0
    off_col = jnp.zeros((16, 512), I32)
    for h in range(H):
        off_col = jnp.where(iota((16, 512), 0) == h, offs[1, h], off_col)
    fbias = jnp.where(jnp.logical_and(lead, fpos + off_col < limit), 0.0, NEG)
    fbias = jnp.concatenate([fbias, fbias], axis=0)
    kvf = far2kv[...].reshape(512, D)
    s = nt(far_diag(floc[2]), kvf) + fbias
    m = jnp.max(s, axis=1, keepdims=True)
    e = jnp.exp(s - m)
    efar[...] = e
    fnum[0:2] = far_fold(nn(pltpu.roll(e, 8, 1).astype(BF), kvf))
    fden[0:2] = far_fold(jnp.broadcast_to(jnp.sum(e, axis=1, keepdims=True), (32, D)))
    fmax[0:2] = far_fold(jnp.broadcast_to(m, (32, D)))

    a_lse = flse[0:2]
    b_lse = fmax[0:2] + jnp.log(fden[0:2])
    top = jnp.maximum(a_lse, b_lse)
    n_lse = top + jnp.log(jnp.exp(a_lse - top) + jnp.exp(b_lse - top))
    wa = jnp.exp(a_lse - n_lse)
    n_at = (wa * fat[0:2] + jnp.exp(b_lse - n_lse) * fnum[0:2] / fden[0:2]).astype(BF)
    f_do = floc[3, 0:2].astype(F32)
    n_prod = f_do * n_at.astype(F32)
    scale = fsc[0:2] * wa
    n_sdo = scale * f_do
    n_npr = -scale * n_prod
    flse[...] = jnp.concatenate([n_lse, jnp.zeros((14, D), F32)], axis=0)
    fprod[...] = jnp.concatenate([n_prod, jnp.zeros((14, D), F32)], axis=0)
    for p in range(6):
        ls = slice(p * 128, p * 128 + 128)
        keep = nfar[:, ls]
        take = farm[:, ls]
        for ref, new in ((attn, n_at.astype(F32)), (sdo, n_sdo), (npr, n_npr)):
            ref[:, ls] = ref[:, ls] * keep + spread_far(new[:, ls]).astype(BF) * take
    g32 = iota((32, D), 0)
    for r in range(2):
        both = jnp.logical_and(g32 == r * 16 + o1 // 8, o1 % 8 == o0)
        mlse[...] = jnp.where(both, n_lse[r : r + 1], mlse[...])
        mprod[...] = jnp.where(both, n_prod[r : r + 1], mprod[...])

    lse_rows = jnp.concatenate([mlse[...], flse[...]], axis=0)
    prod_rows = jnp.concatenate([mprod[...], fprod[...]], axis=0)
    l_hi = lse_rows.astype(BF)
    left = lse_rows - l_hi.astype(F32)
    l_mid = left.astype(BF)
    l_lo = (left - l_mid.astype(F32)).astype(BF)
    p_hi = prod_rows.astype(BF)
    p_lo = (prod_rows - p_hi.astype(F32)).astype(BF)
    lt = nn(jnp.concatenate([l_hi, l_mid, l_lo], axis=0), sel1[...])
    pt = nn(jnp.concatenate([p_hi, p_lo], axis=0), sel2[...])
    st = lt[0:48] + lt[48:96] + lt[96:144] + pt[0:48] + pt[48:96]
    gst[c, z] = st[0:32]
    fs = st[32:48]
    r8 = iota((8, 128), 0)
    far1st[z] = jnp.where(r8 == 2 * z, fs[0:1], jnp.where(r8 == 2 * z + 1, fs[1:2], 0.0))
    f1_start(2)
    m1_start(2)

    attnt[c] = nt(perm[...], attn[...]).astype(BF)
    to_mate(2, attnt.at[c], attnt.at[c]).start()
    out_copy = pltpu.make_async_copy(out_rows, rows_h, os_.at[0])
    til_copy = pltpu.make_async_copy(grad_tiles, gtil_h, os_.at[1])

    def put_part(b, v):
        part[b] = v.astype(BF).reshape(4, 4, 48, 384)

    def dev(x_, y_):
        return ((x_ % 4 * 4 + y_ % 4) * 4 + z) * 2 + c

    pos = (x, y)
    step = (lambda k: dev(x + k, y), lambda k: dev(x, y + k))

    def where_in(b, q, h):
        some = slice(None) if h is None else pl.ds(2 * h, 2)
        return (b, q, some) if b % 2 == 0 else (b, some, q)

    def ring_copy(b, n):
        p = pos[b % 2]
        nxt, prv = step[b % 2](1), step[b % 2](3)
        up, down, far = (p + 1) % 4, (p + 3) % 4, (p + 2) % 4
        src, dst, to = (
            lambda: (part.at[where_in(b, far, 0)], r1.at[b, 0], nxt),
            lambda: (part.at[where_in(b, far, 1)], r1.at[b, 1], prv),
            lambda: (part.at[where_in(b, up, 1)], r2.at[b, 0, pl.ds(2, 2)], nxt),
            lambda: (part.at[where_in(b, down, 0)], r2.at[b, 1, pl.ds(0, 2)], prv),
            lambda: (tmp.at[b, 0], r2.at[b, 0, pl.ds(0, 2)], nxt),
            lambda: (tmp.at[b, 1], r2.at[b, 1, pl.ds(2, 2)], prv),
        )[n]()
        return rc(src, dst, rs.at[b], rr_.at[b, min(n, 2)], to)

    def ring_a(b):
        for n in range(4):
            ring_copy(b, n).start()

    def ring_b(b):
        p = pos[b % 2]
        for h, q in ((0, (p + 1) % 4), (1, (p + 3) % 4)):
            ring_copy(b, h).wait_recv()
            tmp[b, h] = (part[where_in(b, q, h)].astype(F32) + r1[b, h].astype(F32)).astype(BF)
            ring_copy(b, 4 + h).start()

    def second(b, k):
        j = (b + 1) % 2
        q = (pos[j] + k) % 4
        return rc(acc.at[b, q], s2.at[b, pos[j]], ss.at[b], sr.at[b], step[j](k))

    def second_all(b):
        some = s2.at[b, pl.ds(0, 3)]
        return rc(some, some, ss.at[b], sr.at[b], mate)

    def ring_c(b):
        rc(r2.at[b], r2.at[b], rs.at[b], rr_.at[b, 2], mate).wait_recv()
        mine = part[where_in(b, pos[b % 2], None)].astype(F32)
        acc[b] = (mine + r2[b, 0].astype(F32) + r2[b, 1].astype(F32)).astype(BF)
        for k in (2, 1, 3):
            second(b, k).start()

    def ring_d(b):
        j = (b + 1) % 2
        total = acc[b, pos[j]].astype(F32)
        second_all(b).wait_recv()
        for k in (1, 3, 2):
            total = total + s2[b, (pos[j] + k) % 4].astype(F32)
        tot[b] = total.astype(BF)

    own = z * 2 + c
    er = iota((128, 96), 0)
    ek = er % 8
    spread = jnp.where(
        jnp.logical_and(iota((128, 96), 1) == er // 8 % 2 * 48 + er // 16 * 6 + ek, ek < 6), 1.0, 0.0
    ).astype(BF)

    def fin_copy(k):
        o = (own + k) % 8
        return rc(fin.at[o], finr.at[own], es_.at[0], er_.at[0], g * 8 + o)

    def fin_all():
        some = finr.at[pl.ds(0, 7)]
        return rc(some, some, es_.at[0], er_.at[0], mate)

    def fin_start(_):
        fin[...] = nn(spread, tot[...].reshape(96, 384)).astype(BF).reshape(8, 16, 384)
        for k in range(1, 8):
            fin_copy(k).start()
        finr[own] = fin[own]

    def fin_end(_):
        fin_all().wait_recv()
        for a in range(2):
            v = finr[a].astype(F32)
            for o in (2, 4, 6):
                v = v + finr[o + a].astype(F32)
            for i in range(2):
                at = (1 + i) * D + 384 * a
                g_qkv[:, at : at + 384] = v[8 * i : 8 * i + 6]

    def put_z(b, v):
        pz[b] = v.astype(BF).reshape(4, 4, 48, 384)

    def z_copy(b, n):
        nxt, prv = zpeer(1), zpeer(3)
        up, down, far = (z + 1) % 4, (z + 3) % 4, (z + 2) % 4
        lo, hi = pl.ds(0, 2), pl.ds(2, 2)
        src, dst, to = (
            lambda: (pz.at[b, far, lo], z1.at[b, 0], nxt),
            lambda: (pz.at[b, far, hi], z1.at[b, 1], prv),
            lambda: (pz.at[b, up, hi], z2.at[b, 0, hi], nxt),
            lambda: (pz.at[b, down, lo], z2.at[b, 1, lo], prv),
            lambda: (zt.at[b, 0], z2.at[b, 0, lo], nxt),
            lambda: (zt.at[b, 1], z2.at[b, 1, hi], prv),
        )[n]()
        return rc(src, dst, zrs.at[b], zrr.at[b, min(n, 2)], to)

    def z_a(b):
        for n in range(4):
            z_copy(b, n).start()

    def z_b(b):
        for h, q in ((0, (z + 1) % 4), (1, (z + 3) % 4)):
            z_copy(b, h).wait_recv()
            mine = pz[b, q, 2 * h : 2 * h + 2].astype(F32)
            zt[b, h] = (mine + z1[b, h].astype(F32)).astype(BF)
            z_copy(b, 4 + h).start()

    def z_second(b, k):
        return rc(zacc.at[b, (g + k) % 16], zs.at[b, g], zss.at[b], zsr.at[b], gpeer(k))

    def z_second_all(b):
        some = zs.at[b, pl.ds(0, 15)]
        return rc(some, some, zss.at[b], zsr.at[b], mate)

    def z_c(b):
        rc(z2.at[b], z2.at[b], zrs.at[b], zrr.at[b, 2], mate).wait_recv()
        mine = pz[b, z].astype(F32)
        mine = mine + z2[b, 0].astype(F32) + z2[b, 1].astype(F32)
        stage[0:192] = mine.reshape(192, 384)
        for i in range(16):
            zacc[b, i] = stage[12 * i : 12 * i + 16].astype(BF)
        for k in range(1, 16):
            z_second(b, k).start()

    def z_mate(b):
        return rc(zf.at[b], zm.at[b], zms.at[b], zmr.at[b], mate)

    def z_d(b):
        z_second_all(b).wait_recv()
        total = zacc[b, g].astype(F32)
        for k in range(1, 16):
            total = total + zs[b, (g + k) % 16].astype(F32)
        zf[b] = total
        z_mate(b).start()

    def z_e(b):
        z_mate(b).wait_recv()
        target = (g_out, g_qkv)[b]
        for ref, half in ((zf, c), (zm, 1 - c)):
            v = ref[b]
            cols = pl.ds(pl.multiple_of(384 * half, 128), 384)
            target[:, cols] = jnp.where(c == 0, v[0:6], v[6:12])

    def backward_queries(lo, hi):
        @pl.loop(lo, hi)
        def _(p):
            ls = lanes(p)
            k2 = pk[:, lanes(p, D)]
            so = sdo[:, ls]
            sp = npr[:, ls]
            rhs = jnp.concatenate([pk[:, lanes(p, 2 * D)], jnp.ones((N, 128), BF)], axis=1)
            ds = []
            for a in range(2):
                lhs = jnp.concatenate([so * hm[a], sp * hm[a]], axis=1)
                d = (emat[2 * p + a].astype(F32) * nt(lhs, rhs)).astype(BF)
                dsm[2 * p + a] = d
                ds.append(d)
            dq[:, ls] = 0.125 * nn(
                jnp.concatenate(ds, axis=1), jnp.concatenate([k2 * hm[0], k2 * hm[1]], axis=0)
            )

    def backward_keys(lo, hi):
        @pl.loop(lo, hi)
        def _(p):
            ls = lanes(p)
            q2 = pk[:, ls]
            so = sdo[:, ls]
            dk[:, ls] = tn(
                jnp.concatenate([dsm[2 * p], dsm[2 * p + 1]], axis=0),
                jnp.concatenate([q2 * hm[0], q2 * hm[1]], axis=0),
            )
            dv[:, ls] = tn(
                jnp.concatenate([emat[2 * p], emat[2 * p + 1]], axis=0),
                jnp.concatenate([so * hm[0], so * hm[1]], axis=0),
            )

    backward_queries(0, 2)
    to_mate(0, cotr, cotr).wait_recv()
    to_mate(2, attnt.at[1 - c], attnt.at[1 - c]).wait_recv()
    put_z(0, nn(attnt[c], cot[:, own_cols]) + nn(attnt[1 - c], cotr[...]))
    z_a(0)
    m1_forward(1)
    backward_queries(2, 4)
    f1_wait(2)
    f2_start(2)
    m1_forward(2)
    backward_queries(4, 6)

    kg = gkv[:, :, :, :D].reshape(N, D)
    vg = gkv[:, :, :, D:].reshape(N, D)
    scale = jnp.exp(mmax[...] - mlse[...])
    so = (scale * gqd[c, z, :, D:].astype(F32)).astype(BF)
    sp = scale * mprod[...]
    dl = jnp.concatenate(
        [jnp.sum(sp * head_mask(h, F32), axis=1, keepdims=True) for h in range(H)], axis=0
    )
    ds = (emid[...].astype(F32) * (nt(block_diag(so), vg) - dl)).astype(BF)
    dmid[0] = 0.125 * diag_sum(nn(ds, kg), 32)

    scale = jnp.exp(fmax[0:2] - flse[0:2])
    so = (scale * floc[3, 0:2].astype(F32)).astype(BF)
    sp = scale * fprod[0:2]
    dl = jnp.concatenate(
        [jnp.sum(sp[r : r + 1] * heads, axis=1, keepdims=True) for r in range(2)], axis=0
    )
    kvf = far2kv[...].reshape(512, D)
    t = pltpu.roll(nt(far_diag(so), kvf), 504, 1)
    dfar[0, 0:2] = 0.125 * far_fold(nn((efar[...] * (t - dl)).astype(BF), kvf))

    def grad_part(a, near):
        @pl.loop(0, 6)
        def _(p):
            ls = lanes(p)
            mm = midm[:, ls].astype(F32)
            fm = farm[:, ls].astype(F32)
            v = near[:, ls] + mm * spread_mid(dmid[a, :, ls]) + fm * spread_far(dfar[a, 0:2, ls])
            v = v.astype(BF)
            gp[:, lanes(p, a * D)] = v
            gph[a, p // 3, :, lanes(p % 3)] = v

        to_mate(3 + a, gph.at[a, 1 - c], gpr.at[a]).start()

    def weight_part(a):
        to_mate(3 + a, gpr.at[a], gpr.at[a]).wait_recv()
        rows = tilest if a else tilesp
        v = nn(rows[c], gph[a, c]) + nn(rows[1 - c], gpr[a])
        if a == 0:
            put_z(1, v)
        else:
            put_part(a - 1, v)
            ring_a(a - 1)

    grad_part(0, dq)
    backward_keys(0, 4)
    f2_wait(1)
    f3_copy(1).start()
    to_mate(1, tilest.at[1 - c], tilest.at[1 - c]).wait_recv()
    to_mate(6, tilesp.at[1 - c], tilesp.at[1 - c]).wait_recv()
    z_b(0)
    weight_part(0)
    backward_keys(4, 6)
    f2_wait(2)
    f3_copy(2).start()
    m2_wait(1)
    m2_wait(2)

    st = gst[...].reshape(N, 128).T
    ls_rows = st[0:16]
    dl_rows = st[12:28]
    qg = gqd[:, :, :, :D].reshape(N, D)
    og = gqd[:, :, :, D:].reshape(N, D)
    s = nt(block_diag(gkv[c, z, :, :D]), qg)
    t = nt(block_diag(gkv[c, z, :, D:]), og)
    ps, dss = [], []
    for h in range(H):
        ok = me * N + iota((32, N), 0) * 8 + offs[0, h] < limit
        p = jnp.exp(jnp.where(ok, s[h * 32 : (h + 1) * 32] - ls_rows[h : h + 1], NEG))
        ps.append(p.astype(BF))
        dss.append((p * (t[h * 32 : (h + 1) * 32] - dl_rows[h : h + 1])).astype(BF))
    dmid[1] = diag_sum(nn(jnp.concatenate(dss, axis=0), qg), 32)
    pmid = jnp.concatenate(ps, axis=0)

    f3_wait(1)
    f3_wait(2)
    st = far2st[...].reshape(32, 8, 128)
    st = jnp.concatenate([st, jnp.zeros_like(st)], axis=1).reshape(512, 128).T
    ls_rows = jnp.concatenate([st[0:16], st[0:16]], axis=0)
    dl_rows = jnp.concatenate([st[12:28], st[12:28]], axis=0)
    qdf = far2qd[...].reshape(512, D)
    s = nt(far_diag(floc[0]), qdf)
    t = pltpu.roll(nt(far_diag(floc[1]), qdf), 504, 1)
    row_h = iota((16, 512), 0)
    oks = [
        jnp.logical_and(
            jnp.logical_and(lead, row_h < H), (me * 2 + r) * 128 + off_col < limit
        )
        for r in range(2)
    ]
    expo = jnp.concatenate(
        [jnp.where(oks[r], (s - ls_rows)[16 * r : 16 * r + 16], NEG) for r in range(2)], axis=0
    )
    pfar = jnp.exp(expo)
    dfar[1, 0:2] = far_fold(nn((pfar * (t - dl_rows)).astype(BF), qdf))
    grad_part(1, dk)
    z_c(0)
    z_a(1)
    dmid[2] = diag_sum(nn(pmid, og), 32)
    dfar[2, 0:2] = far_fold(nn(pltpu.roll(pfar, 8, 1).astype(BF), qdf))
    grad_part(2, dv)
    weight_part(1)
    weight_part(2)

    @pl.loop(0, 3)
    def _(i):
        ls = pl.ds(pl.multiple_of(i * N, N), N)
        out_rows[:, ls] = (tiles[:, ls].astype(F32) + nn(attn[...], wout[:, ls])).astype(BF)
        grad_tiles[:, ls] = nt(gp[...], wqkv[ls, :]).astype(BF)

    z_b(1)
    ring_b(0)
    ring_b(1)
    out_copy.start()
    til_copy.start()
    ring_c(0)
    ring_c(1)
    z_c(1)
    z_d(0)
    ring_d(0)
    ring_d(1)
    fin_start(1)
    z_d(1)
    z_e(0)
    z_e(1)
    fin_end(1)

    to_mate(0, cot.at[:, half_cols], cotr).wait_send()
    to_mate(1, tilest.at[c], tilest.at[c]).wait_send()
    to_mate(6, tilesp.at[c], tilesp.at[c]).wait_send()
    to_mate(2, attnt.at[c], attnt.at[c]).wait_send()
    for a in range(3):
        to_mate(3 + a, gph.at[a, 1 - c], gpr.at[a]).wait_send()
    for b in range(2):
        some = part.at[b, pl.ds(0, 3)]
        rc(some, some, rs.at[b], rr_.at[b, 2], mate).wait_send()
        second_all(b).wait_send()
        some = pz.at[b, pl.ds(0, 3)]
        rc(some, some, zrs.at[b], zrr.at[b, 2], mate).wait_send()
        z_second_all(b).wait_send()
        z_mate(b).wait_send()
    fin_all().wait_send()
    out_copy.wait()
    til_copy.wait()
    for t in range(3):
        f1_all(t).wait_send()
        m1_all(t).wait_send()
        f2_all(t).wait_send()
        f3_copy(t).wait_send()
        m2_all(t, c).wait_send()


def copy_kernel(*refs):
    for src, dst in zip(refs[:4], refs[4:]):
        dst[...] = src[...]


def per_device(tiles, w_qkv, w_out, cotangent, offsets, pad_count):
    vm = pl.BlockSpec(memory_space=pltpu.VMEM)
    hbm = pl.BlockSpec(memory_space=pl.ANY)
    V = pltpu.VMEM
    dma = pltpu.SemaphoreType.DMA
    big = V((N, D), F32)
    bigb = V((N, D), BF)
    m32 = V((32, D), F32)
    f16 = V((16, D), F32)
    shapes = (
        jax.ShapeDtypeStruct((N, D), BF),
        jax.ShapeDtypeStruct((N, D), BF),
        jax.ShapeDtypeStruct((6, 3 * D), F32),
        jax.ShapeDtypeStruct((6, D), F32),
    )
    outs = pl.pallas_call(
        kernel,
        out_shape=shapes,
        in_specs=[hbm] * 6,
        out_specs=(hbm, hbm, vm, vm),
        scratch_shapes=[
            pltpu.SMEM((2, H), I32), pltpu.SMEM((1,), I32),
            bigb, V((D, 3 * D), BF), V((D, D), BF), bigb, bigb, bigb,
            V((N, 4 * D), BF), bigb, bigb, bigb, V((D, 128), BF), V((D, 128), BF), f16,
            V((H, N, N), BF), V((H, N, N), BF), big, big, big,
            V((2, 4, 32, 2 * D), BF), V((2, 4, 32, 2 * D), BF), V((2, 4, 32, 128), F32),
            V((4, 16, D), BF), V((4, 16, D), BF), V((4, 8, 128), F32),
            V((2, 16, 16, D), BF), V((2, 16, 16, D), BF), V((2, 16, 8, 128), F32),
            V((4, 16, D), BF), m32, m32, m32, f16, f16, f16, V((H * 32, N), BF), V((32, 512), F32),
            bigb, bigb, bigb, m32, m32, f16, f16, f16, f16,
            big, big, big, V((3, 32, D), F32), V((3, 16, D), F32), V((N, 3 * D), BF),
            V((2, D, N), BF), V((2, D, N), BF), V((2, D, N), BF), V((N, 384), BF), V((D, D), BF),
            V((3, 2, N, 384), BF), V((3, N, 384), BF),
            V((2, 4, 4, 48, 384), BF),
            V((2, 2, 2, 48, 384), BF), V((2, 2, 2, 48, 384), BF), V((2, 2, 4, 48, 384), BF),
            V((2, 4, 48, 384), BF), V((2, 4, 48, 384), BF), V((2, 48, 384), BF),
            V((8, 16, 384), BF), V((8, 16, 384), BF),
            V((208, 384), F32), V((2, 4, 4, 48, 384), BF),
            V((2, 2, 2, 48, 384), BF), V((2, 2, 2, 48, 384), BF), V((2, 2, 4, 48, 384), BF),
            V((2, 16, 16, 384), BF), V((2, 16, 16, 384), BF), V((2, 16, 384), F32), V((2, 16, 384), F32),
            dma((9,)), dma((2,)),
            dma((3,)), dma((3,)), dma((3,)), dma((3,)), dma((3,)), dma((3,)),
            dma((3,)), dma((3,)), dma((3,)), dma((3,)),
            dma((7,)), dma((7,)), dma((2,)), dma((2, 3)), dma((2,)), dma((2,)),
            dma((1,)), dma((1,)),
            dma((2,)), dma((2, 3)), dma((2,)), dma((2,)), dma((2,)), dma((2,)),
        ],
        compiler_params=pltpu.CompilerParams(
            collective_id=0, has_side_effects=True, vmem_limit_bytes=64 * 1024 * 1024 - 65536
        ),
        name="layer",
    )(offsets, pad_count, tiles, w_qkv, w_out, cotangent)
    return pl.pallas_call(
        copy_kernel, out_shape=shapes, in_specs=[vm] * 4, out_specs=(vm,) * 4, name="results"
    )(*outs)


def solution(mesh):
    row = P("ctx", None)
    return jax.shard_map(
        per_device,
        mesh=mesh,
        in_specs=(row, P(), P(), row, P(), P()),
        out_specs=(row, row, row, row),
        check_vma=False,
    )
```

```python
import jax
import jax.numpy as jnp
from jax import lax
from jax.experimental import pallas as pl
from jax.experimental.pallas import tpu as pltpu
from jax.sharding import PartitionSpec as P

MESH = pl.DeviceIdType.MESH
N = 256
D = 768
H = 12
E = 64
NEG = -1e30
F32 = jnp.float32
BF = jnp.bfloat16
I32 = jnp.int32


def dot(a, b, ca, cb, precision=None):
    dims = (((ca,), (cb,)), ((), ()))
    return lax.dot_general(a, b, dims, precision=precision, preferred_element_type=F32)


def nn(a, b):
    return dot(a, b, 1, 0)


def nt(a, b):
    return dot(a, b, 1, 1)


def tn(a, b):
    return dot(a, b, 0, 0)


def iota(shape, dim):
    return lax.broadcasted_iota(I32, shape, dim)


def head_mask(h, dtype):
    return jnp.where(iota((1, D), 1) // E == h, 1.0, 0.0).astype(dtype)


def block_diag(x):
    return jnp.concatenate([x * head_mask(h, x.dtype) for h in range(H)], axis=0)


def diag_sum(x, rows):
    head = iota((rows, D), 1) // E
    out = jnp.zeros((rows, D), F32)
    for h in range(H):
        out = jnp.where(head == h, x[h * rows : (h + 1) * rows], out)
    return out


def per_head(cols, rows):
    head = iota((rows, D), 1) // E
    out = jnp.zeros((rows, D), F32)
    for h in range(H):
        out = jnp.where(head == h, cols[h * rows : (h + 1) * rows], out)
    return out


def kernel(
    offs_h, pad_h, tiles_h, wqkv_h, wout_h, cot_h,
    out_rows, grad_tiles, g_qkv, g_out,
    offs, pad, tiles, wqkv, wout, cot,
    pk, midm, farm, nfar, sel1, sel2, hsel, emat, dsm, num, den, mx,
    gkv, gqd, gst, far1kv, far1qd, far1st, far2kv, far2qd, far2st,
    floc, mnum, mden, mmax, fnum, fden, fmax, emid, efar,
    attn, sdo, npr, mlse, mprod, flse, fprod, fat, fsc,
    dq, dk, dv, dmid, dfar, gp, tilest, tilesp, attnt, cotr, perm, gph, gpr,
    part, r1, tmp, r2, acc, s2, tot, fin, finr,
    stage, pz, z1, zt, z2, zacc, zs, zf, zm,
    ls_, os_, f1s, f1r, f2s, f2r, f3s, f3r, m1s, m1r, m2s, m2r,
    xs, xr, rs, rr_, ss, sr, es_, er_,
    zrs, zrr, zss, zsr, zms, zmr,
):
    me = lax.axis_index("ctx")
    c = me % 2
    z = me // 2 % 4
    g = me // 8
    x = g // 4
    y = g % 4
    mate = g * 8 + z * 2 + (1 - c)

    def zpeer(k):
        return g * 8 + (z + k) % 4 * 2 + c

    def gpeer(k):
        return (g + k) % 16 * 8 + z * 2 + c

    def rc(src, dst, ss, rs, dev):
        return pltpu.make_async_remote_copy(
            src_ref=src, dst_ref=dst, send_sem=ss, recv_sem=rs, device_id=(dev,), device_id_type=MESH
        )

    def load(src, dst, n):
        return pltpu.make_async_copy(src, dst, ls_.at[n])

    loads = [load(tiles_h, tiles, 0)]
    for i in range(3):
        for a in (1, 2):
            cols = pl.ds(a * D + i * N, N)
            loads.append(load(wqkv_h.at[:, cols], wqkv.at[:, cols], 1 + i))
    later = [
        load(wqkv_h.at[:, pl.ds(0, D)], wqkv.at[:, pl.ds(0, D)], 4),
        load(cot_h, cot, 5),
        load(wout_h, wout, 6),
    ]
    small = (load(offs_h, offs, 7), load(pad_h, pad, 8))
    for item in small:
        item.start()
    for item in loads:
        item.start()
    barrier = pltpu.get_barrier_semaphore()
    peers = [mate] + [zpeer(k) for k in (1, 2, 3)] + [gpeer(k) for k in range(1, 16)]
    peers += [g * 8 + (z + k) % 4 * 2 + (1 - c) for k in (1, 2, 3)]
    for p in peers:
        pl.semaphore_signal(barrier, inc=1, device_id=(p,), device_id_type=MESH)

    FAR1 = (far1kv, far1qd, far1st)
    FAR2 = (far2kv, far2qd, far2st)
    MID = (gkv, gqd, gst)

    def f1_copy(t, k):
        return rc(FAR1[t].at[z], FAR1[t].at[z], f1s.at[t], f1r.at[t], zpeer(k))

    def f1_all(t):
        some = FAR1[t].at[pl.ds(0, 3)]
        return rc(some, some, f1s.at[t], f1r.at[t], zpeer(1))

    def f1_start(t):
        for k in (1, 3, 2):
            f1_copy(t, k).start()

    def f1_wait(t):
        f1_all(t).wait_recv()

    def f2_copy(t, k):
        return rc(FAR2[t].at[c, g], FAR2[t].at[c, g], f2s.at[t], f2r.at[t], gpeer(k))

    def f2_all(t):
        some = FAR2[t].at[c, pl.ds(0, 15)]
        return rc(some, some, f2s.at[t], f2r.at[t], gpeer(1))

    def f2_start(t):
        a = FAR1[t]
        FAR2[t][c, g] = (
            a[0].astype(F32) + a[1].astype(F32) + a[2].astype(F32) + a[3].astype(F32)
        ).astype(a.dtype)
        for k in range(1, 16):
            f2_copy(t, k).start()

    def f2_wait(t):
        f2_all(t).wait_recv()

    def f3_copy(t):
        return rc(FAR2[t].at[c], FAR2[t].at[c], f3s.at[t], f3r.at[t], mate)

    def f3_wait(t):
        rc(FAR2[t].at[1 - c], FAR2[t].at[1 - c], f3s.at[t], f3r.at[t], mate).wait_recv()

    def m1_copy(t, k):
        return rc(MID[t].at[c, z], MID[t].at[c, z], m1s.at[t], m1r.at[t], zpeer(k))

    def m1_all(t):
        some = MID[t].at[c, pl.ds(0, 3)]
        return rc(some, some, m1s.at[t], m1r.at[t], zpeer(1))

    def m2_copy(t, k):
        o = (z + k) % 4
        return rc(MID[t].at[c, o], MID[t].at[c, o], m2s.at[t], m2r.at[t], mate)

    def m2_all(t, who):
        return rc(MID[t].at[who], MID[t].at[who], m2s.at[t], m2r.at[t], mate)

    def m1_start(t):
        for k in (1, 3, 2):
            m1_copy(t, k).start()
        m2_copy(t, 0).start()

    def m1_forward(t):
        m1_all(t).wait_recv()
        for k in (1, 3, 2):
            m2_copy(t, k).start()

    def m2_wait(t):
        m2_all(t, 1 - c).wait_recv()

    def to_mate(t, src, dst):
        return rc(src, dst, xs.at[t], xr.at[t], mate)

    half_cols = pl.ds(pl.multiple_of(384 * (1 - c), 128), 384)
    own_cols = pl.ds(pl.multiple_of(384 * c, 128), 384)

    for item in small:
        item.wait()
    limit = N * 128 - pad[0]
    lane_head = iota((1, D), 1) // E
    o0 = jnp.zeros((1, D), I32)
    o1 = jnp.zeros((1, D), I32)
    for h in range(H):
        o0 = jnp.where(lane_head == h, offs[0, h], o0)
        o1 = jnp.where(lane_head == h, offs[1, h], o1)
    midm[...] = jnp.where(iota((N, D), 0) % 8 == o0, 1.0, 0.0).astype(BF)
    farm[...] = jnp.where(iota((N, D), 0) % 128 == o1, 1.0, 0.0).astype(BF)

    nfar[...] = jnp.where(iota((N, D), 0) % 128 == o1, 0.0, 1.0).astype(BF)
    r0 = iota((D, 128), 0)
    l0 = iota((D, 128), 1)
    sel1[...] = jnp.where(jnp.logical_and(r0 == l0 * E, l0 < H), 1.0, 0.0).astype(BF)
    sel2[...] = jnp.where(r0 // E == l0 - H, 1.0, 0.0).astype(BF)
    hsel[...] = jnp.where(iota((16, D), 1) // E == iota((16, D), 0), 1.0, 0.0)
    pool_mid = jnp.where(iota((32, N), 1) // 8 == iota((32, N), 0), 1.0, 0.0).astype(BF)
    two = iota((16, N), 1) // 128
    row = iota((16, N), 0)
    pool_far = jnp.where(row == two, 1.0, 0.0)
    none = jnp.zeros_like(pool_far)
    far_a = [jnp.where(row == 2 * z + two, 1.0, 0.0), pool_far, none]
    far_b = [jnp.where(row == 8 + 2 * z + two, 1.0, 0.0), none, pool_far]
    far_a = jnp.concatenate(far_a, axis=0).astype(BF)
    far_b = jnp.concatenate(far_b, axis=0).astype(BF)

    def picks(t, i, a, b):
        ls = pl.ds(pl.multiple_of(i * N, N), N)
        hi = pl.ds(pl.multiple_of(D + i * N, N), N)
        mk = midm[:, ls]
        fk = farm[:, ls]
        rows = (nn(far_a, a * fk) + nn(far_b, b * fk)).astype(BF)
        FAR1[t][z, :, ls] = rows[0:16]
        MID[t][c, z, :, ls] = nn(pool_mid, a * mk).astype(BF)
        MID[t][c, z, :, hi] = nn(pool_mid, b * mk).astype(BF)
        floc[2 * t, :, ls] = rows[16:32]
        floc[2 * t + 1, :, ls] = rows[32:48]

    loads[0].wait()

    for i in range(3):
        cols = pl.ds(i * 2 * N, 2 * N)
        load(wqkv_h.at[:, cols], wqkv.at[:, cols], 1 + i).wait()
        if i == 0:
            for item in later:
                item.start()
        kc = pl.ds(D + i * N, N)
        vc = pl.ds(2 * D + i * N, N)
        kk = nn(tiles[...], wqkv[:, kc]).astype(BF)
        vv = nn(tiles[...], wqkv[:, vc]).astype(BF)
        pk[:, kc] = kk
        pk[:, vc] = vv
        picks(0, i, kk, vv)

    pl.semaphore_wait(barrier, len(peers))
    f1_start(0)
    for item in later:
        item.wait()
    to_mate(0, cot.at[:, half_cols], cotr).start()

    for i in range(3):
        if i == 1:
            m1_start(0)
        qc = pl.ds(i * N, N)
        dc = pl.ds(3 * D + i * N, N)
        qq = nn(tiles[...], wqkv[:, qc]).astype(BF) * jnp.asarray(0.125, BF)
        dd = nt(cot[...], wout[qc, :]).astype(BF)
        pk[:, qc] = qq
        pk[:, dc] = dd
        picks(1, i, qq, dd)


    half = iota((1, 128), 1) // E
    hm = [jnp.where(half == a, 1.0, 0.0).astype(BF) for a in range(2)]

    def lanes(p, base=0):
        return pl.ds(pl.multiple_of(base + p * 128, 128), 128)

    def near_forward(lo, hi):
        @pl.loop(lo, hi)
        def _(p):
            q2 = pk[:, lanes(p)]
            k2 = pk[:, lanes(p, D)]
            v2 = pk[:, lanes(p, 2 * D)]
            bias = jnp.where(me * N + iota((1, N), 1) < limit, 0.0, NEG)
            es, ms = [], []
            for a in range(2):
                s = nt(q2 * hm[a], k2) + bias
                m = jnp.max(s, axis=1, keepdims=True)
                e = jnp.exp(s - m).astype(BF)
                emat[2 * p + a] = e
                es.append(e)
                ms.append(m)
            rhs = jnp.concatenate(
                [
                    jnp.concatenate([v2 * hm[a], jnp.broadcast_to(hm[a], (N, 128))], axis=1)
                    for a in range(2)
                ],
                axis=0,
            )
            nd = nn(jnp.concatenate(es, axis=1), rhs)
            num[:, lanes(p)] = nd[:, :128]
            den[:, lanes(p)] = nd[:, 128:]
            mx[:, lanes(p)] = jnp.where(iota((N, 128), 1) < E, ms[0], ms[1])

    f1_wait(0)
    f2_start(0)
    near_forward(0, 6)
    tilest[c] = tiles[...].T
    m1_forward(0)
    f1_start(1)
    m1_start(1)
    to_mate(1, tilest.at[c], tilest.at[c]).start()
    pr = iota((D, D), 0)
    want = pr // 12 % 16 * 48 + pr // 192 * 12 + pr % 12
    perm[...] = jnp.where(iota((D, D), 1) == want, 1.0, 0.0).astype(BF)
    tilesp[c] = nt(perm[...], tiles[...]).astype(BF)
    to_mate(6, tilesp.at[c], tilesp.at[c]).start()

    m2_wait(0)
    kg = gkv[:, :, :, :D].reshape(N, D)
    vg = gkv[:, :, :, D:].reshape(N, D)
    gdev = g * 8 + iota((32, N), 1) // 32 % 4 * 2 + iota((32, N), 1) // 128
    gpos = gdev * N + iota((32, N), 1) % 32 * 8
    gbias = jnp.concatenate(
        [jnp.where(gpos + offs[0, h] < limit, 0.0, NEG) for h in range(H)], axis=0
    )
    s = nt(block_diag(gqd[c, z, :, :D]), kg) + gbias
    m = jnp.max(s, axis=1, keepdims=True)
    e = jnp.exp(s - m)
    total = jnp.sum(e, axis=1, keepdims=True)
    e = e.astype(BF)
    emid[...] = e
    mnum[...] = diag_sum(nn(e, vg), 32)
    mden[...] = per_head(total, 32)
    mmax[...] = per_head(m, 32)

    f2_wait(0)
    f3_copy(0).start()

    def spread_mid(x):
        return jnp.broadcast_to(x[:, None, :], (32, 8, 128)).reshape(N, 128)

    def spread_far(x):
        return jnp.concatenate(
            [jnp.broadcast_to(x[0:1], (128, 128)), jnp.broadcast_to(x[1:2], (128, 128))], axis=0
        )

    def pick_mid(x):
        return jnp.sum(x.reshape(32, 8, 128), axis=1)

    def pick_far(x):
        return jnp.concatenate(
            [
                jnp.sum(x[:128], axis=0, keepdims=True),
                jnp.sum(x[128:], axis=0, keepdims=True),
            ],
            axis=0,
        )

    @pl.loop(0, 6)
    def _(p):
        ls = lanes(p)
        mm = midm[:, ls].astype(F32)
        fm = farm[:, ls].astype(F32)
        m0 = mx[:, ls]
        m1 = jnp.where(mm > 0.5, spread_mid(mmax[:, ls]), NEG)
        top = jnp.maximum(m0, m1)
        w0 = jnp.exp(m0 - top)
        w1 = jnp.exp(m1 - top)
        total = w0 * den[:, ls] + w1 * spread_mid(mden[:, ls])
        inv = 1.0 / total
        exact = (w0 * num[:, ls] + w1 * spread_mid(mnum[:, ls])) * inv
        at = exact.astype(BF)
        attn[:, ls] = at
        do = pk[:, lanes(p, 3 * D)].astype(F32)
        prod = do * at.astype(F32)
        scale = w0 * inv
        sdo[:, ls] = (scale * do).astype(BF)
        npr[:, ls] = (-scale * prod).astype(BF)
        lse = top + jnp.log(total)
        mlse[:, ls] = pick_mid(lse * mm)
        mprod[:, ls] = pick_mid(prod * mm)
        flse[0:2, ls] = pick_far(lse * fm)
        fat[0:2, ls] = pick_far(exact * fm)
        fsc[0:2, ls] = pick_far(scale * fm)

    f3_wait(0)

    heads = hsel[...]
    headb = heads.astype(BF)

    def far_diag(v):
        return jnp.concatenate([v[0:1] * headb, v[1:2] * headb], axis=0)

    def far_fold(v):
        return jnp.concatenate(
            [jnp.sum(v[16 * r : 16 * r + 16] * heads, axis=0, keepdims=True) for r in range(2)],
            axis=0,
        )

    col = iota((16, 512), 1)
    fdev = col // 16 % 16 * 8 + col // 2 % 4 * 2 + col // 256
    fpos = (fdev * 2 + col % 2) * 128
    lead = col // 8 % 2 == 0
    off_col = jnp.zeros((16, 512), I32)
    for h in range(H):
        off_col = jnp.where(iota((16, 512), 0) == h, offs[1, h], off_col)
    fbias = jnp.where(jnp.logical_and(lead, fpos + off_col < limit), 0.0, NEG)
    fbias = jnp.concatenate([fbias, fbias], axis=0)
    kvf = far2kv[...].reshape(512, D)
    s = nt(far_diag(floc[2]), kvf) + fbias
    m = jnp.max(s, axis=1, keepdims=True)
    e = jnp.exp(s - m)
    efar[...] = e
    fnum[0:2] = far_fold(nn(pltpu.roll(e, 8, 1).astype(BF), kvf))
    fden[0:2] = far_fold(jnp.broadcast_to(jnp.sum(e, axis=1, keepdims=True), (32, D)))
    fmax[0:2] = far_fold(jnp.broadcast_to(m, (32, D)))

    f1_wait(1)
    f2_start(1)
    a_lse = flse[0:2]
    b_lse = fmax[0:2] + jnp.log(fden[0:2])
    top = jnp.maximum(a_lse, b_lse)
    n_lse = top + jnp.log(jnp.exp(a_lse - top) + jnp.exp(b_lse - top))
    wa = jnp.exp(a_lse - n_lse)
    n_at = (wa * fat[0:2] + jnp.exp(b_lse - n_lse) * fnum[0:2] / fden[0:2]).astype(BF)
    f_do = floc[3, 0:2].astype(F32)
    n_prod = f_do * n_at.astype(F32)
    scale = fsc[0:2] * wa
    n_sdo = scale * f_do
    n_npr = -scale * n_prod
    flse[...] = jnp.concatenate([n_lse, jnp.zeros((14, D), F32)], axis=0)
    fprod[...] = jnp.concatenate([n_prod, jnp.zeros((14, D), F32)], axis=0)
    for p in range(6):
        ls = slice(p * 128, p * 128 + 128)
        keep = nfar[:, ls]
        take = farm[:, ls]
        for ref, new in ((attn, n_at.astype(F32)), (sdo, n_sdo), (npr, n_npr)):
            ref[:, ls] = ref[:, ls] * keep + spread_far(new[:, ls]).astype(BF) * take
    g32 = iota((32, D), 0)
    for r in range(2):
        both = jnp.logical_and(g32 == r * 16 + o1 // 8, o1 % 8 == o0)
        mlse[...] = jnp.where(both, n_lse[r : r + 1], mlse[...])
        mprod[...] = jnp.where(both, n_prod[r : r + 1], mprod[...])

    lse_rows = jnp.concatenate([mlse[...], flse[...]], axis=0)
    prod_rows = jnp.concatenate([mprod[...], fprod[...]], axis=0)
    l_hi = lse_rows.astype(BF)
    left = lse_rows - l_hi.astype(F32)
    l_mid = left.astype(BF)
    l_lo = (left - l_mid.astype(F32)).astype(BF)
    p_hi = prod_rows.astype(BF)
    p_lo = (prod_rows - p_hi.astype(F32)).astype(BF)
    lt = nn(jnp.concatenate([l_hi, l_mid, l_lo], axis=0), sel1[...])
    pt = nn(jnp.concatenate([p_hi, p_lo], axis=0), sel2[...])
    st = lt[0:48] + lt[48:96] + lt[96:144] + pt[0:48] + pt[48:96]
    gst[c, z] = st[0:32]
    fs = st[32:48]
    r8 = iota((8, 128), 0)
    far1st[z] = jnp.where(r8 == 2 * z, fs[0:1], jnp.where(r8 == 2 * z + 1, fs[1:2], 0.0))
    f1_start(2)
    m1_start(2)

    attnt[c] = nt(perm[...], attn[...]).astype(BF)
    to_mate(2, attnt.at[c], attnt.at[c]).start()
    def put_part(b, v):
        part[b] = v.astype(BF).reshape(4, 4, 48, 384)

    def dev(x_, y_):
        return ((x_ % 4 * 4 + y_ % 4) * 4 + z) * 2 + c

    pos = (x, y)
    step = (lambda k: dev(x + k, y), lambda k: dev(x, y + k))

    def where_in(b, q, h):
        some = slice(None) if h is None else pl.ds(2 * h, 2)
        return (b, q, some) if b % 2 == 0 else (b, some, q)

    def ring_copy(b, n):
        p = pos[b % 2]
        nxt, prv = step[b % 2](1), step[b % 2](3)
        up, down, far = (p + 1) % 4, (p + 3) % 4, (p + 2) % 4
        src, dst, to = (
            lambda: (part.at[where_in(b, far, 0)], r1.at[b, 0], nxt),
            lambda: (part.at[where_in(b, far, 1)], r1.at[b, 1], prv),
            lambda: (part.at[where_in(b, up, 1)], r2.at[b, 0, pl.ds(2, 2)], nxt),
            lambda: (part.at[where_in(b, down, 0)], r2.at[b, 1, pl.ds(0, 2)], prv),
            lambda: (tmp.at[b, 0], r2.at[b, 0, pl.ds(0, 2)], nxt),
            lambda: (tmp.at[b, 1], r2.at[b, 1, pl.ds(2, 2)], prv),
        )[n]()
        return rc(src, dst, rs.at[b], rr_.at[b, min(n, 2)], to)

    def ring_a(b):
        for n in range(4):
            ring_copy(b, n).start()

    def ring_b(b):
        p = pos[b % 2]
        for h, q in ((0, (p + 1) % 4), (1, (p + 3) % 4)):
            ring_copy(b, h).wait_recv()
            tmp[b, h] = (part[where_in(b, q, h)].astype(F32) + r1[b, h].astype(F32)).astype(BF)
            ring_copy(b, 4 + h).start()

    def second(b, k):
        j = (b + 1) % 2
        q = (pos[j] + k) % 4
        return rc(acc.at[b, q], s2.at[b, pos[j]], ss.at[b], sr.at[b], step[j](k))

    def second_all(b):
        some = s2.at[b, pl.ds(0, 3)]
        return rc(some, some, ss.at[b], sr.at[b], mate)

    def ring_c(b):
        rc(r2.at[b], r2.at[b], rs.at[b], rr_.at[b, 2], mate).wait_recv()
        mine = part[where_in(b, pos[b % 2], None)].astype(F32)
        acc[b] = (mine + r2[b, 0].astype(F32) + r2[b, 1].astype(F32)).astype(BF)
        for k in (2, 1, 3):
            second(b, k).start()

    def ring_d(b):
        j = (b + 1) % 2
        total = acc[b, pos[j]].astype(F32)
        second_all(b).wait_recv()
        for k in (1, 3, 2):
            total = total + s2[b, (pos[j] + k) % 4].astype(F32)
        tot[b] = total.astype(BF)

    own = z * 2 + c
    er = iota((128, 96), 0)
    ek = er % 8
    spread = jnp.where(
        jnp.logical_and(iota((128, 96), 1) == er // 8 % 2 * 48 + er // 16 * 6 + ek, ek < 6), 1.0, 0.0
    ).astype(BF)

    def fin_copy(k):
        o = (own + k) % 8
        return rc(fin.at[o], finr.at[own], es_.at[0], er_.at[0], g * 8 + o)

    def fin_all():
        some = finr.at[pl.ds(0, 7)]
        return rc(some, some, es_.at[0], er_.at[0], mate)

    def fin_start(_):
        fin[...] = nn(spread, tot[...].reshape(96, 384)).astype(BF).reshape(8, 16, 384)
        for k in range(1, 8):
            fin_copy(k).start()
        finr[own] = fin[own]

    def fin_end(_):
        fin_all().wait_recv()
        for a in range(2):
            v = finr[a].astype(F32)
            for o in (2, 4, 6):
                v = v + finr[o + a].astype(F32)
            for i in range(2):
                at = (1 + i) * D + 384 * a
                g_qkv[:, at : at + 384] = v[8 * i : 8 * i + 6]

    def put_z(b, v):
        pz[b] = v.astype(BF).reshape(4, 4, 48, 384)

    def z_copy(b, n):
        nxt, prv = zpeer(1), zpeer(3)
        up, down, far = (z + 1) % 4, (z + 3) % 4, (z + 2) % 4
        lo, hi = pl.ds(0, 2), pl.ds(2, 2)
        src, dst, to = (
            lambda: (pz.at[b, far, lo], z1.at[b, 0], nxt),
            lambda: (pz.at[b, far, hi], z1.at[b, 1], prv),
            lambda: (pz.at[b, up, hi], z2.at[b, 0, hi], nxt),
            lambda: (pz.at[b, down, lo], z2.at[b, 1, lo], prv),
            lambda: (zt.at[b, 0], z2.at[b, 0, lo], nxt),
            lambda: (zt.at[b, 1], z2.at[b, 1, hi], prv),
        )[n]()
        return rc(src, dst, zrs.at[b], zrr.at[b, min(n, 2)], to)

    def z_a(b):
        for n in range(4):
            z_copy(b, n).start()

    def z_b(b):
        for h, q in ((0, (z + 1) % 4), (1, (z + 3) % 4)):
            z_copy(b, h).wait_recv()
            mine = pz[b, q, 2 * h : 2 * h + 2].astype(F32)
            zt[b, h] = (mine + z1[b, h].astype(F32)).astype(BF)
            z_copy(b, 4 + h).start()

    def z_second(b, k):
        return rc(zacc.at[b, (g + k) % 16], zs.at[b, g], zss.at[b], zsr.at[b], gpeer(k))

    def z_second_all(b):
        some = zs.at[b, pl.ds(0, 15)]
        return rc(some, some, zss.at[b], zsr.at[b], mate)

    def z_c(b):
        rc(z2.at[b], z2.at[b], zrs.at[b], zrr.at[b, 2], mate).wait_recv()
        mine = pz[b, z].astype(F32)
        mine = mine + z2[b, 0].astype(F32) + z2[b, 1].astype(F32)
        stage[0:192] = mine.reshape(192, 384)
        for i in range(16):
            zacc[b, i] = stage[12 * i : 12 * i + 16].astype(BF)
        for k in range(1, 16):
            z_second(b, k).start()

    def z_mate(b):
        return rc(zf.at[b], zm.at[b], zms.at[b], zmr.at[b], mate)

    def z_d(b):
        z_second_all(b).wait_recv()
        total = zacc[b, g].astype(F32)
        for k in range(1, 16):
            total = total + zs[b, (g + k) % 16].astype(F32)
        zf[b] = total
        z_mate(b).start()

    def z_e(b):
        z_mate(b).wait_recv()
        target = (g_out, g_qkv)[b]
        for ref, half in ((zf, c), (zm, 1 - c)):
            v = ref[b]
            cols = pl.ds(pl.multiple_of(384 * half, 128), 384)
            target[:, cols] = jnp.where(c == 0, v[0:6], v[6:12])

    def backward_queries(lo, hi):
        @pl.loop(lo, hi)
        def _(p):
            ls = lanes(p)
            k2 = pk[:, lanes(p, D)]
            so = sdo[:, ls]
            sp = npr[:, ls]
            rhs = jnp.concatenate([pk[:, lanes(p, 2 * D)], jnp.ones((N, 128), BF)], axis=1)
            ds = []
            for a in range(2):
                lhs = jnp.concatenate([so * hm[a], sp * hm[a]], axis=1)
                d = (emat[2 * p + a].astype(F32) * nt(lhs, rhs)).astype(BF)
                dsm[2 * p + a] = d
                ds.append(d)
            dq[:, ls] = 0.125 * nn(
                jnp.concatenate(ds, axis=1), jnp.concatenate([k2 * hm[0], k2 * hm[1]], axis=0)
            )

    def backward_keys(lo, hi):
        @pl.loop(lo, hi)
        def _(p):
            ls = lanes(p)
            q2 = pk[:, ls]
            so = sdo[:, ls]
            dk[:, ls] = tn(
                jnp.concatenate([dsm[2 * p], dsm[2 * p + 1]], axis=0),
                jnp.concatenate([q2 * hm[0], q2 * hm[1]], axis=0),
            )
            dv[:, ls] = tn(
                jnp.concatenate([emat[2 * p], emat[2 * p + 1]], axis=0),
                jnp.concatenate([so * hm[0], so * hm[1]], axis=0),
            )

    backward_queries(0, 2)
    to_mate(0, cotr, cotr).wait_recv()
    to_mate(2, attnt.at[1 - c], attnt.at[1 - c]).wait_recv()
    put_z(0, nn(attnt[c], cot[:, own_cols]) + nn(attnt[1 - c], cotr[...]))
    z_a(0)
    m1_forward(1)
    backward_queries(2, 4)
    f1_wait(2)
    f2_start(2)
    m1_forward(2)
    backward_queries(4, 6)

    kg = gkv[:, :, :, :D].reshape(N, D)
    vg = gkv[:, :, :, D:].reshape(N, D)
    scale = jnp.exp(mmax[...] - mlse[...])
    so = (scale * gqd[c, z, :, D:].astype(F32)).astype(BF)
    sp = scale * mprod[...]
    dl = jnp.concatenate(
        [jnp.sum(sp * head_mask(h, F32), axis=1, keepdims=True) for h in range(H)], axis=0
    )
    ds = (emid[...].astype(F32) * (nt(block_diag(so), vg) - dl)).astype(BF)
    dmid[0] = 0.125 * diag_sum(nn(ds, kg), 32)

    scale = jnp.exp(fmax[0:2] - flse[0:2])
    so = (scale * floc[3, 0:2].astype(F32)).astype(BF)
    sp = scale * fprod[0:2]
    dl = jnp.concatenate(
        [jnp.sum(sp[r : r + 1] * heads, axis=1, keepdims=True) for r in range(2)], axis=0
    )
    kvf = far2kv[...].reshape(512, D)
    t = pltpu.roll(nt(far_diag(so), kvf), 504, 1)
    dfar[0, 0:2] = 0.125 * far_fold(nn((efar[...] * (t - dl)).astype(BF), kvf))

    def grad_part(a, near):
        @pl.loop(0, 6)
        def _(p):
            ls = lanes(p)
            mm = midm[:, ls].astype(F32)
            fm = farm[:, ls].astype(F32)
            v = near[:, ls] + mm * spread_mid(dmid[a, :, ls]) + fm * spread_far(dfar[a, 0:2, ls])
            v = v.astype(BF)
            gp[:, lanes(p, a * D)] = v
            gph[a, p // 3, :, lanes(p % 3)] = v

        to_mate(3 + a, gph.at[a, 1 - c], gpr.at[a]).start()

    def weight_part(a):
        to_mate(3 + a, gpr.at[a], gpr.at[a]).wait_recv()
        rows = tilest if a else tilesp
        v = nn(rows[c], gph[a, c]) + nn(rows[1 - c], gpr[a])
        if a == 0:
            put_z(1, v)
        else:
            put_part(a - 1, v)
            ring_a(a - 1)

    grad_part(0, dq)
    backward_keys(0, 4)
    f2_wait(1)
    f3_copy(1).start()
    to_mate(1, tilest.at[1 - c], tilest.at[1 - c]).wait_recv()
    to_mate(6, tilesp.at[1 - c], tilesp.at[1 - c]).wait_recv()
    z_b(0)
    weight_part(0)
    backward_keys(4, 6)
    f2_wait(2)
    f3_copy(2).start()
    m2_wait(1)
    m2_wait(2)

    st = gst[...].reshape(N, 128).T
    ls_rows = st[0:16]
    dl_rows = st[12:28]
    qg = gqd[:, :, :, :D].reshape(N, D)
    og = gqd[:, :, :, D:].reshape(N, D)
    s = nt(block_diag(gkv[c, z, :, :D]), qg)
    t = nt(block_diag(gkv[c, z, :, D:]), og)
    ps, dss = [], []
    for h in range(H):
        ok = me * N + iota((32, N), 0) * 8 + offs[0, h] < limit
        p = jnp.exp(jnp.where(ok, s[h * 32 : (h + 1) * 32] - ls_rows[h : h + 1], NEG))
        ps.append(p.astype(BF))
        dss.append((p * (t[h * 32 : (h + 1) * 32] - dl_rows[h : h + 1])).astype(BF))
    dmid[1] = diag_sum(nn(jnp.concatenate(dss, axis=0), qg), 32)
    pmid = jnp.concatenate(ps, axis=0)

    f3_wait(1)
    f3_wait(2)
    st = far2st[...].reshape(32, 8, 128)
    st = jnp.concatenate([st, jnp.zeros_like(st)], axis=1).reshape(512, 128).T
    ls_rows = jnp.concatenate([st[0:16], st[0:16]], axis=0)
    dl_rows = jnp.concatenate([st[12:28], st[12:28]], axis=0)
    qdf = far2qd[...].reshape(512, D)
    s = nt(far_diag(floc[0]), qdf)
    t = pltpu.roll(nt(far_diag(floc[1]), qdf), 504, 1)
    row_h = iota((16, 512), 0)
    oks = [
        jnp.logical_and(
            jnp.logical_and(lead, row_h < H), (me * 2 + r) * 128 + off_col < limit
        )
        for r in range(2)
    ]
    expo = jnp.concatenate(
        [jnp.where(oks[r], (s - ls_rows)[16 * r : 16 * r + 16], NEG) for r in range(2)], axis=0
    )
    pfar = jnp.exp(expo)
    dfar[1, 0:2] = far_fold(nn((pfar * (t - dl_rows)).astype(BF), qdf))
    grad_part(1, dk)
    dmid[2] = diag_sum(nn(pmid, og), 32)
    dfar[2, 0:2] = far_fold(nn(pltpu.roll(pfar, 8, 1).astype(BF), qdf))
    z_c(0)
    z_a(1)
    grad_part(2, dv)
    weight_part(1)
    weight_part(2)

    @pl.loop(0, 3)
    def _(i):
        ls = pl.ds(pl.multiple_of(i * N, N), N)
        out_rows[:, ls] = (tiles[:, ls].astype(F32) + nn(attn[...], wout[:, ls])).astype(BF)
        grad_tiles[:, ls] = nt(gp[...], wqkv[ls, :]).astype(BF)

    z_b(1)
    ring_b(0)
    ring_b(1)
    z_c(1)
    ring_c(0)
    ring_c(1)
    z_d(0)
    ring_d(0)
    ring_d(1)
    fin_start(1)
    z_d(1)
    z_e(0)
    z_e(1)
    fin_end(1)

    to_mate(0, cot.at[:, half_cols], cotr).wait_send()
    to_mate(1, tilest.at[c], tilest.at[c]).wait_send()
    to_mate(6, tilesp.at[c], tilesp.at[c]).wait_send()
    to_mate(2, attnt.at[c], attnt.at[c]).wait_send()
    for a in range(3):
        to_mate(3 + a, gph.at[a, 1 - c], gpr.at[a]).wait_send()
    for b in range(2):
        some = part.at[b, pl.ds(0, 3)]
        rc(some, some, rs.at[b], rr_.at[b, 2], mate).wait_send()
        second_all(b).wait_send()
        some = pz.at[b, pl.ds(0, 3)]
        rc(some, some, zrs.at[b], zrr.at[b, 2], mate).wait_send()
        z_second_all(b).wait_send()
        z_mate(b).wait_send()
    fin_all().wait_send()
    for t in range(3):
        f1_all(t).wait_send()
        m1_all(t).wait_send()
        f2_all(t).wait_send()
        f3_copy(t).wait_send()
        m2_all(t, c).wait_send()


def copy_kernel(*refs):
    sems = refs[8]
    copies = [pltpu.make_async_copy(refs[i], refs[4 + i], sems.at[i]) for i in range(4)]
    for item in copies:
        item.start()
    for item in copies:
        item.wait()


def per_device(tiles, w_qkv, w_out, cotangent, offsets, pad_count):
    vm = pl.BlockSpec(memory_space=pltpu.VMEM)
    hbm = pl.BlockSpec(memory_space=pl.ANY)
    V = pltpu.VMEM
    dma = pltpu.SemaphoreType.DMA
    big = V((N, D), F32)
    bigb = V((N, D), BF)
    m32 = V((32, D), F32)
    f16 = V((16, D), F32)
    shapes = (
        jax.ShapeDtypeStruct((N, D), BF),
        jax.ShapeDtypeStruct((N, D), BF),
        jax.ShapeDtypeStruct((6, 3 * D), F32),
        jax.ShapeDtypeStruct((6, D), F32),
    )
    outs = pl.pallas_call(
        kernel,
        out_shape=tuple(V(a.shape, a.dtype) for a in shapes),
        in_specs=[hbm] * 6,
        out_specs=(vm,) * 4,
        scratch_shapes=[
            pltpu.SMEM((2, H), I32), pltpu.SMEM((1,), I32),
            bigb, V((D, 3 * D), BF), V((D, D), BF), bigb,
            V((N, 4 * D), BF), bigb, bigb, bigb, V((D, 128), BF), V((D, 128), BF), f16,
            V((H, N, N), BF), V((H, N, N), BF), big, big, big,
            V((2, 4, 32, 2 * D), BF), V((2, 4, 32, 2 * D), BF), V((2, 4, 32, 128), F32),
            V((4, 16, D), BF), V((4, 16, D), BF), V((4, 8, 128), F32),
            V((2, 16, 16, D), BF), V((2, 16, 16, D), BF), V((2, 16, 8, 128), F32),
            V((4, 16, D), BF), m32, m32, m32, f16, f16, f16, V((H * 32, N), BF), V((32, 512), F32),
            bigb, bigb, bigb, m32, m32, f16, f16, f16, f16,
            big, big, big, V((3, 32, D), F32), V((3, 16, D), F32), V((N, 3 * D), BF),
            V((2, D, N), BF), V((2, D, N), BF), V((2, D, N), BF), V((N, 384), BF), V((D, D), BF),
            V((3, 2, N, 384), BF), V((3, N, 384), BF),
            V((2, 4, 4, 48, 384), BF),
            V((2, 2, 2, 48, 384), BF), V((2, 2, 2, 48, 384), BF), V((2, 2, 4, 48, 384), BF),
            V((2, 4, 48, 384), BF), V((2, 4, 48, 384), BF), V((2, 48, 384), BF),
            V((8, 16, 384), BF), V((8, 16, 384), BF),
            V((208, 384), F32), V((2, 4, 4, 48, 384), BF),
            V((2, 2, 2, 48, 384), BF), V((2, 2, 2, 48, 384), BF), V((2, 2, 4, 48, 384), BF),
            V((2, 16, 16, 384), BF), V((2, 16, 16, 384), BF), V((2, 16, 384), F32), V((2, 16, 384), F32),
            dma((9,)), dma((2,)),
            dma((3,)), dma((3,)), dma((3,)), dma((3,)), dma((3,)), dma((3,)),
            dma((3,)), dma((3,)), dma((3,)), dma((3,)),
            dma((7,)), dma((7,)), dma((2,)), dma((2, 3)), dma((2,)), dma((2,)),
            dma((1,)), dma((1,)),
            dma((2,)), dma((2, 3)), dma((2,)), dma((2,)), dma((2,)), dma((2,)),
        ],
        compiler_params=pltpu.CompilerParams(
            collective_id=0, has_side_effects=True, vmem_limit_bytes=61 * 1024 * 1024
        ),
        name="layer",
    )(offsets, pad_count, tiles, w_qkv, w_out, cotangent)
    return pl.pallas_call(
        copy_kernel, out_shape=shapes, in_specs=[vm] * 4, out_specs=(hbm,) * 4, scratch_shapes=[dma((4,))],
        name="results"
    )(*(pltpu.with_memory_space_constraint(o, pltpu.VMEM) for o in outs))


def solution(mesh):
    row = P("ctx", None)
    return jax.shard_map(
        per_device,
        mesh=mesh,
        in_specs=(row, P(), P(), row, P(), P()),
        out_specs=(row, row, row, row),
        check_vma=False,
    )
```

```python
import jax
import jax.numpy as jnp
from jax import lax
from jax.experimental import pallas as pl
from jax.experimental.pallas import tpu as pltpu
from jax.sharding import PartitionSpec as P

MESH = pl.DeviceIdType.MESH
N = 256
D = 768
H = 12
E = 64
NEG = -1e30
F32 = jnp.float32
BF = jnp.bfloat16
I32 = jnp.int32


def dot(a, b, ca, cb, precision=None):
    dims = (((ca,), (cb,)), ((), ()))
    return lax.dot_general(a, b, dims, precision=precision, preferred_element_type=F32)


def nn(a, b):
    return dot(a, b, 1, 0)


def nt(a, b):
    return dot(a, b, 1, 1)


def tn(a, b):
    return dot(a, b, 0, 0)


def iota(shape, dim):
    return lax.broadcasted_iota(I32, shape, dim)


def head_mask(h, dtype):
    return jnp.where(iota((1, D), 1) // E == h, 1.0, 0.0).astype(dtype)


def block_diag(x):
    return jnp.concatenate([x * head_mask(h, x.dtype) for h in range(H)], axis=0)


def diag_sum(x, rows):
    head = iota((rows, D), 1) // E
    out = jnp.zeros((rows, D), F32)
    for h in range(H):
        out = jnp.where(head == h, x[h * rows : (h + 1) * rows], out)
    return out


def per_head(cols, rows):
    head = iota((rows, D), 1) // E
    out = jnp.zeros((rows, D), F32)
    for h in range(H):
        out = jnp.where(head == h, cols[h * rows : (h + 1) * rows], out)
    return out


def kernel(
    offs_h, pad_h, tiles_h, wqkv_h, wout_h, cot_h,
    out_rows, grad_tiles, g_qkv, g_out,
    offs, pad, tiles, wqkv, wout, cot,
    pk, midm, farm, nfar, sel1, sel2, hsel, emat, dsm, num, den, mx,
    gkv, gqd, gst, far1kv, far1qd, far1st, far2kv, far2qd, far2st,
    floc, mnum, mden, mmax, fnum, fden, fmax, emid, efar,
    attn, sdo, npr, mlse, mprod, flse, fprod, fat, fsc,
    dq, dk, dv, dmid, dfar, gp, tilest, tilesp, attnt, cotr, perm, gph, gpr,
    part, r1, tmp, r2, acc, s2, tot, fin, finr,
    stage, pz, z1, zt, z2, zacc, zs, zf, zm,
    ls_, os_, f1s, f1r, f2s, f2r, f3s, f3r, m1s, m1r, m2s, m2r,
    xs, xr, rs, rr_, ss, sr, es_, er_,
    zrs, zrr, zss, zsr, zms, zmr,
):
    me = lax.axis_index("ctx")
    c = me % 2
    z = me // 2 % 4
    g = me // 8
    x = g // 4
    y = g % 4
    mate = g * 8 + z * 2 + (1 - c)

    def zpeer(k):
        return g * 8 + (z + k) % 4 * 2 + c

    def gpeer(k):
        return (g + k) % 16 * 8 + z * 2 + c

    def rc(src, dst, ss, rs, dev):
        return pltpu.make_async_remote_copy(
            src_ref=src, dst_ref=dst, send_sem=ss, recv_sem=rs, device_id=(dev,), device_id_type=MESH
        )

    def load(src, dst, n):
        return pltpu.make_async_copy(src, dst, ls_.at[n])

    loads = [load(tiles_h, tiles, 0)]
    for i in range(3):
        for a in (1, 2):
            cols = pl.ds(a * D + i * N, N)
            loads.append(load(wqkv_h.at[:, cols], wqkv.at[:, cols], 1 + i))
    later = [
        load(wqkv_h.at[:, pl.ds(0, D)], wqkv.at[:, pl.ds(0, D)], 4),
        load(cot_h, cot, 5),
        load(wout_h, wout, 6),
    ]
    small = (load(offs_h, offs, 7), load(pad_h, pad, 8))
    for item in small:
        item.start()
    for item in loads:
        item.start()
    barrier = pltpu.get_barrier_semaphore()
    peers = [mate] + [zpeer(k) for k in (1, 2, 3)] + [gpeer(k) for k in range(1, 16)]
    peers += [g * 8 + (z + k) % 4 * 2 + (1 - c) for k in (1, 2, 3)]
    for p in peers:
        pl.semaphore_signal(barrier, inc=1, device_id=(p,), device_id_type=MESH)

    FAR1 = (far1kv, far1qd, far1st)
    FAR2 = (far2kv, far2qd, far2st)
    MID = (gkv, gqd, gst)

    def f1_copy(t, k):
        return rc(FAR1[t].at[z], FAR1[t].at[z], f1s.at[t], f1r.at[t], zpeer(k))

    def f1_all(t):
        some = FAR1[t].at[pl.ds(0, 3)]
        return rc(some, some, f1s.at[t], f1r.at[t], zpeer(1))

    def f1_start(t):
        for k in (1, 3, 2):
            f1_copy(t, k).start()

    def f1_wait(t):
        f1_all(t).wait_recv()

    def f2_copy(t, k):
        return rc(FAR2[t].at[c, g], FAR2[t].at[c, g], f2s.at[t], f2r.at[t], gpeer(k))

    def f2_all(t):
        some = FAR2[t].at[c, pl.ds(0, 15)]
        return rc(some, some, f2s.at[t], f2r.at[t], gpeer(1))

    def f2_start(t):
        a = FAR1[t]
        FAR2[t][c, g] = (
            a[0].astype(F32) + a[1].astype(F32) + a[2].astype(F32) + a[3].astype(F32)
        ).astype(a.dtype)
        for k in range(1, 16):
            f2_copy(t, k).start()

    def f2_wait(t):
        f2_all(t).wait_recv()

    def f3_copy(t):
        return rc(FAR2[t].at[c], FAR2[t].at[c], f3s.at[t], f3r.at[t], mate)

    def f3_wait(t):
        rc(FAR2[t].at[1 - c], FAR2[t].at[1 - c], f3s.at[t], f3r.at[t], mate).wait_recv()

    def m1_copy(t, k):
        return rc(MID[t].at[c, z], MID[t].at[c, z], m1s.at[t], m1r.at[t], zpeer(k))

    def m1_all(t):
        some = MID[t].at[c, pl.ds(0, 3)]
        return rc(some, some, m1s.at[t], m1r.at[t], zpeer(1))

    def m2_copy(t, k):
        o = (z + k) % 4
        return rc(MID[t].at[c, o], MID[t].at[c, o], m2s.at[t], m2r.at[t], mate)

    def m2_all(t, who):
        return rc(MID[t].at[who], MID[t].at[who], m2s.at[t], m2r.at[t], mate)

    def m1_start(t):
        for k in (1, 3, 2):
            m1_copy(t, k).start()
        m2_copy(t, 0).start()

    def m1_forward(t):
        m1_all(t).wait_recv()
        for k in (1, 3, 2):
            m2_copy(t, k).start()

    def m2_wait(t):
        m2_all(t, 1 - c).wait_recv()

    def to_mate(t, src, dst):
        return rc(src, dst, xs.at[t], xr.at[t], mate)

    half_cols = pl.ds(pl.multiple_of(384 * (1 - c), 128), 384)
    own_cols = pl.ds(pl.multiple_of(384 * c, 128), 384)

    for item in small:
        item.wait()
    limit = N * 128 - pad[0]
    lane_head = iota((1, D), 1) // E
    o0 = jnp.zeros((1, D), I32)
    o1 = jnp.zeros((1, D), I32)
    for h in range(H):
        o0 = jnp.where(lane_head == h, offs[0, h], o0)
        o1 = jnp.where(lane_head == h, offs[1, h], o1)
    midm[...] = jnp.where(iota((N, D), 0) % 8 == o0, 1.0, 0.0).astype(BF)
    farm[...] = jnp.where(iota((N, D), 0) % 128 == o1, 1.0, 0.0).astype(BF)

    nfar[...] = jnp.where(iota((N, D), 0) % 128 == o1, 0.0, 1.0).astype(BF)
    r0 = iota((D, 128), 0)
    l0 = iota((D, 128), 1)
    sel1[...] = jnp.where(jnp.logical_and(r0 == l0 * E, l0 < H), 1.0, 0.0).astype(BF)
    sel2[...] = jnp.where(r0 // E == l0 - H, 1.0, 0.0).astype(BF)
    hsel[...] = jnp.where(iota((16, D), 1) // E == iota((16, D), 0), 1.0, 0.0)
    pool_mid = jnp.where(iota((32, N), 1) // 8 == iota((32, N), 0), 1.0, 0.0).astype(BF)
    two = iota((16, N), 1) // 128
    row = iota((16, N), 0)
    pool_far = jnp.where(row == two, 1.0, 0.0)
    none = jnp.zeros_like(pool_far)
    far_a = [jnp.where(row == 2 * z + two, 1.0, 0.0), pool_far, none]
    far_b = [jnp.where(row == 8 + 2 * z + two, 1.0, 0.0), none, pool_far]
    far_a = jnp.concatenate(far_a, axis=0).astype(BF)
    far_b = jnp.concatenate(far_b, axis=0).astype(BF)

    def picks(t, i, a, b):
        ls = pl.ds(pl.multiple_of(i * N, N), N)
        hi = pl.ds(pl.multiple_of(D + i * N, N), N)
        mk = midm[:, ls]
        fk = farm[:, ls]
        rows = (nn(far_a, a * fk) + nn(far_b, b * fk)).astype(BF)
        FAR1[t][z, :, ls] = rows[0:16]
        MID[t][c, z, :, ls] = nn(pool_mid, a * mk).astype(BF)
        MID[t][c, z, :, hi] = nn(pool_mid, b * mk).astype(BF)
        floc[2 * t, :, ls] = rows[16:32]
        floc[2 * t + 1, :, ls] = rows[32:48]

    loads[0].wait()

    for i in range(3):
        cols = pl.ds(i * 2 * N, 2 * N)
        load(wqkv_h.at[:, cols], wqkv.at[:, cols], 1 + i).wait()
        if i == 0:
            for item in later:
                item.start()
        kc = pl.ds(D + i * N, N)
        vc = pl.ds(2 * D + i * N, N)
        kk = nn(tiles[...], wqkv[:, kc]).astype(BF)
        vv = nn(tiles[...], wqkv[:, vc]).astype(BF)
        pk[:, kc] = kk
        pk[:, vc] = vv
        picks(0, i, kk, vv)

    pl.semaphore_wait(barrier, len(peers))
    f1_start(0)
    for item in later:
        item.wait()
    to_mate(0, cot.at[:, half_cols], cotr).start()

    for i in range(3):
        if i == 1:
            m1_start(0)
        qc = pl.ds(i * N, N)
        dc = pl.ds(3 * D + i * N, N)
        qq = nn(tiles[...], wqkv[:, qc]).astype(BF) * jnp.asarray(0.125, BF)
        dd = nt(cot[...], wout[qc, :]).astype(BF)
        pk[:, qc] = qq
        pk[:, dc] = dd
        picks(1, i, qq, dd)


    half = iota((1, 128), 1) // E
    hm = [jnp.where(half == a, 1.0, 0.0).astype(BF) for a in range(2)]

    def lanes(p, base=0):
        return pl.ds(pl.multiple_of(base + p * 128, 128), 128)

    def near_forward(lo, hi):
        @pl.loop(lo, hi, unroll=2)
        def _(p):
            q2 = pk[:, lanes(p)]
            k2 = pk[:, lanes(p, D)]
            v2 = pk[:, lanes(p, 2 * D)]
            bias = jnp.where(me * N + iota((1, N), 1) < limit, 0.0, NEG)
            es, ms = [], []
            for a in range(2):
                s = nt(q2 * hm[a], k2) + bias
                m = jnp.max(s, axis=1, keepdims=True)
                e = jnp.exp(s - m).astype(BF)
                emat[2 * p + a] = e
                es.append(e)
                ms.append(m)
            rhs = jnp.concatenate(
                [
                    jnp.concatenate([v2 * hm[a], jnp.broadcast_to(hm[a], (N, 128))], axis=1)
                    for a in range(2)
                ],
                axis=0,
            )
            nd = nn(jnp.concatenate(es, axis=1), rhs)
            num[:, lanes(p)] = nd[:, :128]
            den[:, lanes(p)] = nd[:, 128:]
            mx[:, lanes(p)] = jnp.where(iota((N, 128), 1) < E, ms[0], ms[1])

    f1_wait(0)
    f2_start(0)
    near_forward(0, 6)
    tilest[c] = tiles[...].T
    m1_forward(0)
    f1_start(1)
    m1_start(1)
    to_mate(1, tilest.at[c], tilest.at[c]).start()
    pr = iota((D, D), 0)
    want = pr // 12 % 16 * 48 + pr // 192 * 12 + pr % 12
    perm[...] = jnp.where(iota((D, D), 1) == want, 1.0, 0.0).astype(BF)
    tilesp[c] = nt(perm[...], tiles[...]).astype(BF)
    to_mate(6, tilesp.at[c], tilesp.at[c]).start()

    m2_wait(0)
    kg = gkv[:, :, :, :D].reshape(N, D)
    vg = gkv[:, :, :, D:].reshape(N, D)
    gdev = g * 8 + iota((32, N), 1) // 32 % 4 * 2 + iota((32, N), 1) // 128
    gpos = gdev * N + iota((32, N), 1) % 32 * 8
    gbias = jnp.concatenate(
        [jnp.where(gpos + offs[0, h] < limit, 0.0, NEG) for h in range(H)], axis=0
    )
    s = nt(block_diag(gqd[c, z, :, :D]), kg) + gbias
    m = jnp.max(s, axis=1, keepdims=True)
    e = jnp.exp(s - m)
    total = jnp.sum(e, axis=1, keepdims=True)
    e = e.astype(BF)
    emid[...] = e
    mnum[...] = diag_sum(nn(e, vg), 32)
    mden[...] = per_head(total, 32)
    mmax[...] = per_head(m, 32)

    f2_wait(0)
    f3_copy(0).start()

    def spread_mid(x):
        return jnp.broadcast_to(x[:, None, :], (32, 8, 128)).reshape(N, 128)

    def spread_far(x):
        return jnp.concatenate(
            [jnp.broadcast_to(x[0:1], (128, 128)), jnp.broadcast_to(x[1:2], (128, 128))], axis=0
        )

    def pick_mid(x):
        return jnp.sum(x.reshape(32, 8, 128), axis=1)

    def pick_far(x):
        return jnp.concatenate(
            [
                jnp.sum(x[:128], axis=0, keepdims=True),
                jnp.sum(x[128:], axis=0, keepdims=True),
            ],
            axis=0,
        )

    @pl.loop(0, 6, unroll=2)
    def _(p):
        ls = lanes(p)
        mm = midm[:, ls].astype(F32)
        fm = farm[:, ls].astype(F32)
        m0 = mx[:, ls]
        m1 = jnp.where(mm > 0.5, spread_mid(mmax[:, ls]), NEG)
        top = jnp.maximum(m0, m1)
        w0 = jnp.exp(m0 - top)
        w1 = jnp.exp(m1 - top)
        total = w0 * den[:, ls] + w1 * spread_mid(mden[:, ls])
        inv = 1.0 / total
        exact = (w0 * num[:, ls] + w1 * spread_mid(mnum[:, ls])) * inv
        at = exact.astype(BF)
        attn[:, ls] = at
        do = pk[:, lanes(p, 3 * D)].astype(F32)
        prod = do * at.astype(F32)
        scale = w0 * inv
        sdo[:, ls] = (scale * do).astype(BF)
        npr[:, ls] = (-scale * prod).astype(BF)
        lse = top + jnp.log(total)
        mlse[:, ls] = pick_mid(lse * mm)
        mprod[:, ls] = pick_mid(prod * mm)
        flse[0:2, ls] = pick_far(lse * fm)
        fat[0:2, ls] = pick_far(exact * fm)
        fsc[0:2, ls] = pick_far(scale * fm)

    f3_wait(0)

    heads = hsel[...]
    headb = heads.astype(BF)

    def far_diag(v):
        return jnp.concatenate([v[0:1] * headb, v[1:2] * headb], axis=0)

    def far_fold(v):
        return jnp.concatenate(
            [jnp.sum(v[16 * r : 16 * r + 16] * heads, axis=0, keepdims=True) for r in range(2)],
            axis=0,
        )

    col = iota((16, 512), 1)
    fdev = col // 16 % 16 * 8 + col // 2 % 4 * 2 + col // 256
    fpos = (fdev * 2 + col % 2) * 128
    lead = col // 8 % 2 == 0
    off_col = jnp.zeros((16, 512), I32)
    for h in range(H):
        off_col = jnp.where(iota((16, 512), 0) == h, offs[1, h], off_col)
    fbias = jnp.where(jnp.logical_and(lead, fpos + off_col < limit), 0.0, NEG)
    fbias = jnp.concatenate([fbias, fbias], axis=0)
    kvf = far2kv[...].reshape(512, D)
    s = nt(far_diag(floc[2]), kvf) + fbias
    m = jnp.max(s, axis=1, keepdims=True)
    e = jnp.exp(s - m)
    efar[...] = e
    fnum[0:2] = far_fold(nn(pltpu.roll(e, 8, 1).astype(BF), kvf))
    fden[0:2] = far_fold(jnp.broadcast_to(jnp.sum(e, axis=1, keepdims=True), (32, D)))
    fmax[0:2] = far_fold(jnp.broadcast_to(m, (32, D)))

    f1_wait(1)
    f2_start(1)
    a_lse = flse[0:2]
    b_lse = fmax[0:2] + jnp.log(fden[0:2])
    top = jnp.maximum(a_lse, b_lse)
    n_lse = top + jnp.log(jnp.exp(a_lse - top) + jnp.exp(b_lse - top))
    wa = jnp.exp(a_lse - n_lse)
    n_at = (wa * fat[0:2] + jnp.exp(b_lse - n_lse) * fnum[0:2] / fden[0:2]).astype(BF)
    f_do = floc[3, 0:2].astype(F32)
    n_prod = f_do * n_at.astype(F32)
    scale = fsc[0:2] * wa
    n_sdo = scale * f_do
    n_npr = -scale * n_prod
    flse[...] = jnp.concatenate([n_lse, jnp.zeros((14, D), F32)], axis=0)
    fprod[...] = jnp.concatenate([n_prod, jnp.zeros((14, D), F32)], axis=0)
    for p in range(6):
        ls = slice(p * 128, p * 128 + 128)
        keep = nfar[:, ls]
        take = farm[:, ls]
        for ref, new in ((attn, n_at.astype(F32)), (sdo, n_sdo), (npr, n_npr)):
            ref[:, ls] = ref[:, ls] * keep + spread_far(new[:, ls]).astype(BF) * take
    g32 = iota((32, D), 0)
    for r in range(2):
        both = jnp.logical_and(g32 == r * 16 + o1 // 8, o1 % 8 == o0)
        mlse[...] = jnp.where(both, n_lse[r : r + 1], mlse[...])
        mprod[...] = jnp.where(both, n_prod[r : r + 1], mprod[...])

    lse_rows = jnp.concatenate([mlse[...], flse[...]], axis=0)
    prod_rows = jnp.concatenate([mprod[...], fprod[...]], axis=0)
    l_hi = lse_rows.astype(BF)
    left = lse_rows - l_hi.astype(F32)
    l_mid = left.astype(BF)
    l_lo = (left - l_mid.astype(F32)).astype(BF)
    p_hi = prod_rows.astype(BF)
    p_lo = (prod_rows - p_hi.astype(F32)).astype(BF)
    lt = nn(jnp.concatenate([l_hi, l_mid, l_lo], axis=0), sel1[...])
    pt = nn(jnp.concatenate([p_hi, p_lo], axis=0), sel2[...])
    st = lt[0:48] + lt[48:96] + lt[96:144] + pt[0:48] + pt[48:96]
    gst[c, z] = st[0:32]
    fs = st[32:48]
    r8 = iota((8, 128), 0)
    far1st[z] = jnp.where(r8 == 2 * z, fs[0:1], jnp.where(r8 == 2 * z + 1, fs[1:2], 0.0))
    f1_start(2)
    m1_start(2)

    attnt[c] = nt(perm[...], attn[...]).astype(BF)
    to_mate(2, attnt.at[c], attnt.at[c]).start()
    def put_part(b, v):
        part[b] = v.astype(BF).reshape(4, 4, 48, 384)

    def dev(x_, y_):
        return ((x_ % 4 * 4 + y_ % 4) * 4 + z) * 2 + c

    pos = (x, y)
    step = (lambda k: dev(x + k, y), lambda k: dev(x, y + k))

    def where_in(b, q, h):
        some = slice(None) if h is None else pl.ds(2 * h, 2)
        return (b, q, some) if b % 2 == 0 else (b, some, q)

    def ring_copy(b, n):
        p = pos[b % 2]
        nxt, prv = step[b % 2](1), step[b % 2](3)
        up, down, far = (p + 1) % 4, (p + 3) % 4, (p + 2) % 4
        src, dst, to = (
            lambda: (part.at[where_in(b, far, 0)], r1.at[b, 0], nxt),
            lambda: (part.at[where_in(b, far, 1)], r1.at[b, 1], prv),
            lambda: (part.at[where_in(b, up, 1)], r2.at[b, 0, pl.ds(2, 2)], nxt),
            lambda: (part.at[where_in(b, down, 0)], r2.at[b, 1, pl.ds(0, 2)], prv),
            lambda: (tmp.at[b, 0], r2.at[b, 0, pl.ds(0, 2)], nxt),
            lambda: (tmp.at[b, 1], r2.at[b, 1, pl.ds(2, 2)], prv),
        )[n]()
        return rc(src, dst, rs.at[b], rr_.at[b, min(n, 2)], to)

    def ring_a(b):
        for n in range(4):
            ring_copy(b, n).start()

    def ring_b(b):
        p = pos[b % 2]
        for h, q in ((0, (p + 1) % 4), (1, (p + 3) % 4)):
            ring_copy(b, h).wait_recv()
            tmp[b, h] = (part[where_in(b, q, h)].astype(F32) + r1[b, h].astype(F32)).astype(BF)
            ring_copy(b, 4 + h).start()

    def second(b, k):
        j = (b + 1) % 2
        q = (pos[j] + k) % 4
        return rc(acc.at[b, q], s2.at[b, pos[j]], ss.at[b], sr.at[b], step[j](k))

    def second_all(b):
        some = s2.at[b, pl.ds(0, 3)]
        return rc(some, some, ss.at[b], sr.at[b], mate)

    def ring_c(b):
        rc(r2.at[b], r2.at[b], rs.at[b], rr_.at[b, 2], mate).wait_recv()
        mine = part[where_in(b, pos[b % 2], None)].astype(F32)
        acc[b] = (mine + r2[b, 0].astype(F32) + r2[b, 1].astype(F32)).astype(BF)
        for k in (2, 1, 3):
            second(b, k).start()

    def ring_d(b):
        j = (b + 1) % 2
        total = acc[b, pos[j]].astype(F32)
        second_all(b).wait_recv()
        for k in (1, 3, 2):
            total = total + s2[b, (pos[j] + k) % 4].astype(F32)
        tot[b] = total.astype(BF)

    own = z * 2 + c
    er = iota((128, 96), 0)
    ek = er % 8
    spread = jnp.where(
        jnp.logical_and(iota((128, 96), 1) == er // 8 % 2 * 48 + er // 16 * 6 + ek, ek < 6), 1.0, 0.0
    ).astype(BF)

    def fin_copy(k):
        o = (own + k) % 8
        return rc(fin.at[o], finr.at[own], es_.at[0], er_.at[0], g * 8 + o)

    def fin_all():
        some = finr.at[pl.ds(0, 7)]
        return rc(some, some, es_.at[0], er_.at[0], mate)

    def fin_start(_):
        fin[...] = nn(spread, tot[...].reshape(96, 384)).astype(BF).reshape(8, 16, 384)
        for k in range(1, 8):
            fin_copy(k).start()
        finr[own] = fin[own]

    def fin_end(_):
        fin_all().wait_recv()
        for a in range(2):
            v = finr[a].astype(F32)
            for o in (2, 4, 6):
                v = v + finr[o + a].astype(F32)
            for i in range(2):
                at = (1 + i) * D + 384 * a
                g_qkv[:, at : at + 384] = v[8 * i : 8 * i + 6]

    def put_z(b, v):
        pz[b] = v.astype(BF).reshape(4, 4, 48, 384)

    def z_copy(b, n):
        nxt, prv = zpeer(1), zpeer(3)
        up, down, far = (z + 1) % 4, (z + 3) % 4, (z + 2) % 4
        lo, hi = pl.ds(0, 2), pl.ds(2, 2)
        src, dst, to = (
            lambda: (pz.at[b, far, lo], z1.at[b, 0], nxt),
            lambda: (pz.at[b, far, hi], z1.at[b, 1], prv),
            lambda: (pz.at[b, up, hi], z2.at[b, 0, hi], nxt),
            lambda: (pz.at[b, down, lo], z2.at[b, 1, lo], prv),
            lambda: (zt.at[b, 0], z2.at[b, 0, lo], nxt),
            lambda: (zt.at[b, 1], z2.at[b, 1, hi], prv),
        )[n]()
        return rc(src, dst, zrs.at[b], zrr.at[b, min(n, 2)], to)

    def z_a(b):
        for n in range(4):
            z_copy(b, n).start()

    def z_b(b):
        for h, q in ((0, (z + 1) % 4), (1, (z + 3) % 4)):
            z_copy(b, h).wait_recv()
            mine = pz[b, q, 2 * h : 2 * h + 2].astype(F32)
            zt[b, h] = (mine + z1[b, h].astype(F32)).astype(BF)
            z_copy(b, 4 + h).start()

    def z_second(b, k):
        return rc(zacc.at[b, (g + k) % 16], zs.at[b, g], zss.at[b], zsr.at[b], gpeer(k))

    def z_second_all(b):
        some = zs.at[b, pl.ds(0, 15)]
        return rc(some, some, zss.at[b], zsr.at[b], mate)

    def z_c(b):
        rc(z2.at[b], z2.at[b], zrs.at[b], zrr.at[b, 2], mate).wait_recv()
        mine = pz[b, z].astype(F32)
        mine = mine + z2[b, 0].astype(F32) + z2[b, 1].astype(F32)
        stage[0:192] = mine.reshape(192, 384)
        for i in range(16):
            zacc[b, i] = stage[12 * i : 12 * i + 16].astype(BF)
        for k in range(1, 16):
            z_second(b, k).start()

    def z_mate(b):
        return rc(zf.at[b], zm.at[b], zms.at[b], zmr.at[b], mate)

    def z_d(b):
        z_second_all(b).wait_recv()
        total = zacc[b, g].astype(F32)
        for k in range(1, 16):
            total = total + zs[b, (g + k) % 16].astype(F32)
        zf[b] = total
        z_mate(b).start()

    def z_e(b):
        z_mate(b).wait_recv()
        target = (g_out, g_qkv)[b]
        for ref, half in ((zf, c), (zm, 1 - c)):
            v = ref[b]
            cols = pl.ds(pl.multiple_of(384 * half, 128), 384)
            target[:, cols] = jnp.where(c == 0, v[0:6], v[6:12])

    def backward_queries(lo, hi):
        @pl.loop(lo, hi, unroll=2)
        def _(p):
            ls = lanes(p)
            k2 = pk[:, lanes(p, D)]
            so = sdo[:, ls]
            sp = npr[:, ls]
            rhs = jnp.concatenate([pk[:, lanes(p, 2 * D)], jnp.ones((N, 128), BF)], axis=1)
            ds = []
            for a in range(2):
                lhs = jnp.concatenate([so * hm[a], sp * hm[a]], axis=1)
                d = (emat[2 * p + a].astype(F32) * nt(lhs, rhs)).astype(BF)
                dsm[2 * p + a] = d
                ds.append(d)
            dq[:, ls] = 0.125 * nn(
                jnp.concatenate(ds, axis=1), jnp.concatenate([k2 * hm[0], k2 * hm[1]], axis=0)
            )

    def backward_keys(lo, hi):
        @pl.loop(lo, hi, unroll=2)
        def _(p):
            ls = lanes(p)
            q2 = pk[:, ls]
            so = sdo[:, ls]
            dk[:, ls] = tn(
                jnp.concatenate([dsm[2 * p], dsm[2 * p + 1]], axis=0),
                jnp.concatenate([q2 * hm[0], q2 * hm[1]], axis=0),
            )
            dv[:, ls] = tn(
                jnp.concatenate([emat[2 * p], emat[2 * p + 1]], axis=0),
                jnp.concatenate([so * hm[0], so * hm[1]], axis=0),
            )

    backward_queries(0, 4)
    m1_forward(1)
    to_mate(0, cotr, cotr).wait_recv()
    to_mate(2, attnt.at[1 - c], attnt.at[1 - c]).wait_recv()
    put_z(0, nn(attnt[c], cot[:, own_cols]) + nn(attnt[1 - c], cotr[...]))
    z_a(0)
    f1_wait(2)
    f2_start(2)
    backward_queries(4, 6)
    m1_forward(2)

    kg = gkv[:, :, :, :D].reshape(N, D)
    vg = gkv[:, :, :, D:].reshape(N, D)
    scale = jnp.exp(mmax[...] - mlse[...])
    so = (scale * gqd[c, z, :, D:].astype(F32)).astype(BF)
    sp = scale * mprod[...]
    dl = jnp.concatenate(
        [jnp.sum(sp * head_mask(h, F32), axis=1, keepdims=True) for h in range(H)], axis=0
    )
    ds = (emid[...].astype(F32) * (nt(block_diag(so), vg) - dl)).astype(BF)
    dmid[0] = 0.125 * diag_sum(nn(ds, kg), 32)

    scale = jnp.exp(fmax[0:2] - flse[0:2])
    so = (scale * floc[3, 0:2].astype(F32)).astype(BF)
    sp = scale * fprod[0:2]
    dl = jnp.concatenate(
        [jnp.sum(sp[r : r + 1] * heads, axis=1, keepdims=True) for r in range(2)], axis=0
    )
    kvf = far2kv[...].reshape(512, D)
    t = pltpu.roll(nt(far_diag(so), kvf), 504, 1)
    dfar[0, 0:2] = 0.125 * far_fold(nn((efar[...] * (t - dl)).astype(BF), kvf))

    def grad_part(a, near):
        @pl.loop(0, 6)
        def _(p):
            ls = lanes(p)
            mm = midm[:, ls].astype(F32)
            fm = farm[:, ls].astype(F32)
            v = near[:, ls] + mm * spread_mid(dmid[a, :, ls]) + fm * spread_far(dfar[a, 0:2, ls])
            v = v.astype(BF)
            gp[:, lanes(p, a * D)] = v
            gph[a, p // 3, :, lanes(p % 3)] = v

        to_mate(3 + a, gph.at[a, 1 - c], gpr.at[a]).start()

    def weight_part(a):
        to_mate(3 + a, gpr.at[a], gpr.at[a]).wait_recv()
        rows = tilest if a else tilesp
        v = nn(rows[c], gph[a, c]) + nn(rows[1 - c], gpr[a])
        if a == 0:
            put_z(1, v)
        else:
            put_part(a - 1, v)
            ring_a(a - 1)

    grad_part(0, dq)
    backward_keys(0, 4)
    f2_wait(1)
    f3_copy(1).start()
    to_mate(1, tilest.at[1 - c], tilest.at[1 - c]).wait_recv()
    to_mate(6, tilesp.at[1 - c], tilesp.at[1 - c]).wait_recv()
    z_b(0)
    weight_part(0)
    backward_keys(4, 6)
    f2_wait(2)
    f3_copy(2).start()
    m2_wait(1)
    m2_wait(2)

    st = gst[...].reshape(N, 128).T
    ls_rows = st[0:16]
    dl_rows = st[12:28]
    qg = gqd[:, :, :, :D].reshape(N, D)
    og = gqd[:, :, :, D:].reshape(N, D)
    s = nt(block_diag(gkv[c, z, :, :D]), qg)
    t = nt(block_diag(gkv[c, z, :, D:]), og)
    ps, dss = [], []
    for h in range(H):
        ok = me * N + iota((32, N), 0) * 8 + offs[0, h] < limit
        p = jnp.exp(jnp.where(ok, s[h * 32 : (h + 1) * 32] - ls_rows[h : h + 1], NEG))
        ps.append(p.astype(BF))
        dss.append((p * (t[h * 32 : (h + 1) * 32] - dl_rows[h : h + 1])).astype(BF))
    dmid[1] = diag_sum(nn(jnp.concatenate(dss, axis=0), qg), 32)
    pmid = jnp.concatenate(ps, axis=0)

    f3_wait(1)
    f3_wait(2)
    st = far2st[...].reshape(32, 8, 128)
    st = jnp.concatenate([st, jnp.zeros_like(st)], axis=1).reshape(512, 128).T
    ls_rows = jnp.concatenate([st[0:16], st[0:16]], axis=0)
    dl_rows = jnp.concatenate([st[12:28], st[12:28]], axis=0)
    qdf = far2qd[...].reshape(512, D)
    s = nt(far_diag(floc[0]), qdf)
    t = pltpu.roll(nt(far_diag(floc[1]), qdf), 504, 1)
    row_h = iota((16, 512), 0)
    oks = [
        jnp.logical_and(
            jnp.logical_and(lead, row_h < H), (me * 2 + r) * 128 + off_col < limit
        )
        for r in range(2)
    ]
    expo = jnp.concatenate(
        [jnp.where(oks[r], (s - ls_rows)[16 * r : 16 * r + 16], NEG) for r in range(2)], axis=0
    )
    pfar = jnp.exp(expo)
    dfar[1, 0:2] = far_fold(nn((pfar * (t - dl_rows)).astype(BF), qdf))
    grad_part(1, dk)
    dmid[2] = diag_sum(nn(pmid, og), 32)
    dfar[2, 0:2] = far_fold(nn(pltpu.roll(pfar, 8, 1).astype(BF), qdf))
    z_c(0)
    z_a(1)
    grad_part(2, dv)
    weight_part(1)
    weight_part(2)

    @pl.loop(0, 3)
    def _(i):
        ls = pl.ds(pl.multiple_of(i * N, N), N)
        out_rows[:, ls] = (tiles[:, ls].astype(F32) + nn(attn[...], wout[:, ls])).astype(BF)
        grad_tiles[:, ls] = nt(gp[...], wqkv[ls, :]).astype(BF)

    z_b(1)
    ring_b(0)
    ring_b(1)
    z_c(1)
    ring_c(0)
    ring_c(1)
    z_d(0)
    ring_d(0)
    ring_d(1)
    fin_start(1)
    z_d(1)
    z_e(0)
    z_e(1)
    fin_end(1)

    to_mate(0, cot.at[:, half_cols], cotr).wait_send()
    to_mate(1, tilest.at[c], tilest.at[c]).wait_send()
    to_mate(6, tilesp.at[c], tilesp.at[c]).wait_send()
    to_mate(2, attnt.at[c], attnt.at[c]).wait_send()
    for a in range(3):
        to_mate(3 + a, gph.at[a, 1 - c], gpr.at[a]).wait_send()
    for b in range(2):
        some = part.at[b, pl.ds(0, 3)]
        rc(some, some, rs.at[b], rr_.at[b, 2], mate).wait_send()
        second_all(b).wait_send()
        some = pz.at[b, pl.ds(0, 3)]
        rc(some, some, zrs.at[b], zrr.at[b, 2], mate).wait_send()
        z_second_all(b).wait_send()
        z_mate(b).wait_send()
    fin_all().wait_send()
    for t in range(3):
        f1_all(t).wait_send()
        m1_all(t).wait_send()
        f2_all(t).wait_send()
        f3_copy(t).wait_send()
        m2_all(t, c).wait_send()


def copy_kernel(*refs):
    sems = refs[8]
    copies = [pltpu.make_async_copy(refs[i], refs[4 + i], sems.at[i]) for i in range(4)]
    for item in copies:
        item.start()
    for item in copies:
        item.wait()


def per_device(tiles, w_qkv, w_out, cotangent, offsets, pad_count):
    vm = pl.BlockSpec(memory_space=pltpu.VMEM)
    hbm = pl.BlockSpec(memory_space=pl.ANY)
    V = pltpu.VMEM
    dma = pltpu.SemaphoreType.DMA
    big = V((N, D), F32)
    bigb = V((N, D), BF)
    m32 = V((32, D), F32)
    f16 = V((16, D), F32)
    shapes = (
        jax.ShapeDtypeStruct((N, D), BF),
        jax.ShapeDtypeStruct((N, D), BF),
        jax.ShapeDtypeStruct((6, 3 * D), F32),
        jax.ShapeDtypeStruct((6, D), F32),
    )
    outs = pl.pallas_call(
        kernel,
        out_shape=tuple(V(a.shape, a.dtype) for a in shapes),
        in_specs=[hbm] * 6,
        out_specs=(vm,) * 4,
        scratch_shapes=[
            pltpu.SMEM((2, H), I32), pltpu.SMEM((1,), I32),
            bigb, V((D, 3 * D), BF), V((D, D), BF), bigb,
            V((N, 4 * D), BF), bigb, bigb, bigb, V((D, 128), BF), V((D, 128), BF), f16,
            V((H, N, N), BF), V((H, N, N), BF), big, big, big,
            V((2, 4, 32, 2 * D), BF), V((2, 4, 32, 2 * D), BF), V((2, 4, 32, 128), F32),
            V((4, 16, D), BF), V((4, 16, D), BF), V((4, 8, 128), F32),
            V((2, 16, 16, D), BF), V((2, 16, 16, D), BF), V((2, 16, 8, 128), F32),
            V((4, 16, D), BF), m32, m32, m32, f16, f16, f16, V((H * 32, N), BF), V((32, 512), F32),
            bigb, bigb, bigb, m32, m32, f16, f16, f16, f16,
            big, big, big, V((3, 32, D), F32), V((3, 16, D), F32), V((N, 3 * D), BF),
            V((2, D, N), BF), V((2, D, N), BF), V((2, D, N), BF), V((N, 384), BF), V((D, D), BF),
            V((3, 2, N, 384), BF), V((3, N, 384), BF),
            V((2, 4, 4, 48, 384), BF),
            V((2, 2, 2, 48, 384), BF), V((2, 2, 2, 48, 384), BF), V((2, 2, 4, 48, 384), BF),
            V((2, 4, 48, 384), BF), V((2, 4, 48, 384), BF), V((2, 48, 384), BF),
            V((8, 16, 384), BF), V((8, 16, 384), BF),
            V((208, 384), F32), V((2, 4, 4, 48, 384), BF),
            V((2, 2, 2, 48, 384), BF), V((2, 2, 2, 48, 384), BF), V((2, 2, 4, 48, 384), BF),
            V((2, 16, 16, 384), BF), V((2, 16, 16, 384), BF), V((2, 16, 384), F32), V((2, 16, 384), F32),
            dma((9,)), dma((2,)),
            dma((3,)), dma((3,)), dma((3,)), dma((3,)), dma((3,)), dma((3,)),
            dma((3,)), dma((3,)), dma((3,)), dma((3,)),
            dma((7,)), dma((7,)), dma((2,)), dma((2, 3)), dma((2,)), dma((2,)),
            dma((1,)), dma((1,)),
            dma((2,)), dma((2, 3)), dma((2,)), dma((2,)), dma((2,)), dma((2,)),
        ],
        compiler_params=pltpu.CompilerParams(
            collective_id=0, has_side_effects=True, vmem_limit_bytes=61 * 1024 * 1024
        ),
        name="layer",
    )(offsets, pad_count, tiles, w_qkv, w_out, cotangent)
    return pl.pallas_call(
        copy_kernel, out_shape=shapes, in_specs=[vm] * 4, out_specs=(hbm,) * 4, scratch_shapes=[dma((4,))],
        name="results"
    )(*(pltpu.with_memory_space_constraint(o, pltpu.VMEM) for o in outs))


def solution(mesh):
    row = P("ctx", None)
    return jax.shard_map(
        per_device,
        mesh=mesh,
        in_specs=(row, P(), P(), row, P(), P()),
        out_specs=(row, row, row, row),
        check_vma=False,
    )
```

```python
import jax
import jax.numpy as jnp
from jax import lax
from jax.experimental import pallas as pl
from jax.experimental.pallas import tpu as pltpu
from jax.sharding import PartitionSpec as P

MESH = pl.DeviceIdType.MESH
N = 256
D = 768
H = 12
E = 64
NEG = -1e30
F32 = jnp.float32
BF = jnp.bfloat16
I32 = jnp.int32


def dot(a, b, ca, cb, precision=None):
    dims = (((ca,), (cb,)), ((), ()))
    return lax.dot_general(a, b, dims, precision=precision, preferred_element_type=F32)


def nn(a, b):
    return dot(a, b, 1, 0)


def nt(a, b):
    return dot(a, b, 1, 1)


def tn(a, b):
    return dot(a, b, 0, 0)


def iota(shape, dim):
    return lax.broadcasted_iota(I32, shape, dim)


def head_mask(h, dtype):
    return jnp.where(iota((1, D), 1) // E == h, 1.0, 0.0).astype(dtype)


def block_diag(x):
    return jnp.concatenate([x * head_mask(h, x.dtype) for h in range(H)], axis=0)


def diag_sum(x, rows):
    head = iota((rows, D), 1) // E
    out = jnp.zeros((rows, D), F32)
    for h in range(H):
        out = jnp.where(head == h, x[h * rows : (h + 1) * rows], out)
    return out


def per_head(cols, rows):
    head = iota((rows, D), 1) // E
    out = jnp.zeros((rows, D), F32)
    for h in range(H):
        out = jnp.where(head == h, cols[h * rows : (h + 1) * rows], out)
    return out


def kernel(
    offs_h, pad_h, tiles_h, wqkv_h, wout_h, cot_h,
    out_rows, grad_tiles, g_qkv, g_out,
    offs, pad, tiles, wqkv, wout, cot,
    pk, midm, farm, nfar, sel1, sel2, hsel, emat, dsm, num, den, mx,
    gkv, gqd, gst, far1kv, far1qd, far1st, far2kv, far2qd, far2st,
    floc, mnum, mden, mmax, fnum, fden, fmax, emid, efar,
    attn, sdo, npr, mlse, mprod, flse, fprod, fat, fsc,
    dq, dk, dv, dmid, dfar, gp, tilest, tilesp, attnt, cotr, perm, gph, gpr,
    part, r1, tmp, r2, acc, s2, tot, fin, finr,
    stage, pz, z1, zt, z2, zacc, zs, zf, zm,
    ls_, os_, f1s, f1r, f2s, f2r, f3s, f3r, m1s, m1r, m2s, m2r,
    xs, xr, rs, rr_, ss, sr, es_, er_,
    zrs, zrr, zss, zsr, zms, zmr,
):
    me = lax.axis_index("ctx")
    c = me % 2
    z = me // 2 % 4
    g = me // 8
    x = g // 4
    y = g % 4
    mate = g * 8 + z * 2 + (1 - c)

    def zpeer(k):
        return g * 8 + (z + k) % 4 * 2 + c

    def gpeer(k):
        return (g + k) % 16 * 8 + z * 2 + c

    def rc(src, dst, ss, rs, dev):
        return pltpu.make_async_remote_copy(
            src_ref=src, dst_ref=dst, send_sem=ss, recv_sem=rs, device_id=(dev,), device_id_type=MESH
        )

    def load(src, dst, n):
        return pltpu.make_async_copy(src, dst, ls_.at[n])

    loads = [load(tiles_h, tiles, 0)]
    for i in range(3):
        for a in (1, 2):
            cols = pl.ds(a * D + i * N, N)
            loads.append(load(wqkv_h.at[:, cols], wqkv.at[:, cols], 1 + i))
    later = [
        load(wqkv_h.at[:, pl.ds(0, D)], wqkv.at[:, pl.ds(0, D)], 4),
        load(cot_h, cot, 5),
        load(wout_h, wout, 6),
    ]
    small = (load(offs_h, offs, 7), load(pad_h, pad, 8))
    for item in small:
        item.start()
    for item in loads:
        item.start()
    barrier = pltpu.get_barrier_semaphore()
    peers = [mate] + [zpeer(k) for k in (1, 2, 3)] + [gpeer(k) for k in range(1, 16)]
    peers += [g * 8 + (z + k) % 4 * 2 + (1 - c) for k in (1, 2, 3)]
    for p in peers:
        pl.semaphore_signal(barrier, inc=1, device_id=(p,), device_id_type=MESH)

    FAR1 = (far1kv, far1qd, far1st)
    FAR2 = (far2kv, far2qd, far2st)
    MID = (gkv, gqd, gst)

    def f1_copy(t, k):
        return rc(FAR1[t].at[z], FAR1[t].at[z], f1s.at[t], f1r.at[t], zpeer(k))

    def f1_all(t):
        some = FAR1[t].at[pl.ds(0, 3)]
        return rc(some, some, f1s.at[t], f1r.at[t], zpeer(1))

    def f1_start(t):
        for k in (1, 3, 2):
            f1_copy(t, k).start()

    def f1_wait(t):
        f1_all(t).wait_recv()

    def f2_copy(t, k):
        return rc(FAR2[t].at[c, g], FAR2[t].at[c, g], f2s.at[t], f2r.at[t], gpeer(k))

    def f2_all(t):
        some = FAR2[t].at[c, pl.ds(0, 15)]
        return rc(some, some, f2s.at[t], f2r.at[t], gpeer(1))

    def f2_start(t):
        a = FAR1[t]
        FAR2[t][c, g] = (
            a[0].astype(F32) + a[1].astype(F32) + a[2].astype(F32) + a[3].astype(F32)
        ).astype(a.dtype)
        for k in range(1, 16):
            f2_copy(t, k).start()

    def f2_wait(t):
        f2_all(t).wait_recv()

    def f3_copy(t):
        return rc(FAR2[t].at[c], FAR2[t].at[c], f3s.at[t], f3r.at[t], mate)

    def f3_wait(t):
        rc(FAR2[t].at[1 - c], FAR2[t].at[1 - c], f3s.at[t], f3r.at[t], mate).wait_recv()

    def m1_copy(t, k):
        return rc(MID[t].at[c, z], MID[t].at[c, z], m1s.at[t], m1r.at[t], zpeer(k))

    def m1_all(t):
        some = MID[t].at[c, pl.ds(0, 3)]
        return rc(some, some, m1s.at[t], m1r.at[t], zpeer(1))

    def m2_copy(t, k):
        o = (z + k) % 4
        return rc(MID[t].at[c, o], MID[t].at[c, o], m2s.at[t], m2r.at[t], mate)

    def m2_all(t, who):
        return rc(MID[t].at[who], MID[t].at[who], m2s.at[t], m2r.at[t], mate)

    def m1_start(t):
        for k in (1, 3, 2):
            m1_copy(t, k).start()
        m2_copy(t, 0).start()

    def m1_forward(t):
        m1_all(t).wait_recv()
        for k in (1, 3, 2):
            m2_copy(t, k).start()

    def m2_wait(t):
        m2_all(t, 1 - c).wait_recv()

    def to_mate(t, src, dst):
        return rc(src, dst, xs.at[t], xr.at[t], mate)

    half_cols = pl.ds(pl.multiple_of(384 * (1 - c), 128), 384)
    own_cols = pl.ds(pl.multiple_of(384 * c, 128), 384)

    for item in small:
        item.wait()
    limit = N * 128 - pad[0]
    lane_head = iota((1, D), 1) // E
    o0 = jnp.zeros((1, D), I32)
    o1 = jnp.zeros((1, D), I32)
    for h in range(H):
        o0 = jnp.where(lane_head == h, offs[0, h], o0)
        o1 = jnp.where(lane_head == h, offs[1, h], o1)
    midm[...] = jnp.where(iota((N, D), 0) % 8 == o0, 1.0, 0.0).astype(BF)
    farm[...] = jnp.where(iota((N, D), 0) % 128 == o1, 1.0, 0.0).astype(BF)

    nfar[...] = jnp.where(iota((N, D), 0) % 128 == o1, 0.0, 1.0).astype(BF)
    r0 = iota((D, 128), 0)
    l0 = iota((D, 128), 1)
    sel1[...] = jnp.where(jnp.logical_and(r0 == l0 * E, l0 < H), 1.0, 0.0).astype(BF)
    sel2[...] = jnp.where(r0 // E == l0 - H, 1.0, 0.0).astype(BF)
    hsel[...] = jnp.where(iota((16, D), 1) // E == iota((16, D), 0), 1.0, 0.0)
    pool_mid = jnp.where(iota((32, N), 1) // 8 == iota((32, N), 0), 1.0, 0.0).astype(BF)
    two = iota((16, N), 1) // 128
    row = iota((16, N), 0)
    pool_far = jnp.where(row == two, 1.0, 0.0)
    none = jnp.zeros_like(pool_far)
    far_a = [jnp.where(row == 2 * z + two, 1.0, 0.0), pool_far, none]
    far_b = [jnp.where(row == 8 + 2 * z + two, 1.0, 0.0), none, pool_far]
    far_a = jnp.concatenate(far_a, axis=0).astype(BF)
    far_b = jnp.concatenate(far_b, axis=0).astype(BF)

    def picks(t, i, a, b):
        ls = pl.ds(pl.multiple_of(i * N, N), N)
        hi = pl.ds(pl.multiple_of(D + i * N, N), N)
        mk = midm[:, ls]
        fk = farm[:, ls]
        rows = (nn(far_a, a * fk) + nn(far_b, b * fk)).astype(BF)
        FAR1[t][z, :, ls] = rows[0:16]
        MID[t][c, z, :, ls] = nn(pool_mid, a * mk).astype(BF)
        MID[t][c, z, :, hi] = nn(pool_mid, b * mk).astype(BF)
        floc[2 * t, :, ls] = rows[16:32]
        floc[2 * t + 1, :, ls] = rows[32:48]

    loads[0].wait()

    for i in range(3):
        cols = pl.ds(i * 2 * N, 2 * N)
        load(wqkv_h.at[:, cols], wqkv.at[:, cols], 1 + i).wait()
        if i == 0:
            for item in later:
                item.start()
        kc = pl.ds(D + i * N, N)
        vc = pl.ds(2 * D + i * N, N)
        kk = nn(tiles[...], wqkv[:, kc]).astype(BF)
        vv = nn(tiles[...], wqkv[:, vc]).astype(BF)
        pk[:, kc] = kk
        pk[:, vc] = vv
        picks(0, i, kk, vv)

    pl.semaphore_wait(barrier, len(peers))
    f1_start(0)
    for item in later:
        item.wait()
    to_mate(0, cot.at[:, half_cols], cotr).start()

    for i in range(3):
        if i == 1:
            m1_start(0)
        qc = pl.ds(i * N, N)
        dc = pl.ds(3 * D + i * N, N)
        qq = nn(tiles[...], wqkv[:, qc]).astype(BF) * jnp.asarray(0.125, BF)
        dd = nt(cot[...], wout[qc, :]).astype(BF)
        pk[:, qc] = qq
        pk[:, dc] = dd
        picks(1, i, qq, dd)


    half = iota((1, 128), 1) // E
    hm = [jnp.where(half == a, 1.0, 0.0).astype(BF) for a in range(2)]

    def lanes(p, base=0):
        return pl.ds(pl.multiple_of(base + p * 128, 128), 128)

    def near_forward(lo, hi):
        @pl.loop(lo, hi, unroll=2)
        def _(p):
            q2 = pk[:, lanes(p)]
            k2 = pk[:, lanes(p, D)]
            v2 = pk[:, lanes(p, 2 * D)]
            bias = jnp.where(me * N + iota((1, N), 1) < limit, 0.0, NEG)
            es, ms = [], []
            for a in range(2):
                s = nt(q2 * hm[a], k2) + bias
                m = jnp.max(s, axis=1, keepdims=True)
                e = jnp.exp(s - m).astype(BF)
                emat[2 * p + a] = e
                es.append(e)
                ms.append(m)
            rhs = jnp.concatenate(
                [
                    jnp.concatenate([v2 * hm[a], jnp.broadcast_to(hm[a], (N, 128))], axis=1)
                    for a in range(2)
                ],
                axis=0,
            )
            nd = nn(jnp.concatenate(es, axis=1), rhs)
            num[:, lanes(p)] = nd[:, :128]
            den[:, lanes(p)] = nd[:, 128:]
            mx[:, lanes(p)] = jnp.where(iota((N, 128), 1) < E, ms[0], ms[1])

    f1_wait(0)
    f2_start(0)
    near_forward(0, 6)
    tilest[c] = tiles[...].T
    m1_forward(0)
    f1_start(1)
    m1_start(1)
    to_mate(1, tilest.at[c], tilest.at[c]).start()
    pr = iota((D, D), 0)
    want = pr // 12 % 16 * 48 + pr // 192 * 12 + pr % 12
    perm[...] = jnp.where(iota((D, D), 1) == want, 1.0, 0.0).astype(BF)
    tilesp[c] = nt(perm[...], tiles[...]).astype(BF)
    to_mate(6, tilesp.at[c], tilesp.at[c]).start()

    m2_wait(0)
    kg = gkv[:, :, :, :D].reshape(N, D)
    vg = gkv[:, :, :, D:].reshape(N, D)
    gdev = g * 8 + iota((32, N), 1) // 32 % 4 * 2 + iota((32, N), 1) // 128
    gpos = gdev * N + iota((32, N), 1) % 32 * 8
    gbias = jnp.concatenate(
        [jnp.where(gpos + offs[0, h] < limit, 0.0, NEG) for h in range(H)], axis=0
    )
    s = nt(block_diag(gqd[c, z, :, :D]), kg) + gbias
    m = jnp.max(s, axis=1, keepdims=True)
    e = jnp.exp(s - m)
    total = jnp.sum(e, axis=1, keepdims=True)
    e = e.astype(BF)
    emid[...] = e
    mnum[...] = diag_sum(nn(e, vg), 32)
    mden[...] = per_head(total, 32)
    mmax[...] = per_head(m, 32)

    f2_wait(0)
    f3_copy(0).start()

    def spread_mid(x):
        return jnp.broadcast_to(x[:, None, :], (32, 8, 128)).reshape(N, 128)

    def spread_far(x):
        return jnp.concatenate(
            [jnp.broadcast_to(x[0:1], (128, 128)), jnp.broadcast_to(x[1:2], (128, 128))], axis=0
        )

    def pick_mid(x):
        return jnp.sum(x.reshape(32, 8, 128), axis=1)

    def pick_far(x):
        return jnp.concatenate(
            [
                jnp.sum(x[:128], axis=0, keepdims=True),
                jnp.sum(x[128:], axis=0, keepdims=True),
            ],
            axis=0,
        )

    @pl.loop(0, 6, unroll=2)
    def _(p):
        ls = lanes(p)
        mm = midm[:, ls].astype(F32)
        fm = farm[:, ls].astype(F32)
        m0 = mx[:, ls]
        m1 = jnp.where(mm > 0.5, spread_mid(mmax[:, ls]), NEG)
        top = jnp.maximum(m0, m1)
        w0 = jnp.exp(m0 - top)
        w1 = jnp.exp(m1 - top)
        total = w0 * den[:, ls] + w1 * spread_mid(mden[:, ls])
        inv = 1.0 / total
        exact = (w0 * num[:, ls] + w1 * spread_mid(mnum[:, ls])) * inv
        at = exact.astype(BF)
        attn[:, ls] = at
        do = pk[:, lanes(p, 3 * D)].astype(F32)
        prod = do * at.astype(F32)
        scale = w0 * inv
        sdo[:, ls] = (scale * do).astype(BF)
        npr[:, ls] = (-scale * prod).astype(BF)
        lse = top + jnp.log(total)
        mlse[:, ls] = pick_mid(lse * mm)
        mprod[:, ls] = pick_mid(prod * mm)
        flse[0:2, ls] = pick_far(lse * fm)
        fat[0:2, ls] = pick_far(exact * fm)
        fsc[0:2, ls] = pick_far(scale * fm)

    f3_wait(0)

    heads = hsel[...]
    headb = heads.astype(BF)

    def far_diag(v):
        return jnp.concatenate([v[0:1] * headb, v[1:2] * headb], axis=0)

    def far_fold(v):
        return jnp.concatenate(
            [jnp.sum(v[16 * r : 16 * r + 16] * heads, axis=0, keepdims=True) for r in range(2)],
            axis=0,
        )

    col = iota((16, 512), 1)
    fdev = col // 16 % 16 * 8 + col // 2 % 4 * 2 + col // 256
    fpos = (fdev * 2 + col % 2) * 128
    lead = col // 8 % 2 == 0
    off_col = jnp.zeros((16, 512), I32)
    for h in range(H):
        off_col = jnp.where(iota((16, 512), 0) == h, offs[1, h], off_col)
    fbias = jnp.where(jnp.logical_and(lead, fpos + off_col < limit), 0.0, NEG)
    fbias = jnp.concatenate([fbias, fbias], axis=0)
    kvf = far2kv[...].reshape(512, D)
    s = nt(far_diag(floc[2]), kvf) + fbias
    m = jnp.max(s, axis=1, keepdims=True)
    e = jnp.exp(s - m)
    efar[...] = e
    fnum[0:2] = far_fold(nn(pltpu.roll(e, 8, 1).astype(BF), kvf))
    fden[0:2] = far_fold(jnp.broadcast_to(jnp.sum(e, axis=1, keepdims=True), (32, D)))
    fmax[0:2] = far_fold(jnp.broadcast_to(m, (32, D)))

    f1_wait(1)
    f2_start(1)
    a_lse = flse[0:2]
    b_lse = fmax[0:2] + jnp.log(fden[0:2])
    top = jnp.maximum(a_lse, b_lse)
    n_lse = top + jnp.log(jnp.exp(a_lse - top) + jnp.exp(b_lse - top))
    wa = jnp.exp(a_lse - n_lse)
    n_at = (wa * fat[0:2] + jnp.exp(b_lse - n_lse) * fnum[0:2] / fden[0:2]).astype(BF)
    f_do = floc[3, 0:2].astype(F32)
    n_prod = f_do * n_at.astype(F32)
    scale = fsc[0:2] * wa
    n_sdo = scale * f_do
    n_npr = -scale * n_prod
    flse[...] = jnp.concatenate([n_lse, jnp.zeros((14, D), F32)], axis=0)
    fprod[...] = jnp.concatenate([n_prod, jnp.zeros((14, D), F32)], axis=0)
    for p in range(6):
        ls = slice(p * 128, p * 128 + 128)
        keep = nfar[:, ls]
        take = farm[:, ls]
        for ref, new in ((attn, n_at.astype(F32)), (sdo, n_sdo), (npr, n_npr)):
            ref[:, ls] = ref[:, ls] * keep + spread_far(new[:, ls]).astype(BF) * take
    g32 = iota((32, D), 0)
    for r in range(2):
        both = jnp.logical_and(g32 == r * 16 + o1 // 8, o1 % 8 == o0)
        mlse[...] = jnp.where(both, n_lse[r : r + 1], mlse[...])
        mprod[...] = jnp.where(both, n_prod[r : r + 1], mprod[...])

    lse_rows = jnp.concatenate([mlse[...], flse[...]], axis=0)
    prod_rows = jnp.concatenate([mprod[...], fprod[...]], axis=0)
    l_hi = lse_rows.astype(BF)
    left = lse_rows - l_hi.astype(F32)
    l_mid = left.astype(BF)
    l_lo = (left - l_mid.astype(F32)).astype(BF)
    p_hi = prod_rows.astype(BF)
    p_lo = (prod_rows - p_hi.astype(F32)).astype(BF)
    lt = nn(jnp.concatenate([l_hi, l_mid, l_lo], axis=0), sel1[...])
    pt = nn(jnp.concatenate([p_hi, p_lo], axis=0), sel2[...])
    st = lt[0:48] + lt[48:96] + lt[96:144] + pt[0:48] + pt[48:96]
    gst[c, z] = st[0:32]
    fs = st[32:48]
    r8 = iota((8, 128), 0)
    far1st[z] = jnp.where(r8 == 2 * z, fs[0:1], jnp.where(r8 == 2 * z + 1, fs[1:2], 0.0))
    f1_start(2)
    m1_start(2)

    attnt[c] = nt(perm[...], attn[...]).astype(BF)
    to_mate(2, attnt.at[c], attnt.at[c]).start()
    turn = [c, 1 - c]

    def put_part(b, v):
        v = v.astype(BF).reshape(4, 4, 48, 384)
        for i in range(4):
            for j in range(4):
                skip = (j - i) * turn[b]
                part[b, i + skip, j - skip] = v[i, j]

    def dev(x_, y_):
        return ((x_ % 4 * 4 + y_ % 4) * 4 + z) * 2 + c

    first = [x + (y - x) * turn[b] for b in range(2)]
    other = [y + (x - y) * turn[b] for b in range(2)]

    def along(b, k):
        return dev(x + k * (1 - turn[b]), y + k * turn[b])

    def across(b, k):
        return dev(x + k * turn[b], y + k * (1 - turn[b]))

    def where_in(b, q, h):
        return (b, q, slice(None) if h is None else pl.ds(2 * h, 2))

    def ring_copy(b, n):
        p = first[b]
        nxt, prv = along(b, 1), along(b, 3)
        up, down, far = (p + 1) % 4, (p + 3) % 4, (p + 2) % 4
        src, dst, to = (
            lambda: (part.at[where_in(b, far, 0)], r1.at[b, 0], nxt),
            lambda: (part.at[where_in(b, far, 1)], r1.at[b, 1], prv),
            lambda: (part.at[where_in(b, up, 1)], r2.at[b, 0, pl.ds(2, 2)], nxt),
            lambda: (part.at[where_in(b, down, 0)], r2.at[b, 1, pl.ds(0, 2)], prv),
            lambda: (tmp.at[b, 0], r2.at[b, 0, pl.ds(0, 2)], nxt),
            lambda: (tmp.at[b, 1], r2.at[b, 1, pl.ds(2, 2)], prv),
        )[n]()
        return rc(src, dst, rs.at[b], rr_.at[b, min(n, 2)], to)

    def ring_a(b):
        for n in range(4):
            ring_copy(b, n).start()

    def ring_b(b):
        p = first[b]
        for h, q in ((0, (p + 1) % 4), (1, (p + 3) % 4)):
            ring_copy(b, h).wait_recv()
            tmp[b, h] = (part[where_in(b, q, h)].astype(F32) + r1[b, h].astype(F32)).astype(BF)
            ring_copy(b, 4 + h).start()

    def second(b, k):
        q = (other[b] + k) % 4
        return rc(acc.at[b, q], s2.at[b, other[b]], ss.at[b], sr.at[b], across(b, k))

    def second_all(b):
        some = s2.at[b, pl.ds(0, 3)]
        return rc(some, some, ss.at[b], sr.at[b], mate)

    def ring_c(b):
        rc(r2.at[b], r2.at[b], rs.at[b], rr_.at[b, 2], mate).wait_recv()
        mine = part[where_in(b, first[b], None)].astype(F32)
        acc[b] = (mine + r2[b, 0].astype(F32) + r2[b, 1].astype(F32)).astype(BF)
        for k in (2, 1, 3):
            second(b, k).start()

    def ring_d(b):
        total = acc[b, other[b]].astype(F32)
        second_all(b).wait_recv()
        for k in (1, 3, 2):
            total = total + s2[b, (other[b] + k) % 4].astype(F32)
        tot[b] = total.astype(BF)

    own = z * 2 + c
    er = iota((128, 96), 0)
    ek = er % 8
    spread = jnp.where(
        jnp.logical_and(iota((128, 96), 1) == er // 8 % 2 * 48 + er // 16 * 6 + ek, ek < 6), 1.0, 0.0
    ).astype(BF)

    def fin_copy(k):
        o = (own + k) % 8
        return rc(fin.at[o], finr.at[own], es_.at[0], er_.at[0], g * 8 + o)

    def fin_all():
        some = finr.at[pl.ds(0, 7)]
        return rc(some, some, es_.at[0], er_.at[0], mate)

    def fin_start(_):
        fin[...] = nn(spread, tot[...].reshape(96, 384)).astype(BF).reshape(8, 16, 384)
        for k in range(1, 8):
            fin_copy(k).start()
        finr[own] = fin[own]

    def fin_end(_):
        fin_all().wait_recv()
        for a in range(2):
            v = finr[a].astype(F32)
            for o in (2, 4, 6):
                v = v + finr[o + a].astype(F32)
            for i in range(2):
                at = (1 + i) * D + 384 * a
                g_qkv[:, at : at + 384] = v[8 * i : 8 * i + 6]

    def put_z(b, v):
        pz[b] = v.astype(BF).reshape(4, 4, 48, 384)

    def z_copy(b, n):
        nxt, prv = zpeer(1), zpeer(3)
        up, down, far = (z + 1) % 4, (z + 3) % 4, (z + 2) % 4
        lo, hi = pl.ds(0, 2), pl.ds(2, 2)
        src, dst, to = (
            lambda: (pz.at[b, far, lo], z1.at[b, 0], nxt),
            lambda: (pz.at[b, far, hi], z1.at[b, 1], prv),
            lambda: (pz.at[b, up, hi], z2.at[b, 0, hi], nxt),
            lambda: (pz.at[b, down, lo], z2.at[b, 1, lo], prv),
            lambda: (zt.at[b, 0], z2.at[b, 0, lo], nxt),
            lambda: (zt.at[b, 1], z2.at[b, 1, hi], prv),
        )[n]()
        return rc(src, dst, zrs.at[b], zrr.at[b, min(n, 2)], to)

    def z_a(b):
        for n in range(4):
            z_copy(b, n).start()

    def z_b(b):
        for h, q in ((0, (z + 1) % 4), (1, (z + 3) % 4)):
            z_copy(b, h).wait_recv()
            mine = pz[b, q, 2 * h : 2 * h + 2].astype(F32)
            zt[b, h] = (mine + z1[b, h].astype(F32)).astype(BF)
            z_copy(b, 4 + h).start()

    def z_second(b, k):
        return rc(zacc.at[b, (g + k) % 16], zs.at[b, g], zss.at[b], zsr.at[b], gpeer(k))

    def z_second_all(b):
        some = zs.at[b, pl.ds(0, 15)]
        return rc(some, some, zss.at[b], zsr.at[b], mate)

    def z_c(b):
        rc(z2.at[b], z2.at[b], zrs.at[b], zrr.at[b, 2], mate).wait_recv()
        mine = pz[b, z].astype(F32)
        mine = mine + z2[b, 0].astype(F32) + z2[b, 1].astype(F32)
        stage[0:192] = mine.reshape(192, 384)
        for i in range(16):
            zacc[b, i] = stage[12 * i : 12 * i + 16].astype(BF)
        for k in range(1, 16):
            z_second(b, k).start()

    def z_mate(b):
        return rc(zf.at[b], zm.at[b], zms.at[b], zmr.at[b], mate)

    def z_d(b):
        z_second_all(b).wait_recv()
        total = zacc[b, g].astype(F32)
        for k in range(1, 16):
            total = total + zs[b, (g + k) % 16].astype(F32)
        zf[b] = total
        z_mate(b).start()

    def z_e(b):
        z_mate(b).wait_recv()
        target = (g_out, g_qkv)[b]
        for ref, half in ((zf, c), (zm, 1 - c)):
            v = ref[b]
            cols = pl.ds(pl.multiple_of(384 * half, 128), 384)
            target[:, cols] = jnp.where(c == 0, v[0:6], v[6:12])

    def backward_queries(lo, hi):
        @pl.loop(lo, hi, unroll=2)
        def _(p):
            ls = lanes(p)
            k2 = pk[:, lanes(p, D)]
            so = sdo[:, ls]
            sp = npr[:, ls]
            rhs = jnp.concatenate([pk[:, lanes(p, 2 * D)], jnp.ones((N, 128), BF)], axis=1)
            ds = []
            for a in range(2):
                lhs = jnp.concatenate([so * hm[a], sp * hm[a]], axis=1)
                d = (emat[2 * p + a].astype(F32) * nt(lhs, rhs)).astype(BF)
                dsm[2 * p + a] = d
                ds.append(d)
            dq[:, ls] = 0.125 * nn(
                jnp.concatenate(ds, axis=1), jnp.concatenate([k2 * hm[0], k2 * hm[1]], axis=0)
            )

    def backward_keys(lo, hi):
        @pl.loop(lo, hi, unroll=2)
        def _(p):
            ls = lanes(p)
            q2 = pk[:, ls]
            so = sdo[:, ls]
            dk[:, ls] = tn(
                jnp.concatenate([dsm[2 * p], dsm[2 * p + 1]], axis=0),
                jnp.concatenate([q2 * hm[0], q2 * hm[1]], axis=0),
            )
            dv[:, ls] = tn(
                jnp.concatenate([emat[2 * p], emat[2 * p + 1]], axis=0),
                jnp.concatenate([so * hm[0], so * hm[1]], axis=0),
            )

    backward_queries(0, 4)
    m1_forward(1)
    to_mate(0, cotr, cotr).wait_recv()
    to_mate(2, attnt.at[1 - c], attnt.at[1 - c]).wait_recv()
    put_z(0, nn(attnt[c], cot[:, own_cols]) + nn(attnt[1 - c], cotr[...]))
    z_a(0)
    f1_wait(2)
    f2_start(2)
    backward_queries(4, 6)
    m1_forward(2)

    kg = gkv[:, :, :, :D].reshape(N, D)
    vg = gkv[:, :, :, D:].reshape(N, D)
    scale = jnp.exp(mmax[...] - mlse[...])
    so = (scale * gqd[c, z, :, D:].astype(F32)).astype(BF)
    sp = scale * mprod[...]
    dl = jnp.concatenate(
        [jnp.sum(sp * head_mask(h, F32), axis=1, keepdims=True) for h in range(H)], axis=0
    )
    ds = (emid[...].astype(F32) * (nt(block_diag(so), vg) - dl)).astype(BF)
    dmid[0] = 0.125 * diag_sum(nn(ds, kg), 32)

    scale = jnp.exp(fmax[0:2] - flse[0:2])
    so = (scale * floc[3, 0:2].astype(F32)).astype(BF)
    sp = scale * fprod[0:2]
    dl = jnp.concatenate(
        [jnp.sum(sp[r : r + 1] * heads, axis=1, keepdims=True) for r in range(2)], axis=0
    )
    kvf = far2kv[...].reshape(512, D)
    t = pltpu.roll(nt(far_diag(so), kvf), 504, 1)
    dfar[0, 0:2] = 0.125 * far_fold(nn((efar[...] * (t - dl)).astype(BF), kvf))

    def grad_part(a, near):
        @pl.loop(0, 6)
        def _(p):
            ls = lanes(p)
            mm = midm[:, ls].astype(F32)
            fm = farm[:, ls].astype(F32)
            v = near[:, ls] + mm * spread_mid(dmid[a, :, ls]) + fm * spread_far(dfar[a, 0:2, ls])
            v = v.astype(BF)
            gp[:, lanes(p, a * D)] = v
            gph[a, p // 3, :, lanes(p % 3)] = v

        to_mate(3 + a, gph.at[a, 1 - c], gpr.at[a]).start()

    def weight_part(a):
        to_mate(3 + a, gpr.at[a], gpr.at[a]).wait_recv()
        rows = tilest if a else tilesp
        v = nn(rows[c], gph[a, c]) + nn(rows[1 - c], gpr[a])
        if a == 0:
            put_z(1, v)
        else:
            put_part(a - 1, v)
            ring_a(a - 1)

    grad_part(0, dq)
    backward_keys(0, 4)
    f2_wait(1)
    f3_copy(1).start()
    to_mate(1, tilest.at[1 - c], tilest.at[1 - c]).wait_recv()
    to_mate(6, tilesp.at[1 - c], tilesp.at[1 - c]).wait_recv()
    z_b(0)
    weight_part(0)
    backward_keys(4, 6)
    f2_wait(2)
    f3_copy(2).start()
    m2_wait(1)
    m2_wait(2)

    st = gst[...].reshape(N, 128).T
    ls_rows = st[0:16]
    dl_rows = st[12:28]
    qg = gqd[:, :, :, :D].reshape(N, D)
    og = gqd[:, :, :, D:].reshape(N, D)
    s = nt(block_diag(gkv[c, z, :, :D]), qg)
    t = nt(block_diag(gkv[c, z, :, D:]), og)
    ps, dss = [], []
    for h in range(H):
        ok = me * N + iota((32, N), 0) * 8 + offs[0, h] < limit
        p = jnp.exp(jnp.where(ok, s[h * 32 : (h + 1) * 32] - ls_rows[h : h + 1], NEG))
        ps.append(p.astype(BF))
        dss.append((p * (t[h * 32 : (h + 1) * 32] - dl_rows[h : h + 1])).astype(BF))
    dmid[1] = diag_sum(nn(jnp.concatenate(dss, axis=0), qg), 32)
    pmid = jnp.concatenate(ps, axis=0)

    f3_wait(1)
    f3_wait(2)
    st = far2st[...].reshape(32, 8, 128)
    st = jnp.concatenate([st, jnp.zeros_like(st)], axis=1).reshape(512, 128).T
    ls_rows = jnp.concatenate([st[0:16], st[0:16]], axis=0)
    dl_rows = jnp.concatenate([st[12:28], st[12:28]], axis=0)
    qdf = far2qd[...].reshape(512, D)
    s = nt(far_diag(floc[0]), qdf)
    t = pltpu.roll(nt(far_diag(floc[1]), qdf), 504, 1)
    row_h = iota((16, 512), 0)
    oks = [
        jnp.logical_and(
            jnp.logical_and(lead, row_h < H), (me * 2 + r) * 128 + off_col < limit
        )
        for r in range(2)
    ]
    expo = jnp.concatenate(
        [jnp.where(oks[r], (s - ls_rows)[16 * r : 16 * r + 16], NEG) for r in range(2)], axis=0
    )
    pfar = jnp.exp(expo)
    dfar[1, 0:2] = far_fold(nn((pfar * (t - dl_rows)).astype(BF), qdf))
    grad_part(1, dk)
    dmid[2] = diag_sum(nn(pmid, og), 32)
    dfar[2, 0:2] = far_fold(nn(pltpu.roll(pfar, 8, 1).astype(BF), qdf))
    z_c(0)
    z_a(1)
    grad_part(2, dv)
    weight_part(1)
    weight_part(2)

    @pl.loop(0, 3)
    def _(i):
        ls = pl.ds(pl.multiple_of(i * N, N), N)
        out_rows[:, ls] = (tiles[:, ls].astype(F32) + nn(attn[...], wout[:, ls])).astype(BF)
        grad_tiles[:, ls] = nt(gp[...], wqkv[ls, :]).astype(BF)

    z_b(1)
    ring_b(0)
    ring_b(1)
    z_c(1)
    ring_c(0)
    ring_c(1)
    z_d(0)
    ring_d(0)
    ring_d(1)
    fin_start(1)
    z_d(1)
    z_e(0)
    z_e(1)
    fin_end(1)

    to_mate(0, cot.at[:, half_cols], cotr).wait_send()
    to_mate(1, tilest.at[c], tilest.at[c]).wait_send()
    to_mate(6, tilesp.at[c], tilesp.at[c]).wait_send()
    to_mate(2, attnt.at[c], attnt.at[c]).wait_send()
    for a in range(3):
        to_mate(3 + a, gph.at[a, 1 - c], gpr.at[a]).wait_send()
    for b in range(2):
        some = part.at[b, pl.ds(0, 3)]
        rc(some, some, rs.at[b], rr_.at[b, 2], mate).wait_send()
        second_all(b).wait_send()
        some = pz.at[b, pl.ds(0, 3)]
        rc(some, some, zrs.at[b], zrr.at[b, 2], mate).wait_send()
        z_second_all(b).wait_send()
        z_mate(b).wait_send()
    fin_all().wait_send()
    for t in range(3):
        f1_all(t).wait_send()
        m1_all(t).wait_send()
        f2_all(t).wait_send()
        f3_copy(t).wait_send()
        m2_all(t, c).wait_send()


def copy_kernel(*refs):
    sems = refs[8]
    copies = [pltpu.make_async_copy(refs[i], refs[4 + i], sems.at[i]) for i in range(4)]
    for item in copies:
        item.start()
    for item in copies:
        item.wait()


def per_device(tiles, w_qkv, w_out, cotangent, offsets, pad_count):
    vm = pl.BlockSpec(memory_space=pltpu.VMEM)
    hbm = pl.BlockSpec(memory_space=pl.ANY)
    V = pltpu.VMEM
    dma = pltpu.SemaphoreType.DMA
    big = V((N, D), F32)
    bigb = V((N, D), BF)
    m32 = V((32, D), F32)
    f16 = V((16, D), F32)
    shapes = (
        jax.ShapeDtypeStruct((N, D), BF),
        jax.ShapeDtypeStruct((N, D), BF),
        jax.ShapeDtypeStruct((6, 3 * D), F32),
        jax.ShapeDtypeStruct((6, D), F32),
    )
    outs = pl.pallas_call(
        kernel,
        out_shape=tuple(V(a.shape, a.dtype) for a in shapes),
        in_specs=[hbm] * 6,
        out_specs=(vm,) * 4,
        scratch_shapes=[
            pltpu.SMEM((2, H), I32), pltpu.SMEM((1,), I32),
            bigb, V((D, 3 * D), BF), V((D, D), BF), bigb,
            V((N, 4 * D), BF), bigb, bigb, bigb, V((D, 128), BF), V((D, 128), BF), f16,
            V((H, N, N), BF), V((H, N, N), BF), big, big, big,
            V((2, 4, 32, 2 * D), BF), V((2, 4, 32, 2 * D), BF), V((2, 4, 32, 128), F32),
            V((4, 16, D), BF), V((4, 16, D), BF), V((4, 8, 128), F32),
            V((2, 16, 16, D), BF), V((2, 16, 16, D), BF), V((2, 16, 8, 128), F32),
            V((4, 16, D), BF), m32, m32, m32, f16, f16, f16, V((H * 32, N), BF), V((32, 512), F32),
            bigb, bigb, bigb, m32, m32, f16, f16, f16, f16,
            big, big, big, V((3, 32, D), F32), V((3, 16, D), F32), V((N, 3 * D), BF),
            V((2, D, N), BF), V((2, D, N), BF), V((2, D, N), BF), V((N, 384), BF), V((D, D), BF),
            V((3, 2, N, 384), BF), V((3, N, 384), BF),
            V((2, 4, 4, 48, 384), BF),
            V((2, 2, 2, 48, 384), BF), V((2, 2, 2, 48, 384), BF), V((2, 2, 4, 48, 384), BF),
            V((2, 4, 48, 384), BF), V((2, 4, 48, 384), BF), V((2, 48, 384), BF),
            V((8, 16, 384), BF), V((8, 16, 384), BF),
            V((208, 384), F32), V((2, 4, 4, 48, 384), BF),
            V((2, 2, 2, 48, 384), BF), V((2, 2, 2, 48, 384), BF), V((2, 2, 4, 48, 384), BF),
            V((2, 16, 16, 384), BF), V((2, 16, 16, 384), BF), V((2, 16, 384), F32), V((2, 16, 384), F32),
            dma((9,)), dma((2,)),
            dma((3,)), dma((3,)), dma((3,)), dma((3,)), dma((3,)), dma((3,)),
            dma((3,)), dma((3,)), dma((3,)), dma((3,)),
            dma((7,)), dma((7,)), dma((2,)), dma((2, 3)), dma((2,)), dma((2,)),
            dma((1,)), dma((1,)),
            dma((2,)), dma((2, 3)), dma((2,)), dma((2,)), dma((2,)), dma((2,)),
        ],
        compiler_params=pltpu.CompilerParams(
            collective_id=0, has_side_effects=True, vmem_limit_bytes=61 * 1024 * 1024
        ),
        name="layer",
    )(offsets, pad_count, tiles, w_qkv, w_out, cotangent)
    return pl.pallas_call(
        copy_kernel, out_shape=shapes, in_specs=[vm] * 4, out_specs=(hbm,) * 4, scratch_shapes=[dma((4,))],
        name="results"
    )(*(pltpu.with_memory_space_constraint(o, pltpu.VMEM) for o in outs))


def solution(mesh):
    row = P("ctx", None)
    return jax.shard_map(
        per_device,
        mesh=mesh,
        in_specs=(row, P(), P(), row, P(), P()),
        out_specs=(row, row, row, row),
        check_vma=False,
    )
```

```python
import jax
import jax.numpy as jnp
from jax import lax
from jax.experimental import pallas as pl
from jax.experimental.pallas import tpu as pltpu
from jax.sharding import PartitionSpec as P

MESH = pl.DeviceIdType.MESH
N = 256
D = 768
H = 12
E = 64
NEG = -1e30
F32 = jnp.float32
BF = jnp.bfloat16
I32 = jnp.int32


def dot(a, b, ca, cb, precision=None):
    dims = (((ca,), (cb,)), ((), ()))
    return lax.dot_general(a, b, dims, precision=precision, preferred_element_type=F32)


def nn(a, b):
    return dot(a, b, 1, 0)


def nt(a, b):
    return dot(a, b, 1, 1)


def tn(a, b):
    return dot(a, b, 0, 0)


def iota(shape, dim):
    return lax.broadcasted_iota(I32, shape, dim)


def head_mask(h, dtype):
    return jnp.where(iota((1, D), 1) // E == h, 1.0, 0.0).astype(dtype)


def block_diag(x):
    return jnp.concatenate([x * head_mask(h, x.dtype) for h in range(H)], axis=0)


def diag_sum(x, rows):
    head = iota((rows, D), 1) // E
    out = jnp.zeros((rows, D), F32)
    for h in range(H):
        out = jnp.where(head == h, x[h * rows : (h + 1) * rows], out)
    return out


def per_head(cols, rows):
    head = iota((rows, D), 1) // E
    out = jnp.zeros((rows, D), F32)
    for h in range(H):
        out = jnp.where(head == h, cols[h * rows : (h + 1) * rows], out)
    return out


def kernel(
    offs_h, pad_h, tiles_h, wqkv_h, wout_h, cot_h,
    out_rows, grad_tiles, g_qkv, g_out,
    offs, pad, tiles, wqkv, wout, cot,
    pk, midm, farm, nfar, sel1, sel2, hsel, emat, dsm, num, den, mx,
    gkv, gqd, gst, far1kv, far1qd, far1st, far2kv, far2qd, far2st,
    floc, mnum, mden, mmax, fnum, fden, fmax, emid, efar,
    attn, sdo, npr, mlse, mprod, flse, fprod, fat, fsc,
    dq, dk, dv, dmid, dfar, gp, tilest, tilesp, attnt, cotr, perm, gph, gpr,
    part, r1, tmp, r2, acc, s2, tot, fin, finr,
    stage, pz, z1, zt, z2, zacc, zs, zf, zm,
    ls_, os_, f1s, f1r, f2s, f2r, f3s, f3r, m1s, m1r, m2s, m2r,
    xs, xr, rs, rr_, ss, sr, es_, er_,
    zrs, zrr, zss, zsr, zms, zmr,
):
    me = lax.axis_index("ctx")
    c = me % 2
    z = me // 2 % 4
    g = me // 8
    x = g // 4
    y = g % 4
    mate = g * 8 + z * 2 + (1 - c)

    def zpeer(k):
        return g * 8 + (z + k) % 4 * 2 + c

    def gpeer(k):
        return (g + k) % 16 * 8 + z * 2 + c

    def rc(src, dst, ss, rs, dev):
        return pltpu.make_async_remote_copy(
            src_ref=src, dst_ref=dst, send_sem=ss, recv_sem=rs, device_id=(dev,), device_id_type=MESH
        )

    def load(src, dst, n):
        return pltpu.make_async_copy(src, dst, ls_.at[n])

    loads = [load(tiles_h, tiles, 0)]
    for i in range(3):
        for a in (1, 2):
            cols = pl.ds(a * D + i * N, N)
            loads.append(load(wqkv_h.at[:, cols], wqkv.at[:, cols], 1 + i))
    later = [
        load(wqkv_h.at[:, pl.ds(0, D)], wqkv.at[:, pl.ds(0, D)], 4),
        load(cot_h, cot, 5),
        load(wout_h, wout, 6),
    ]
    small = (load(offs_h, offs, 7), load(pad_h, pad, 8))
    for item in small:
        item.start()
    for item in loads:
        item.start()
    barrier = pltpu.get_barrier_semaphore()
    peers = [mate] + [zpeer(k) for k in (1, 2, 3)] + [gpeer(k) for k in range(1, 16)]
    peers += [g * 8 + (z + k) % 4 * 2 + (1 - c) for k in (1, 2, 3)]
    for p in peers:
        pl.semaphore_signal(barrier, inc=1, device_id=(p,), device_id_type=MESH)

    FAR1 = (far1kv, far1qd, far1st)
    FAR2 = (far2kv, far2qd, far2st)
    MID = (gkv, gqd, gst)

    def f1_copy(t, k):
        return rc(FAR1[t].at[z], FAR1[t].at[z], f1s.at[t], f1r.at[t], zpeer(k))

    def f1_all(t):
        some = FAR1[t].at[pl.ds(0, 3)]
        return rc(some, some, f1s.at[t], f1r.at[t], zpeer(1))

    def f1_start(t):
        for k in (1, 3, 2):
            f1_copy(t, k).start()

    def f1_wait(t):
        f1_all(t).wait_recv()

    def f2_copy(t, k):
        return rc(FAR2[t].at[c, g], FAR2[t].at[c, g], f2s.at[t], f2r.at[t], gpeer(k))

    def f2_all(t):
        some = FAR2[t].at[c, pl.ds(0, 15)]
        return rc(some, some, f2s.at[t], f2r.at[t], gpeer(1))

    def f2_start(t):
        a = FAR1[t]
        FAR2[t][c, g] = (
            a[0].astype(F32) + a[1].astype(F32) + a[2].astype(F32) + a[3].astype(F32)
        ).astype(a.dtype)
        for k in range(1, 16):
            f2_copy(t, k).start()

    def f2_wait(t):
        f2_all(t).wait_recv()

    def f3_copy(t):
        return rc(FAR2[t].at[c], FAR2[t].at[c], f3s.at[t], f3r.at[t], mate)

    def f3_wait(t):
        rc(FAR2[t].at[1 - c], FAR2[t].at[1 - c], f3s.at[t], f3r.at[t], mate).wait_recv()

    def m1_copy(t, k):
        return rc(MID[t].at[c, z], MID[t].at[c, z], m1s.at[t], m1r.at[t], zpeer(k))

    def m1_all(t):
        some = MID[t].at[c, pl.ds(0, 3)]
        return rc(some, some, m1s.at[t], m1r.at[t], zpeer(1))

    def m2_copy(t, k):
        o = (z + k) % 4
        return rc(MID[t].at[c, o], MID[t].at[c, o], m2s.at[t], m2r.at[t], mate)

    def m2_all(t, who):
        return rc(MID[t].at[who], MID[t].at[who], m2s.at[t], m2r.at[t], mate)

    def m1_start(t):
        for k in (1, 3, 2):
            m1_copy(t, k).start()
        m2_copy(t, 0).start()

    def m1_forward(t):
        m1_all(t).wait_recv()
        for k in (1, 3, 2):
            m2_copy(t, k).start()

    def m2_wait(t):
        m2_all(t, 1 - c).wait_recv()

    def to_mate(t, src, dst):
        return rc(src, dst, xs.at[t], xr.at[t], mate)

    half_cols = pl.ds(pl.multiple_of(384 * (1 - c), 128), 384)
    own_cols = pl.ds(pl.multiple_of(384 * c, 128), 384)

    for item in small:
        item.wait()
    limit = N * 128 - pad[0]
    lane_head = iota((1, D), 1) // E
    o0 = jnp.zeros((1, D), I32)
    o1 = jnp.zeros((1, D), I32)
    for h in range(H):
        o0 = jnp.where(lane_head == h, offs[0, h], o0)
        o1 = jnp.where(lane_head == h, offs[1, h], o1)
    midm[...] = jnp.where(iota((N, D), 0) % 8 == o0, 1.0, 0.0).astype(BF)
    farm[...] = jnp.where(iota((N, D), 0) % 128 == o1, 1.0, 0.0).astype(BF)

    nfar[...] = jnp.where(iota((N, D), 0) % 128 == o1, 0.0, 1.0).astype(BF)
    r0 = iota((D, 128), 0)
    l0 = iota((D, 128), 1)
    sel1[...] = jnp.where(jnp.logical_and(r0 == l0 * E, l0 < H), 1.0, 0.0).astype(BF)
    sel2[...] = jnp.where(r0 // E == l0 - H, 1.0, 0.0).astype(BF)
    hsel[...] = jnp.where(iota((16, D), 1) // E == iota((16, D), 0), 1.0, 0.0)
    pool_mid = jnp.where(iota((32, N), 1) // 8 == iota((32, N), 0), 1.0, 0.0).astype(BF)
    two = iota((16, N), 1) // 128
    row = iota((16, N), 0)
    pool_far = jnp.where(row == two, 1.0, 0.0)
    none = jnp.zeros_like(pool_far)
    far_a = [jnp.where(row == 2 * z + two, 1.0, 0.0), pool_far, none]
    far_b = [jnp.where(row == 8 + 2 * z + two, 1.0, 0.0), none, pool_far]
    far_a = jnp.concatenate(far_a, axis=0).astype(BF)
    far_b = jnp.concatenate(far_b, axis=0).astype(BF)

    def picks(t, i, a, b):
        ls = pl.ds(pl.multiple_of(i * N, N), N)
        hi = pl.ds(pl.multiple_of(D + i * N, N), N)
        mk = midm[:, ls]
        fk = farm[:, ls]
        rows = (nn(far_a, a * fk) + nn(far_b, b * fk)).astype(BF)
        FAR1[t][z, :, ls] = rows[0:16]
        MID[t][c, z, :, ls] = nn(pool_mid, a * mk).astype(BF)
        MID[t][c, z, :, hi] = nn(pool_mid, b * mk).astype(BF)
        floc[2 * t, :, ls] = rows[16:32]
        floc[2 * t + 1, :, ls] = rows[32:48]

    loads[0].wait()

    for i in range(3):
        cols = pl.ds(i * 2 * N, 2 * N)
        load(wqkv_h.at[:, cols], wqkv.at[:, cols], 1 + i).wait()
        if i == 0:
            for item in later:
                item.start()
        kc = pl.ds(D + i * N, N)
        vc = pl.ds(2 * D + i * N, N)
        kk = nn(tiles[...], wqkv[:, kc]).astype(BF)
        vv = nn(tiles[...], wqkv[:, vc]).astype(BF)
        pk[:, kc] = kk
        pk[:, vc] = vv
        picks(0, i, kk, vv)

    pl.semaphore_wait(barrier, len(peers))
    f1_start(0)
    for item in later:
        item.wait()
    to_mate(0, cot.at[:, half_cols], cotr).start()

    for i in range(3):
        if i == 1:
            m1_start(0)
        qc = pl.ds(i * N, N)
        dc = pl.ds(3 * D + i * N, N)
        qq = nn(tiles[...], wqkv[:, qc]).astype(BF) * jnp.asarray(0.125, BF)
        dd = nt(cot[...], wout[qc, :]).astype(BF)
        pk[:, qc] = qq
        pk[:, dc] = dd
        picks(1, i, qq, dd)


    half = iota((1, 128), 1) // E
    hm = [jnp.where(half == a, 1.0, 0.0).astype(BF) for a in range(2)]

    def lanes(p, base=0):
        return pl.ds(pl.multiple_of(base + p * 128, 128), 128)

    def near_forward(lo, hi):
        @pl.loop(lo, hi, unroll=2)
        def _(p):
            q2 = pk[:, lanes(p)]
            k2 = pk[:, lanes(p, D)]
            v2 = pk[:, lanes(p, 2 * D)]
            bias = jnp.where(me * N + iota((1, N), 1) < limit, 0.0, NEG)
            es, ms = [], []
            for a in range(2):
                s = nt(q2 * hm[a], k2) + bias
                m = jnp.max(s, axis=1, keepdims=True)
                e = jnp.exp(s - m).astype(BF)
                emat[2 * p + a] = e
                es.append(e)
                ms.append(m)
            rhs = jnp.concatenate(
                [
                    jnp.concatenate([v2 * hm[a], jnp.broadcast_to(hm[a], (N, 128))], axis=1)
                    for a in range(2)
                ],
                axis=0,
            )
            nd = nn(jnp.concatenate(es, axis=1), rhs)
            num[:, lanes(p)] = nd[:, :128]
            den[:, lanes(p)] = nd[:, 128:]
            mx[:, lanes(p)] = jnp.where(iota((N, 128), 1) < E, ms[0], ms[1])

    f1_wait(0)
    f2_start(0)
    near_forward(0, 6)
    tilest[c] = tiles[...].T
    m1_forward(0)
    f1_start(1)
    m1_start(1)
    to_mate(1, tilest.at[c], tilest.at[c]).start()
    pr = iota((D, D), 0)
    want = pr // 12 % 16 * 48 + pr // 192 * 12 + pr % 12
    perm[...] = jnp.where(iota((D, D), 1) == want, 1.0, 0.0).astype(BF)
    tilesp[c] = nt(perm[...], tiles[...]).astype(BF)
    to_mate(6, tilesp.at[c], tilesp.at[c]).start()

    m2_wait(0)
    kg = gkv[:, :, :, :D].reshape(N, D)
    vg = gkv[:, :, :, D:].reshape(N, D)
    gdev = g * 8 + iota((32, N), 1) // 32 % 4 * 2 + iota((32, N), 1) // 128
    gpos = gdev * N + iota((32, N), 1) % 32 * 8
    gbias = jnp.concatenate(
        [jnp.where(gpos + offs[0, h] < limit, 0.0, NEG) for h in range(H)], axis=0
    )
    s = nt(block_diag(gqd[c, z, :, :D]), kg) + gbias
    m = jnp.max(s, axis=1, keepdims=True)
    e = jnp.exp(s - m)
    total = jnp.sum(e, axis=1, keepdims=True)
    e = e.astype(BF)
    emid[...] = e
    mnum[...] = diag_sum(nn(e, vg), 32)
    mden[...] = per_head(total, 32)
    mmax[...] = per_head(m, 32)

    f2_wait(0)
    f3_copy(0).start()

    def spread_mid(x):
        return jnp.broadcast_to(x[:, None, :], (32, 8, 128)).reshape(N, 128)

    def spread_far(x):
        return jnp.concatenate(
            [jnp.broadcast_to(x[0:1], (128, 128)), jnp.broadcast_to(x[1:2], (128, 128))], axis=0
        )

    def pick_mid(x):
        return jnp.sum(x.reshape(32, 8, 128), axis=1)

    def pick_far(x):
        return jnp.concatenate(
            [
                jnp.sum(x[:128], axis=0, keepdims=True),
                jnp.sum(x[128:], axis=0, keepdims=True),
            ],
            axis=0,
        )

    @pl.loop(0, 6, unroll=2)
    def _(p):
        ls = lanes(p)
        mm = midm[:, ls].astype(F32)
        fm = farm[:, ls].astype(F32)
        m0 = mx[:, ls]
        m1 = jnp.where(mm > 0.5, spread_mid(mmax[:, ls]), NEG)
        top = jnp.maximum(m0, m1)
        w0 = jnp.exp(m0 - top)
        w1 = jnp.exp(m1 - top)
        total = w0 * den[:, ls] + w1 * spread_mid(mden[:, ls])
        inv = 1.0 / total
        exact = (w0 * num[:, ls] + w1 * spread_mid(mnum[:, ls])) * inv
        at = exact.astype(BF)
        attn[:, ls] = at
        do = pk[:, lanes(p, 3 * D)].astype(F32)
        prod = do * at.astype(F32)
        scale = w0 * inv
        sdo[:, ls] = (scale * do).astype(BF)
        npr[:, ls] = (-scale * prod).astype(BF)
        lse = top + jnp.log(total)
        mlse[:, ls] = pick_mid(lse * mm)
        mprod[:, ls] = pick_mid(prod * mm)
        flse[0:2, ls] = pick_far(lse * fm)
        fat[0:2, ls] = pick_far(exact * fm)
        fsc[0:2, ls] = pick_far(scale * fm)

    f3_wait(0)

    heads = hsel[...]
    headb = heads.astype(BF)

    def far_diag(v):
        return jnp.concatenate([v[0:1] * headb, v[1:2] * headb], axis=0)

    def far_fold(v):
        return jnp.concatenate(
            [jnp.sum(v[16 * r : 16 * r + 16] * heads, axis=0, keepdims=True) for r in range(2)],
            axis=0,
        )

    col = iota((16, 512), 1)
    fdev = col // 16 % 16 * 8 + col // 2 % 4 * 2 + col // 256
    fpos = (fdev * 2 + col % 2) * 128
    lead = col // 8 % 2 == 0
    off_col = jnp.zeros((16, 512), I32)
    for h in range(H):
        off_col = jnp.where(iota((16, 512), 0) == h, offs[1, h], off_col)
    fbias = jnp.where(jnp.logical_and(lead, fpos + off_col < limit), 0.0, NEG)
    fbias = jnp.concatenate([fbias, fbias], axis=0)
    kvf = far2kv[...].reshape(512, D)
    s = nt(far_diag(floc[2]), kvf) + fbias
    m = jnp.max(s, axis=1, keepdims=True)
    e = jnp.exp(s - m)
    efar[...] = e
    fnum[0:2] = far_fold(nn(pltpu.roll(e, 8, 1).astype(BF), kvf))
    fden[0:2] = far_fold(jnp.broadcast_to(jnp.sum(e, axis=1, keepdims=True), (32, D)))
    fmax[0:2] = far_fold(jnp.broadcast_to(m, (32, D)))

    f1_wait(1)
    f2_start(1)
    a_lse = flse[0:2]
    b_lse = fmax[0:2] + jnp.log(fden[0:2])
    top = jnp.maximum(a_lse, b_lse)
    n_lse = top + jnp.log(jnp.exp(a_lse - top) + jnp.exp(b_lse - top))
    wa = jnp.exp(a_lse - n_lse)
    n_at = (wa * fat[0:2] + jnp.exp(b_lse - n_lse) * fnum[0:2] / fden[0:2]).astype(BF)
    f_do = floc[3, 0:2].astype(F32)
    n_prod = f_do * n_at.astype(F32)
    scale = fsc[0:2] * wa
    n_sdo = scale * f_do
    n_npr = -scale * n_prod
    flse[...] = jnp.concatenate([n_lse, jnp.zeros((14, D), F32)], axis=0)
    fprod[...] = jnp.concatenate([n_prod, jnp.zeros((14, D), F32)], axis=0)
    for p in range(6):
        ls = slice(p * 128, p * 128 + 128)
        keep = nfar[:, ls]
        take = farm[:, ls]
        for ref, new in ((attn, n_at.astype(F32)), (sdo, n_sdo), (npr, n_npr)):
            ref[:, ls] = ref[:, ls] * keep + spread_far(new[:, ls]).astype(BF) * take
    g32 = iota((32, D), 0)
    for r in range(2):
        both = jnp.logical_and(g32 == r * 16 + o1 // 8, o1 % 8 == o0)
        mlse[...] = jnp.where(both, n_lse[r : r + 1], mlse[...])
        mprod[...] = jnp.where(both, n_prod[r : r + 1], mprod[...])

    lse_rows = jnp.concatenate([mlse[...], flse[...]], axis=0)
    prod_rows = jnp.concatenate([mprod[...], fprod[...]], axis=0)
    l_hi = lse_rows.astype(BF)
    left = lse_rows - l_hi.astype(F32)
    l_mid = left.astype(BF)
    l_lo = (left - l_mid.astype(F32)).astype(BF)
    p_hi = prod_rows.astype(BF)
    p_lo = (prod_rows - p_hi.astype(F32)).astype(BF)
    lt = nn(jnp.concatenate([l_hi, l_mid, l_lo], axis=0), sel1[...])
    pt = nn(jnp.concatenate([p_hi, p_lo], axis=0), sel2[...])
    st = lt[0:48] + lt[48:96] + lt[96:144] + pt[0:48] + pt[48:96]
    gst[c, z] = st[0:32]
    fs = st[32:48]
    r8 = iota((8, 128), 0)
    far1st[z] = jnp.where(r8 == 2 * z, fs[0:1], jnp.where(r8 == 2 * z + 1, fs[1:2], 0.0))
    f1_start(2)
    m1_start(2)

    attnt[c] = nt(perm[...], attn[...]).astype(BF)
    to_mate(2, attnt.at[c], attnt.at[c]).start()
    turn = [c, 1 - c]

    def put_part(b, v):
        v = v.astype(BF).reshape(4, 4, 48, 384)
        for i in range(4):
            for j in range(4):
                skip = (j - i) * turn[b]
                part[b, i + skip, j - skip] = v[i, j]

    def dev(x_, y_):
        return ((x_ % 4 * 4 + y_ % 4) * 4 + z) * 2 + c

    first = [x + (y - x) * turn[b] for b in range(2)]
    other = [y + (x - y) * turn[b] for b in range(2)]

    def along(b, k):
        return dev(x + k * (1 - turn[b]), y + k * turn[b])

    def across(b, k):
        return dev(x + k * turn[b], y + k * (1 - turn[b]))

    def where_in(b, q, h):
        return (b, q, slice(None) if h is None else pl.ds(2 * h, 2))

    def ring_copy(b, n):
        p = first[b]
        nxt, prv = along(b, 1), along(b, 3)
        up, down, far = (p + 1) % 4, (p + 3) % 4, (p + 2) % 4
        src, dst, to = (
            lambda: (part.at[where_in(b, far, 0)], r1.at[b, 0], nxt),
            lambda: (part.at[where_in(b, far, 1)], r1.at[b, 1], prv),
            lambda: (part.at[where_in(b, up, 1)], r2.at[b, 0, pl.ds(2, 2)], nxt),
            lambda: (part.at[where_in(b, down, 0)], r2.at[b, 1, pl.ds(0, 2)], prv),
            lambda: (tmp.at[b, 0], r2.at[b, 0, pl.ds(0, 2)], nxt),
            lambda: (tmp.at[b, 1], r2.at[b, 1, pl.ds(2, 2)], prv),
        )[n]()
        return rc(src, dst, rs.at[b], rr_.at[b, min(n, 2)], to)

    def ring_a(b):
        for n in range(4):
            ring_copy(b, n).start()

    def ring_b(b):
        p = first[b]
        for h, q in ((0, (p + 1) % 4), (1, (p + 3) % 4)):
            ring_copy(b, h).wait_recv()
            tmp[b, h] = (part[where_in(b, q, h)].astype(F32) + r1[b, h].astype(F32)).astype(BF)
            ring_copy(b, 4 + h).start()

    def second(b, k):
        q = (other[b] + k) % 4
        return rc(acc.at[b, q], s2.at[b, other[b]], ss.at[b], sr.at[b], across(b, k))

    def second_all(b):
        some = s2.at[b, pl.ds(0, 3)]
        return rc(some, some, ss.at[b], sr.at[b], mate)

    def ring_c(b):
        rc(r2.at[b], r2.at[b], rs.at[b], rr_.at[b, 2], mate).wait_recv()
        mine = part[where_in(b, first[b], None)].astype(F32)
        acc[b] = (mine + r2[b, 0].astype(F32) + r2[b, 1].astype(F32)).astype(BF)
        for k in (2, 1, 3):
            second(b, k).start()

    def ring_d(b):
        total = acc[b, other[b]].astype(F32)
        second_all(b).wait_recv()
        for k in (1, 3, 2):
            total = total + s2[b, (other[b] + k) % 4].astype(F32)
        tot[b] = total.astype(BF)

    own = z * 2 + c
    er = iota((128, 96), 0)
    ek = er % 8
    spread = jnp.where(
        jnp.logical_and(iota((128, 96), 1) == er // 8 % 2 * 48 + er // 16 * 6 + ek, ek < 6), 1.0, 0.0
    ).astype(BF)

    def fin_copy(k):
        o = (own + k) % 8
        return rc(fin.at[o], finr.at[own], es_.at[0], er_.at[0], g * 8 + o)

    def fin_all():
        some = finr.at[pl.ds(0, 7)]
        return rc(some, some, es_.at[0], er_.at[0], mate)

    def fin_start(_):
        fin[...] = nn(spread, tot[...].reshape(96, 384)).astype(BF).reshape(8, 16, 384)
        for k in range(1, 8):
            fin_copy(k).start()
        finr[own] = fin[own]

    def fin_end(_):
        fin_all().wait_recv()
        for a in range(2):
            v = finr[a].astype(F32)
            for o in (2, 4, 6):
                v = v + finr[o + a].astype(F32)
            for i in range(2):
                at = (1 + i) * D + 384 * a
                g_qkv[:, at : at + 384] = v[8 * i : 8 * i + 6]

    def put_z(b, v):
        pz[b] = v.astype(BF).reshape(4, 4, 48, 384)

    def z_copy(b, n):
        nxt, prv = zpeer(1), zpeer(3)
        up, down, far = (z + 1) % 4, (z + 3) % 4, (z + 2) % 4
        lo, hi = pl.ds(0, 2), pl.ds(2, 2)
        src, dst, to = (
            lambda: (pz.at[b, far, lo], z1.at[b, 0], nxt),
            lambda: (pz.at[b, far, hi], z1.at[b, 1], prv),
            lambda: (pz.at[b, up, hi], z2.at[b, 0, hi], nxt),
            lambda: (pz.at[b, down, lo], z2.at[b, 1, lo], prv),
            lambda: (zt.at[b, 0], z2.at[b, 0, lo], nxt),
            lambda: (zt.at[b, 1], z2.at[b, 1, hi], prv),
        )[n]()
        return rc(src, dst, zrs.at[b], zrr.at[b, min(n, 2)], to)

    def z_a(b):
        for n in range(4):
            z_copy(b, n).start()

    def z_b(b):
        for h, q in ((0, (z + 1) % 4), (1, (z + 3) % 4)):
            z_copy(b, h).wait_recv()
            mine = pz[b, q, 2 * h : 2 * h + 2].astype(F32)
            zt[b, h] = (mine + z1[b, h].astype(F32)).astype(BF)
            z_copy(b, 4 + h).start()

    def z_second(b, k):
        return rc(zacc.at[b, (g + k) % 16], zs.at[b, g], zss.at[b], zsr.at[b], gpeer(k))

    def z_second_all(b):
        some = zs.at[b, pl.ds(0, 15)]
        return rc(some, some, zss.at[b], zsr.at[b], mate)

    def z_c(b):
        rc(z2.at[b], z2.at[b], zrs.at[b], zrr.at[b, 2], mate).wait_recv()
        mine = pz[b, z].astype(F32)
        mine = mine + z2[b, 0].astype(F32) + z2[b, 1].astype(F32)
        stage[0:192] = mine.reshape(192, 384)
        for i in range(16):
            zacc[b, i] = stage[12 * i : 12 * i + 16].astype(BF)
        for k in range(1, 16):
            z_second(b, k).start()

    def z_mate(b):
        return rc(zf.at[b], zm.at[b], zms.at[b], zmr.at[b], mate)

    def z_d(b):
        z_second_all(b).wait_recv()
        total = zacc[b, g].astype(F32)
        for k in range(1, 16):
            total = total + zs[b, (g + k) % 16].astype(F32)
        zf[b] = total
        z_mate(b).start()

    def z_e(b):
        z_mate(b).wait_recv()
        target = (g_out, g_qkv)[b]
        for ref, half in ((zf, c), (zm, 1 - c)):
            v = ref[b]
            cols = pl.ds(pl.multiple_of(384 * half, 128), 384)
            target[:, cols] = jnp.where(c == 0, v[0:6], v[6:12])

    def backward_queries(lo, hi):
        @pl.loop(lo, hi, unroll=2)
        def _(p):
            ls = lanes(p)
            k2 = pk[:, lanes(p, D)]
            so = sdo[:, ls]
            v2 = pk[:, lanes(p, 2 * D)]
            prod = so.astype(F32) * attn[:, ls].astype(F32)
            ds = []
            for a in range(2):
                delta = jnp.sum(prod * hm[a].astype(F32), axis=1, keepdims=True)
                t = nt(so * hm[a], v2) - delta
                d = (emat[2 * p + a].astype(F32) * t).astype(BF)
                dsm[2 * p + a] = d
                ds.append(d)
            dq[:, ls] = 0.125 * nn(
                jnp.concatenate(ds, axis=1), jnp.concatenate([k2 * hm[0], k2 * hm[1]], axis=0)
            )

    def backward_keys(lo, hi):
        @pl.loop(lo, hi, unroll=2)
        def _(p):
            ls = lanes(p)
            q2 = pk[:, ls]
            so = sdo[:, ls]
            dk[:, ls] = tn(
                jnp.concatenate([dsm[2 * p], dsm[2 * p + 1]], axis=0),
                jnp.concatenate([q2 * hm[0], q2 * hm[1]], axis=0),
            )
            dv[:, ls] = tn(
                jnp.concatenate([emat[2 * p], emat[2 * p + 1]], axis=0),
                jnp.concatenate([so * hm[0], so * hm[1]], axis=0),
            )

    backward_queries(0, 4)
    m1_forward(1)
    to_mate(0, cotr, cotr).wait_recv()
    to_mate(2, attnt.at[1 - c], attnt.at[1 - c]).wait_recv()
    put_z(0, nn(attnt[c], cot[:, own_cols]) + nn(attnt[1 - c], cotr[...]))
    z_a(0)
    f1_wait(2)
    f2_start(2)
    backward_queries(4, 6)
    m1_forward(2)

    kg = gkv[:, :, :, :D].reshape(N, D)
    vg = gkv[:, :, :, D:].reshape(N, D)
    scale = jnp.exp(mmax[...] - mlse[...])
    so = (scale * gqd[c, z, :, D:].astype(F32)).astype(BF)
    sp = scale * mprod[...]
    dl = jnp.concatenate(
        [jnp.sum(sp * head_mask(h, F32), axis=1, keepdims=True) for h in range(H)], axis=0
    )
    ds = (emid[...].astype(F32) * (nt(block_diag(so), vg) - dl)).astype(BF)
    dmid[0] = 0.125 * diag_sum(nn(ds, kg), 32)

    scale = jnp.exp(fmax[0:2] - flse[0:2])
    so = (scale * floc[3, 0:2].astype(F32)).astype(BF)
    sp = scale * fprod[0:2]
    dl = jnp.concatenate(
        [jnp.sum(sp[r : r + 1] * heads, axis=1, keepdims=True) for r in range(2)], axis=0
    )
    kvf = far2kv[...].reshape(512, D)
    t = pltpu.roll(nt(far_diag(so), kvf), 504, 1)
    dfar[0, 0:2] = 0.125 * far_fold(nn((efar[...] * (t - dl)).astype(BF), kvf))

    def grad_part(a, near):
        @pl.loop(0, 6)
        def _(p):
            ls = lanes(p)
            mm = midm[:, ls].astype(F32)
            fm = farm[:, ls].astype(F32)
            v = near[:, ls] + mm * spread_mid(dmid[a, :, ls]) + fm * spread_far(dfar[a, 0:2, ls])
            v = v.astype(BF)
            gp[:, lanes(p, a * D)] = v
            gph[a, p // 3, :, lanes(p % 3)] = v

        to_mate(3 + a, gph.at[a, 1 - c], gpr.at[a]).start()

    def weight_part(a):
        to_mate(3 + a, gpr.at[a], gpr.at[a]).wait_recv()
        rows = tilest if a else tilesp
        v = nn(rows[c], gph[a, c]) + nn(rows[1 - c], gpr[a])
        if a == 0:
            put_z(1, v)
        else:
            put_part(a - 1, v)
            ring_a(a - 1)

    grad_part(0, dq)
    backward_keys(0, 4)
    f2_wait(1)
    f3_copy(1).start()
    to_mate(1, tilest.at[1 - c], tilest.at[1 - c]).wait_recv()
    to_mate(6, tilesp.at[1 - c], tilesp.at[1 - c]).wait_recv()
    z_b(0)
    weight_part(0)
    backward_keys(4, 6)
    f2_wait(2)
    f3_copy(2).start()
    m2_wait(1)
    m2_wait(2)

    st = gst[...].reshape(N, 128).T
    ls_rows = st[0:16]
    dl_rows = st[12:28]
    qg = gqd[:, :, :, :D].reshape(N, D)
    og = gqd[:, :, :, D:].reshape(N, D)
    s = nt(block_diag(gkv[c, z, :, :D]), qg)
    t = nt(block_diag(gkv[c, z, :, D:]), og)
    ps, dss = [], []
    for h in range(H):
        ok = me * N + iota((32, N), 0) * 8 + offs[0, h] < limit
        p = jnp.exp(jnp.where(ok, s[h * 32 : (h + 1) * 32] - ls_rows[h : h + 1], NEG))
        ps.append(p.astype(BF))
        dss.append((p * (t[h * 32 : (h + 1) * 32] - dl_rows[h : h + 1])).astype(BF))
    dmid[1] = diag_sum(nn(jnp.concatenate(dss, axis=0), qg), 32)
    pmid = jnp.concatenate(ps, axis=0)

    f3_wait(1)
    f3_wait(2)
    st = far2st[...].reshape(32, 8, 128)
    st = jnp.concatenate([st, jnp.zeros_like(st)], axis=1).reshape(512, 128).T
    ls_rows = jnp.concatenate([st[0:16], st[0:16]], axis=0)
    dl_rows = jnp.concatenate([st[12:28], st[12:28]], axis=0)
    qdf = far2qd[...].reshape(512, D)
    s = nt(far_diag(floc[0]), qdf)
    t = pltpu.roll(nt(far_diag(floc[1]), qdf), 504, 1)
    row_h = iota((16, 512), 0)
    oks = [
        jnp.logical_and(
            jnp.logical_and(lead, row_h < H), (me * 2 + r) * 128 + off_col < limit
        )
        for r in range(2)
    ]
    expo = jnp.concatenate(
        [jnp.where(oks[r], (s - ls_rows)[16 * r : 16 * r + 16], NEG) for r in range(2)], axis=0
    )
    pfar = jnp.exp(expo)
    dfar[1, 0:2] = far_fold(nn((pfar * (t - dl_rows)).astype(BF), qdf))
    grad_part(1, dk)
    dmid[2] = diag_sum(nn(pmid, og), 32)
    dfar[2, 0:2] = far_fold(nn(pltpu.roll(pfar, 8, 1).astype(BF), qdf))
    z_c(0)
    z_a(1)
    grad_part(2, dv)
    weight_part(1)
    weight_part(2)

    @pl.loop(0, 3)
    def _(i):
        ls = pl.ds(pl.multiple_of(i * N, N), N)
        out_rows[:, ls] = (tiles[:, ls].astype(F32) + nn(attn[...], wout[:, ls])).astype(BF)
        grad_tiles[:, ls] = nt(gp[...], wqkv[ls, :]).astype(BF)

    z_b(1)
    ring_b(0)
    ring_b(1)
    z_c(1)
    ring_c(0)
    ring_c(1)
    z_d(0)
    ring_d(0)
    ring_d(1)
    fin_start(1)
    z_d(1)
    z_e(0)
    z_e(1)
    fin_end(1)

    to_mate(0, cot.at[:, half_cols], cotr).wait_send()
    to_mate(1, tilest.at[c], tilest.at[c]).wait_send()
    to_mate(6, tilesp.at[c], tilesp.at[c]).wait_send()
    to_mate(2, attnt.at[c], attnt.at[c]).wait_send()
    for a in range(3):
        to_mate(3 + a, gph.at[a, 1 - c], gpr.at[a]).wait_send()
    for b in range(2):
        some = part.at[b, pl.ds(0, 3)]
        rc(some, some, rs.at[b], rr_.at[b, 2], mate).wait_send()
        second_all(b).wait_send()
        some = pz.at[b, pl.ds(0, 3)]
        rc(some, some, zrs.at[b], zrr.at[b, 2], mate).wait_send()
        z_second_all(b).wait_send()
        z_mate(b).wait_send()
    fin_all().wait_send()
    for t in range(3):
        f1_all(t).wait_send()
        m1_all(t).wait_send()
        f2_all(t).wait_send()
        f3_copy(t).wait_send()
        m2_all(t, c).wait_send()


def copy_kernel(*refs):
    sems = refs[8]
    copies = [pltpu.make_async_copy(refs[i], refs[4 + i], sems.at[i]) for i in range(4)]
    for item in copies:
        item.start()
    for item in copies:
        item.wait()


def per_device(tiles, w_qkv, w_out, cotangent, offsets, pad_count):
    vm = pl.BlockSpec(memory_space=pltpu.VMEM)
    hbm = pl.BlockSpec(memory_space=pl.ANY)
    V = pltpu.VMEM
    dma = pltpu.SemaphoreType.DMA
    big = V((N, D), F32)
    bigb = V((N, D), BF)
    m32 = V((32, D), F32)
    f16 = V((16, D), F32)
    shapes = (
        jax.ShapeDtypeStruct((N, D), BF),
        jax.ShapeDtypeStruct((N, D), BF),
        jax.ShapeDtypeStruct((6, 3 * D), F32),
        jax.ShapeDtypeStruct((6, D), F32),
    )
    outs = pl.pallas_call(
        kernel,
        out_shape=tuple(V(a.shape, a.dtype) for a in shapes),
        in_specs=[hbm] * 6,
        out_specs=(vm,) * 4,
        scratch_shapes=[
            pltpu.SMEM((2, H), I32), pltpu.SMEM((1,), I32),
            bigb, V((D, 3 * D), BF), V((D, D), BF), bigb,
            V((N, 4 * D), BF), bigb, bigb, bigb, V((D, 128), BF), V((D, 128), BF), f16,
            V((H, N, N), BF), V((H, N, N), BF), big, big, big,
            V((2, 4, 32, 2 * D), BF), V((2, 4, 32, 2 * D), BF), V((2, 4, 32, 128), F32),
            V((4, 16, D), BF), V((4, 16, D), BF), V((4, 8, 128), F32),
            V((2, 16, 16, D), BF), V((2, 16, 16, D), BF), V((2, 16, 8, 128), F32),
            V((4, 16, D), BF), m32, m32, m32, f16, f16, f16, V((H * 32, N), BF), V((32, 512), F32),
            bigb, bigb, bigb, m32, m32, f16, f16, f16, f16,
            big, big, big, V((3, 32, D), F32), V((3, 16, D), F32), V((N, 3 * D), BF),
            V((2, D, N), BF), V((2, D, N), BF), V((2, D, N), BF), V((N, 384), BF), V((D, D), BF),
            V((3, 2, N, 384), BF), V((3, N, 384), BF),
            V((2, 4, 4, 48, 384), BF),
            V((2, 2, 2, 48, 384), BF), V((2, 2, 2, 48, 384), BF), V((2, 2, 4, 48, 384), BF),
            V((2, 4, 48, 384), BF), V((2, 4, 48, 384), BF), V((2, 48, 384), BF),
            V((8, 16, 384), BF), V((8, 16, 384), BF),
            V((208, 384), F32), V((2, 4, 4, 48, 384), BF),
            V((2, 2, 2, 48, 384), BF), V((2, 2, 2, 48, 384), BF), V((2, 2, 4, 48, 384), BF),
            V((2, 16, 16, 384), BF), V((2, 16, 16, 384), BF), V((2, 16, 384), F32), V((2, 16, 384), F32),
            dma((9,)), dma((2,)),
            dma((3,)), dma((3,)), dma((3,)), dma((3,)), dma((3,)), dma((3,)),
            dma((3,)), dma((3,)), dma((3,)), dma((3,)),
            dma((7,)), dma((7,)), dma((2,)), dma((2, 3)), dma((2,)), dma((2,)),
            dma((1,)), dma((1,)),
            dma((2,)), dma((2, 3)), dma((2,)), dma((2,)), dma((2,)), dma((2,)),
        ],
        compiler_params=pltpu.CompilerParams(
            collective_id=0, has_side_effects=True, vmem_limit_bytes=61 * 1024 * 1024
        ),
        name="layer",
    )(offsets, pad_count, tiles, w_qkv, w_out, cotangent)
    return pl.pallas_call(
        copy_kernel, out_shape=shapes, in_specs=[vm] * 4, out_specs=(hbm,) * 4, scratch_shapes=[dma((4,))],
        name="results"
    )(*(pltpu.with_memory_space_constraint(o, pltpu.VMEM) for o in outs))


def solution(mesh):
    row = P("ctx", None)
    return jax.shard_map(
        per_device,
        mesh=mesh,
        in_specs=(row, P(), P(), row, P(), P()),
        out_specs=(row, row, row, row),
        check_vma=False,
    )
```
